32 devices in a mesh: slab: 8 (over z, y), sector: 4 (over x, core).
Axes of the slice: x: 2, y: 2, z: 4, core: 2. Of those that a mesh axis runs over, the one named last changes fastest.
Arguments:
- source: float32 [8, 4, 8, 4096], P('slab', 'sector'), may hold values from -6 to 6
- periods: float32 [8, 8], replicated, may hold values from -4 to 4
- tiles: float32 [8, 4, 64, 4, 4096], P('slab', 'sector'), may hold values from -0.01 to 0.01
- columns: int32 [8, 4, 64, 4], P('slab', 'sector'), may hold values from 0 to 63, as said below
- coupling: float32 [8, 4, 4, 32, 4096], P('slab', 'sector'), may hold values from -0.01 to 0.01
- send_list: int32 [8, 4, 4, 32], P('slab', 'sector'), may hold values from 0 to 63, as said below
- recv_rows: int32 [8, 4, 4, 32], P('slab', 'sector'), may hold values from 0 to 63, as said below
- counts: int32 [8, 4, 4], P('slab', 'sector'), may hold values from 1 to 32, as said below
- cycle_edges: int32 [8, 4, 8, 32], P('slab', 'sector'), may hold values from 0 to 4095, as said below
- cycle_signs: int32 [8, 4, 8, 32], P('slab', 'sector'), may hold values from 0 to 1
- inverse_blocks: float32 [8, 4, 64, 4096], P('slab', 'sector'), as said below
Outputs:
- solution: float32 [8, 4, 8, 4096], P('slab', 'sector')
- residual: float32 [8, 4, 8, 4096], P('slab', 'sector')
The draws below stay inside these ranges and needn't reach their ends.
Inputs may be any that keep to these rules, and one draw needn't show every extreme that they name: `columns`: block b's 4 column blocks are (b + o_k) mod 64 with 4 distinct offsets o_k of the device. `send_list`: the 32 blocks of one list are distinct. `recv_rows`: the 32 row blocks toward one neighbour are distinct. `counts`: some list is full. `cycle_edges`: the edges of one cycle on one device are distinct. `inverse_blocks`: each block is symmetric with diagonal entries of 0.8 or more and off-diagonal entries of magnitude 0.012 or less.
All inputs are finite; a program needn't handle non-finite values.
Results may differ from the reference program's by a relative error of at most 0.0003.
Values sent between devices are 32-bit elements; how exact they have to be, the bound alone decides.
No kernel may reach another device: no remote copies, remote signals or barrier semaphores. Data moves between devices by JAX's collectives and lax.ppermute only.
A program may use at most 128 MiB of HBM per device.

```python
import jax
import jax.numpy as jnp
from jax import lax

F = 8
G = 8
TILE = 64
KT = 4
NB = 64
CYC_LEN = 32
ITERS = 2
CAP = 32
EDGES_DEV = 4096
SLABS = 8
SECTORS = 4


def draw_columns(key, part):
    key_list = jax.random.split(jax.random.fold_in(key, 13), SLABS * SECTORS)

    def one_device(subkey):
        offsets = jax.random.permutation(subkey, NB)[:KT].astype(jnp.int32)
        return (jnp.arange(NB, dtype=jnp.int32)[:, None] + offsets[None, :]) % NB
    return jax.vmap(one_device)(key_list).reshape(SLABS, SECTORS, NB, KT)


def pick_rows(key):
    key_list = jax.random.split(key, SLABS * SECTORS * 4)

    def one_list(subkey):
        return jax.random.permutation(subkey, NB)[:CAP].astype(jnp.int32)
    return jax.vmap(one_list)(key_list).reshape(SLABS, SECTORS, 4, CAP)


def draw_send_list(key, part):
    return pick_rows(jax.random.fold_in(key, 11))


def draw_recv_rows(key, part):
    return pick_rows(jax.random.fold_in(key, 12))


def draw_counts(key, part):
    drawn = jax.random.randint(jax.random.fold_in(key, 14), (SLABS, SECTORS, 4), 1, CAP + 1).astype(jnp.int32)
    return drawn.at[0, 0, 0].set(CAP)


def draw_cycle_edges(key, part):
    key_list = jax.random.split(jax.random.fold_in(key, 15), SLABS * SECTORS * G)

    def one_cycle(subkey):
        return jax.random.permutation(subkey, NB * TILE)[:CYC_LEN].astype(jnp.int32)
    return jax.vmap(one_cycle)(key_list).reshape(SLABS, SECTORS, G, CYC_LEN)


def draw_inverse_blocks(key, part):
    first, second = jax.random.split(jax.random.fold_in(key, 16))
    shape = (SLABS, SECTORS, NB, TILE, TILE)
    offdiag = jax.random.uniform(second, shape, jnp.float32, -0.012, 0.012)
    offdiag = 0.5 * (offdiag + jnp.swapaxes(offdiag, -1, -2))
    diagonal = jax.random.uniform(first, shape[:-1], jnp.float32, 0.8, 1.2)
    identity = jnp.eye(TILE, dtype=jnp.float32)
    matrices = offdiag * (1.0 - identity) + identity * diagonal[..., None]
    return matrices.reshape(SLABS, SECTORS, NB, TILE * TILE)


def touch_ends(values, rng, low, largest):
    longest = values.shape.index(max(values.shape))
    spots = []
    for shift in (0, 1):
        where = [jax.random.randint(jax.random.fold_in(rng, axis), (), 0, length) for axis, length in enumerate(values.shape)]
        where[longest] = (where[longest] + shift) % values.shape[longest]
        spots.append(tuple(where))
    return values.at[spots[0]].set(low).at[spots[1]].set(largest)


def block_scale(rng, extent, shards, least, top_value):
    def one(dim, blocks):
        heights = jax.random.uniform(jax.random.fold_in(jax.random.fold_in(rng, 6), dim), (blocks,), jnp.float32, least / len(shards), top_value / len(shards))
        return jnp.repeat(jnp.exp(heights), extent[dim] // blocks).reshape((-1,) + (1,) * (len(extent) - dim - 1))

    gain = one(*shards[0])
    for cut in shards[1:]:
        gain = gain * one(*cut)
    return gain


def normal_values(own_key, extent, width, bound, pieces=(), held_as=jnp.bfloat16):
    values = width * jax.random.normal(own_key, extent, jnp.float32)
    if pieces:
        values = values * block_scale(own_key, extent, pieces, -0.22, 0.18)
    return jnp.clip(values, -bound, bound).astype(held_as)


def setup_inputs(seed: int = 0) -> dict:
    arg_keys = jax.random.split(jax.random.key(seed), 12)
    return {
        "source": normal_values(arg_keys[0], (SLABS, SECTORS, F, EDGES_DEV), 1.0, 6.0, ((0, 8), (1, 4)), jnp.float32),
        "periods": normal_values(arg_keys[1], (G, F), 1.0, 4.0, (), jnp.float32),
        "tiles": jnp.clip(jax.random.uniform(arg_keys[2], (SLABS, SECTORS, NB, KT, TILE * TILE), jnp.float32, -0.01, 0.01) * block_scale(arg_keys[2], (SLABS, SECTORS, NB, KT, TILE * TILE), ((0, 8), (1, 4)), -0.4, 0.0), -0.01, 0.01),
        "columns": draw_columns(jax.random.fold_in(arg_keys[11], 71), 0),
        "coupling": jnp.clip(jax.random.uniform(arg_keys[4], (SLABS, SECTORS, 4, CAP, TILE * TILE), jnp.float32, -0.01, 0.01) * block_scale(arg_keys[4], (SLABS, SECTORS, 4, CAP, TILE * TILE), ((0, 8), (1, 4)), -0.4, 0.0), -0.01, 0.01),
        "send_list": draw_send_list(jax.random.fold_in(arg_keys[11], 71), 0),
        "recv_rows": draw_recv_rows(jax.random.fold_in(arg_keys[11], 71), 0),
        "counts": draw_counts(jax.random.fold_in(arg_keys[11], 71), 0),
        "cycle_edges": draw_cycle_edges(jax.random.fold_in(arg_keys[11], 71), 0),
        "cycle_signs": touch_ends(jax.random.randint(arg_keys[9], (SLABS, SECTORS, G, CYC_LEN), 0, 2), jax.random.fold_in(arg_keys[9], 1), 0, 1).astype(jnp.int32),
        "inverse_blocks": draw_inverse_blocks(jax.random.fold_in(arg_keys[11], 71), 0),
    }


PRECISE = lax.Precision.HIGHEST
DIAGONAL_SHIFT = 1.0


def local_part(vector, tiles_here, columns_here):
    fields = vector.shape[0]
    block_count = columns_here.shape[0]
    blocked = vector.reshape(fields, block_count, TILE)
    blocks = tiles_here.reshape(block_count, -1, TILE, TILE)
    picked = blocked[:, columns_here]
    result = DIAGONAL_SHIFT * blocked + jnp.einsum("fnkj,nkij->fni", picked, blocks, precision=PRECISE)
    mirrored = jnp.einsum("fni,nkij->fnkj", blocked, blocks, precision=PRECISE)
    result = result.at[:, columns_here.reshape(-1)].add(mirrored.reshape(fields, -1, TILE))
    return result


def slot_weight(counts_here, capacity):
    return (lax.broadcasted_iota(jnp.int32, (4, capacity), 1) < counts_here[:, None]).astype(jnp.float32)


def outgoing(vector, coupling_here, send_here, recv_here, counts_here):
    fields = vector.shape[0]
    blocked = vector.reshape(fields, -1, TILE)
    couple = coupling_here.reshape(4, -1, TILE, TILE)
    weight = slot_weight(counts_here, couple.shape[1])
    leaving = jnp.transpose(blocked[:, send_here], (1, 0, 2, 3)) * weight[:, None, :, None]
    partner = jnp.einsum("dcij,fdci->dfcj", couple, blocked[:, recv_here], precision=PRECISE)
    return jnp.stack([leaving, partner], axis=1)


def absorb(result, incoming, coupling_here, send_here, recv_here, counts_here):
    couple = coupling_here.reshape(4, -1, TILE, TILE)
    weight = slot_weight(counts_here, couple.shape[1])
    arriving = incoming[:, 0]
    returned = incoming[:, 1]
    result = result.at[:, recv_here].add(jnp.einsum("dcij,dfcj->fdci", couple, arriving, precision=PRECISE))
    result = result.at[:, send_here].add(jnp.transpose(returned, (1, 0, 2, 3)) * weight[None, :, :, None])
    return result.reshape(result.shape[0], -1)


def period_part(vector, edges_here, orient):
    return jnp.sum(vector[:, edges_here] * orient[None], axis=2)


def spread(vector, edges_here, orient, totals):
    fields = vector.shape[0]
    return vector.at[:, edges_here.reshape(-1)].add((orient[None] * totals[:, :, None]).reshape(fields, -1))


def smooth(vector, inverse_here):
    fields = vector.shape[0]
    blocks = inverse_here.reshape(-1, TILE, TILE)
    blocked = vector.reshape(fields, -1, TILE)
    return jnp.einsum("nij,fnj->fni", blocks, blocked, precision=PRECISE).reshape(fields, -1)


def on_devices(function):
    return jax.vmap(jax.vmap(function))


def inner(left, right):
    return jnp.sum(left * right, axis=(0, 1, 3))


def reference(source, periods, tiles, columns, coupling, send_list, recv_rows, counts, cycle_edges, cycle_signs, inverse_blocks):
    orient = (2 * cycle_signs - 1).astype(jnp.float32)
    penalty = 1.0 / (CYC_LEN * SLABS * SECTORS)

    def apply_full(vector):
        result = on_devices(local_part)(vector, tiles, columns)
        message = on_devices(outgoing)(vector, coupling, send_list, recv_rows, counts)
        nothing = jnp.zeros_like(message[:1, :, 1])
        from_lower = jnp.concatenate([nothing, message[:-1, :, 1]], axis=0)
        from_upper = jnp.concatenate([message[1:, :, 0], nothing], axis=0)
        from_left = jnp.roll(message[:, :, 3], 1, axis=1)
        from_right = jnp.roll(message[:, :, 2], -1, axis=1)
        incoming = jnp.stack([from_lower, from_upper, from_left, from_right], axis=2)
        result = on_devices(absorb)(result, incoming, coupling, send_list, recv_rows, counts)
        totals = jnp.sum(on_devices(period_part)(vector, cycle_edges, orient), axis=(0, 1))
        scaled = jnp.broadcast_to(penalty * totals, (SLABS, SECTORS) + totals.shape)
        return on_devices(spread)(result, cycle_edges, orient, scaled)

    prescribed = jnp.broadcast_to(periods.T, (SLABS, SECTORS, F, G))
    rhs = on_devices(spread)(source, cycle_edges, orient, prescribed)
    solution = jnp.zeros_like(source)
    residual = rhs
    smoothed = on_devices(smooth)(residual, inverse_blocks)
    direction = smoothed
    energy_now = inner(residual, smoothed)
    for iteration in range(ITERS):
        image = apply_full(direction)
        step_size = energy_now / inner(direction, image)
        solution = solution + step_size[None, None, :, None] * direction
        residual = residual - step_size[None, None, :, None] * image
        smoothed = on_devices(smooth)(residual, inverse_blocks)
        energy_next = inner(residual, smoothed)
        direction = smoothed + (energy_next / energy_now)[None, None, :, None] * direction
        energy_now = energy_next
    return solution, residual
```

```python
import functools

import jax
import jax.numpy as jnp
from jax import lax
from jax.experimental import pallas as pl
from jax.experimental.pallas import tpu as pltpu
from jax.sharding import PartitionSpec as P

TILE = 64
LANES = 128
F32 = jnp.float32
BF16 = jnp.bfloat16
HIGH = lax.Precision.HIGHEST
AXES = ("slab", "sector")


def lane_of(shape):
    return lax.broadcasted_iota(jnp.int32, shape, len(shape) - 1)


def split(x):
    hi = x.astype(BF16)
    lo = x - hi.astype(F32)
    return hi.astype(F32), lo


def turn(x):
    return pltpu.roll(x, 64, x.ndim - 1)


def into_rows():
    row = lax.broadcasted_iota(jnp.int32, (LANES, 2 * LANES), 0)
    col = lax.broadcasted_iota(jnp.int32, (LANES, 2 * LANES), 1)
    parity = col // LANES
    group = (col % LANES) // 32
    m = col % 32
    keep = (row % 64 == 2 * m + parity) & (row // 64 == group % 2)
    return jnp.where(keep, 1.0, 0.0).astype(BF16)


def out_of_rows():
    row = lax.broadcasted_iota(jnp.int32, (LANES, 2 * LANES), 0)
    col = lax.broadcasted_iota(jnp.int32, (LANES, 2 * LANES), 1)
    keep = (col % 64) == 2 * (row % 32) + col // LANES
    return jnp.where(keep, 1.0, 0.0).astype(BF16)


def tile_split(ref, start, stride):
    v = ref[pl.ds(start, 32, stride=stride), :]
    hi = v.astype(BF16)
    lo = (v - hi.astype(F32)).astype(BF16)
    return hi, lo


def dot(a, b):
    return lax.dot_general(a, b, (((1,), (0,)), ((), ())), preferred_element_type=F32)


def dot_nt(a, b):
    return lax.dot_general(a, b, (((1,), (1,)), ((), ())), preferred_element_type=F32)


def fold(out, nf):
    t = jnp.where(lane_of((nf, LANES)) < 64, out[:nf], out[nf:])
    return t + turn(t)


def left_form(x, nf):
    low = lane_of(x.shape) < 64
    hi, lo = split(x)
    zero = jnp.zeros_like(hi)
    return jnp.concatenate(
        [jnp.where(low, hi, zero), jnp.where(low, zero, hi), jnp.where(low, lo, zero), jnp.where(low, zero, lo)],
        axis=0,
    ).astype(BF16)


def write_row_form(load, y_ref, nf, blocks, matrix):
    step = 8

    def body(i, carry):
        parts = [load(i * step + j) for j in range(step)]
        x = jnp.concatenate(parts, axis=0)
        hi, lo = split(x)
        mixed = jnp.where(lane_of(x.shape) < 64, hi, lo).astype(BF16)
        out = dot(mixed, matrix)
        for j in range(step):
            o = out[j * nf : (j + 1) * nf]
            y_ref[i * step + j] = jnp.concatenate([o[:, :LANES], o[:, LANES:]], axis=0).astype(BF16)
        return carry

    lax.fori_loop(0, blocks // step, body, 0)


def pick_two(u):
    hi, lo = split(u)
    return jnp.where(lane_of(u.shape) < 64, hi, lo).astype(BF16)


def mat_t(y, hi, lo, nf):
    w = jnp.concatenate([hi, hi, lo, lo], axis=0)
    return fold(dot(y, w), nf)


def to_natural(ref, row, nat_ref, blocks):
    for t in range(blocks // 2):
        a = ref[2 * t]
        b = ref[2 * t + 1]
        rows = nat_ref.shape[0]
        low = lane_of((rows, LANES)) < 64
        nat_ref[:, t * LANES : (t + 1) * LANES] = jnp.where(low, a[row : row + rows], b[row : row + rows])


def smooth_into(inv_ref, y_ref, out_ref, nf, blocks):
    def body(g, carry):
        for c in range(8):
            hi, lo = tile_split(inv_ref, g * 256 + c, 8)
            out_ref[g * 8 + c] = mat_t(y_ref[g * 8 + c], hi, lo, nf)
        return carry

    lax.fori_loop(0, blocks // 8, body, 0)


def write_messages(load, y_ref, coup_ref, send_ref, recv_ref, counts_ref, msgs, nf, cap):
    low = lane_of((nf, LANES)) < 64
    for d in range(4):
        def body(g, carry, d=d):
            for j in range(8):
                c = g * 8 + j
                hi, lo = tile_split(coup_ref, d * cap * 32 + g * 256 + j, 8)
                partner = mat_t(y_ref[recv_ref[d, c]], hi, lo, nf)
                weight = jnp.where(c < counts_ref[0, 0, d], 1.0, 0.0)
                msgs[d][c] = jnp.where(low, load(send_ref[d, c]) * weight, partner)
            return carry

        lax.fori_loop(0, cap // 8, body, 0)


def first_kernel(nf, blocks, cap, src_ref, per_ref, edges_ref, signs_ref, inv_ref, coup_ref, send_ref, recv_ref, counts_ref,
                 m0, m1, m2, m3, z_ref, zn_ref, r0_ref, cd_ref, y_ref, x_ref, y0_ref):
    fields = src_ref.shape[0]
    width = src_ref.shape[1]
    edges = edges_ref[...]
    orient = (2 * signs_ref[...] - 1).astype(F32)
    place = lax.broadcasted_iota(jnp.int32, (edges.shape[0], LANES), 1)
    low = lane_of((fields, LANES)) < 64

    def cycles(t, carry):
        here = place + t * LANES
        total = jnp.zeros((edges.shape[0], LANES), F32)
        for l in range(edges.shape[1]):
            total = jnp.where(edges[:, l : l + 1] == here, orient[:, l : l + 1], total)
        cd_ref[:, pl.ds(pl.multiple_of(t * LANES, LANES), LANES)] = total
        return carry

    lax.fori_loop(0, width // LANES, cycles, 0)
    r0_ref[...] = src_ref[...] + lax.dot_general(
        per_ref[...], cd_ref[...], (((0,), (0,)), ((), ())), precision=HIGH, preferred_element_type=F32)
    for t in range(width // LANES):
        r = r0_ref[:, t * LANES : (t + 1) * LANES]
        c = cd_ref[:, t * LANES : (t + 1) * LANES]
        rt = turn(r)
        ct = turn(c)
        x_ref[2 * t] = jnp.concatenate([jnp.where(low, r, rt), jnp.where(low, c, ct)], axis=0)
        x_ref[2 * t + 1] = jnp.concatenate([jnp.where(low, rt, r), jnp.where(low, ct, c)], axis=0)
    matrix = into_rows()
    write_row_form(lambda b: x_ref[b], y0_ref, nf, blocks, matrix)
    smooth_into(inv_ref, y0_ref, z_ref, nf, blocks)
    write_row_form(lambda b: z_ref[b], y_ref, nf, blocks, matrix)
    write_messages(lambda b: z_ref[b], y_ref, coup_ref, send_ref, recv_ref, counts_ref, (m0, m1, m2, m3), nf, cap)
    to_natural(z_ref, 0, zn_ref, blocks)


def local_kernel(nf, blocks, kt, cols_ref, tiles_ref, z_ref, y_ref, acc_ref, x_ref, u_ref, t_ref):
    def left(b, carry):
        x_ref[b] = left_form(z_ref[b], nf)
        return carry

    lax.fori_loop(0, blocks, left, 0, unroll=4)

    def body(i, carry):
        for s in range(2):
            b = i * 2 + s
            pieces = [tile_split(tiles_ref, b * (32 * kt) + k, kt) for k in range(kt)]
            y = y_ref[b]
            u = None
            for k in range(kt):
                hi, lo = pieces[k]
                out = dot(y, jnp.concatenate([hi, hi, lo, lo], axis=0))
                t_ref[k, b] = jnp.where(lane_of((nf, LANES)) < 64, out[:nf], out[nf:])
                col = lax.rem(b + cols_ref[0, k], blocks)
                part = dot_nt(x_ref[col], jnp.concatenate([hi, lo, hi, lo], axis=0))
                u = part if u is None else u + part
            u_ref[b] = pick_two(u[: 2 * nf] + u[2 * nf :])
        return carry

    lax.fori_loop(0, blocks // 2, body, 0)
    matrix = out_of_rows()

    def finish(i, carry):
        rows = u_ref[pl.ds(i * 8, 8)].reshape(8 * 2 * nf, LANES)
        out = dot(rows, matrix)
        for j in range(8):
            b = i * 8 + j
            o = out[j * 2 * nf : (j + 1) * 2 * nf]
            t = None
            for k in range(kt):
                v = t_ref[k, lax.rem(b + blocks - cols_ref[0, k], blocks)]
                t = v if t is None else t + v
            acc_ref[b] = z_ref[b] + o[:nf, :LANES] + o[nf:, LANES:] + t + turn(t)
        return carry

    lax.fori_loop(0, blocks // 8, finish, 0)


def absorb(acc_ref, incs, coup_ref, send_ref, recv_ref, counts_ref, nf, cap):
    matrix = out_of_rows()
    low = lane_of((nf, LANES)) < 64
    for d in range(4):
        def body(g, carry, d=d):
            rows = []
            back = []
            for j in range(8):
                c = g * 8 + j
                arr = incs[d][c]
                first = jnp.where(low, arr, 0.0)
                second = arr - first
                hi, lo = split(first)
                x = jnp.concatenate([hi, turn(hi), lo, turn(lo)], axis=0).astype(BF16)
                whi, wlo = tile_split(coup_ref, d * cap * 32 + g * 256 + j, 8)
                u = dot_nt(x, jnp.concatenate([whi, wlo, whi, wlo], axis=0))
                rows.append(pick_two(u[: 2 * nf] + u[2 * nf :]))
                weight = jnp.where(c < counts_ref[0, 0, d], 1.0, 0.0)
                back.append((second + turn(second)) * weight)
            out = dot(jnp.concatenate(rows, axis=0), matrix)
            spots = [recv_ref[d, g * 8 + j] for j in range(8)]
            old = [acc_ref[s] for s in spots]
            for j in range(8):
                o = out[j * 2 * nf : (j + 1) * 2 * nf]
                acc_ref[spots[j]] = old[j] + (o[:nf, :LANES] + o[nf:, LANES:])
            spots = [send_ref[d, g * 8 + j] for j in range(8)]
            old = [acc_ref[s] for s in spots]
            for j in range(8):
                acc_ref[spots[j]] = old[j] + back[j]
            return carry

        lax.fori_loop(0, cap // 8, body, 0)


def second_kernel(nf, blocks, cap, acc_in, i0, i1, i2, i3, inv_ref, coup_ref, send_ref, recv_ref, counts_ref,
                  m0, m1, m2, m3, qn_ref, w_ref, wn_ref, y_ref, acc_ref, y0_ref):
    acc_ref[...] = acc_in[...]
    absorb(acc_ref, (i0, i1, i2, i3), coup_ref, send_ref, recv_ref, counts_ref, 2 * nf, cap)
    to_natural(acc_ref, 0, qn_ref, blocks)
    matrix = into_rows()
    write_row_form(lambda b: acc_ref[b, 0:nf], y0_ref, nf, blocks, matrix)
    smooth_into(inv_ref, y0_ref, w_ref, nf, blocks)
    write_row_form(lambda b: w_ref[b], y_ref, nf, blocks, matrix)
    write_messages(lambda b: w_ref[b], y_ref, coup_ref, send_ref, recv_ref, counts_ref, (m0, m1, m2, m3), nf, cap)
    to_natural(w_ref, 0, wn_ref, blocks)


def column_of(values, lane, at):
    return jnp.sum(jnp.where(lane == at, values, 0.0), axis=1, keepdims=True)


def third_kernel(nf, blocks, cap, acc_in, i0, i1, i2, i3, coup_ref, send_ref, recv_ref, counts_ref,
                 zn_ref, qn_ref, wn_ref, r0_ref, cd_ref, sn_ref, pay_ref, acc_ref, g_ref):
    acc_ref[...] = acc_in[...]
    absorb(acc_ref, (i0, i1, i2, i3), coup_ref, send_ref, recv_ref, counts_ref, nf, cap)
    to_natural(acc_ref, 0, sn_ref, blocks)
    z = zn_ref[0:nf, :]
    q = qn_ref[0:nf, :]
    w = wn_ref[...]
    r = r0_ref[...]
    s = sn_ref[...]

    def inner(a, b):
        return jnp.sum(a * b, axis=1, keepdims=True)

    gamma = inner(r, z)
    base = inner(z, q)
    safe = jnp.where(base > 0.0, base, 1.0)
    centre = jnp.where(base > 0.0, jnp.clip(gamma / safe, 0.0, 4.0), 0.0)
    zc = z - centre * w
    kz = q - centre * s
    values = [
        gamma,
        base,
        centre,
        inner(r - centre * q, zc),
        inner(q, zc),
        inner(q, w),
        inner(zc, kz),
        inner(zc, s),
        inner(w, s),
    ]
    left_hi, left_lo = split(jnp.concatenate([z, w, zn_ref[nf:, :]], axis=0))
    right_hi, right_lo = split(jnp.concatenate([cd_ref[...], qn_ref[nf:, :]], axis=0))
    left = jnp.concatenate([left_hi, left_lo], axis=0).astype(BF16)
    products = dot_nt(left, right_hi.astype(BF16)) + dot_nt(left, right_lo.astype(BF16))
    g_ref[...] = jnp.zeros_like(g_ref)
    g_ref[:, 0:16] = products[:24] + products[24:]
    lane = lane_of((nf, LANES))
    pay = g_ref[0:8, :] + pltpu.roll(g_ref[8:16, :], 32, 1) + pltpu.roll(g_ref[16:24, :], 64, 1)
    for at, value in enumerate(values):
        pay = jnp.where(lane == 16 + at, value, pay)
    pay_ref[...] = pay


def last_kernel(nf, rho, all_ref, zn_ref, wn_ref, qn_ref, r0_ref, cd_ref, sn_ref, x_ref, res_ref):
    lane = lane_of((nf, LANES))
    total = all_ref[0]
    for d in range(1, all_ref.shape[0]):
        total = total + all_ref[d]

    def mat(x):
        return lax.dot_general(x[0], x[1], (((1,), (0,)), ((), ())), precision=HIGH, preferred_element_type=F32)

    t0 = total[:, 0:8]
    z_h = total[:, 8:16]
    cw = total[:, 32:40]
    w_h = total[:, 40:48]
    b = total[:, 64:72]
    d_h = total[:, 72:80]
    gamma0 = column_of(total, lane, 16)
    base = column_of(total, lane, 17) + rho * jnp.sum(t0 * t0, axis=1, keepdims=True)
    alpha0 = gamma0 / base

    def about(d, carry):
        g1, kz = carry
        part = all_ref[d]
        off = alpha0 - column_of(part, lane, 18)
        g1 = g1 + column_of(part, lane, 19) - 2.0 * off * column_of(part, lane, 20) + off * off * column_of(part, lane, 21)
        kz = kz + column_of(part, lane, 22) - 2.0 * off * column_of(part, lane, 23) + off * off * column_of(part, lane, 24)
        return g1, kz

    zero = jnp.zeros((nf, 1), F32)
    gamma1, delta = lax.fori_loop(0, all_ref.shape[0], about, (zero, zero))
    t0b = mat((t0, b))
    t0d = mat((t0, d_h))
    step = alpha0 * rho
    gamma1 = gamma1 - 2.0 * step * jnp.sum(t0 * (t0 - alpha0 * cw), axis=1, keepdims=True)
    gamma1 = gamma1 + step * step * jnp.sum(t0 * t0b, axis=1, keepdims=True)
    delta = delta - 2.0 * step * jnp.sum(t0 * (z_h - alpha0 * w_h), axis=1, keepdims=True)
    delta = delta + step * step * jnp.sum(t0 * t0d, axis=1, keepdims=True)
    tw = cw + rho * t0b
    cz = t0 - alpha0 * tw
    delta = delta + rho * jnp.sum(cz * cz, axis=1, keepdims=True)
    beta = gamma1 / gamma0
    alpha1 = gamma1 / (delta - beta * (gamma1 / alpha0))
    both = alpha0 * alpha1
    lead = alpha0 + alpha1 * (1.0 + beta)
    x_ref[...] = lead * zn_ref[0:nf, :] - both * wn_ref[...] + mat((-(both * rho) * t0, zn_ref[nf:, :]))
    res_ref[...] = (
        r0_ref[...] - lead * qn_ref[0:nf, :] + both * sn_ref[...]
        + mat((rho * (both * tw - lead * t0), cd_ref[...]))
        + mat((both * rho * t0, qn_ref[nf:, :]))
    )


SMEM = pl.BlockSpec(memory_space=pltpu.SMEM)
VMEM = pl.BlockSpec(memory_space=pltpu.VMEM)
PARAMS = pltpu.CompilerParams(vmem_limit_bytes=56 * 1024 * 1024)


def like(*shape, dtype=F32):
    return jax.ShapeDtypeStruct(shape, dtype)


def call(kernel, ins, outs, scratch, name, flops=0):
    return pl.pallas_call(
        kernel, in_specs=ins, out_shape=outs, out_specs=jax.tree.map(lambda _: VMEM, outs), scratch_shapes=scratch,
        compiler_params=PARAMS, name=name,
        cost_estimate=pl.CostEstimate(flops=flops, transcendentals=0, bytes_accessed=8 << 20) if flops else None)


def exchange(msgs):
    slabs = lax.axis_size("slab")
    sectors = lax.axis_size("sector")
    up = [(i, i + 1) for i in range(slabs - 1)]
    down = [(i + 1, i) for i in range(slabs - 1)]
    right = [(i, (i + 1) % sectors) for i in range(sectors)]
    left = [((i + 1) % sectors, i) for i in range(sectors)]
    return (
        lax.ppermute(msgs[1], "slab", up),
        lax.ppermute(msgs[0], "slab", down),
        lax.ppermute(msgs[3], "sector", right),
        lax.ppermute(msgs[2], "sector", left),
    )


def rows_of(x, group):
    n = x.shape[0]
    return x.reshape(n // group, group, 32, LANES).transpose(0, 2, 1, 3).reshape(n * 32, LANES)


def on_device(source, periods, tiles, columns, coupling, send_list, recv_rows, counts, cycle_edges, cycle_signs, inverse_blocks):
    src = source[0, 0]
    nf, width = src.shape
    blocks = width // TILE
    kt = tiles.shape[3]
    cap = coupling.shape[3]
    cycles = periods.shape[0]
    both = nf + cycles
    devices = lax.axis_size("slab") * lax.axis_size("sector")
    rho = 1.0 / (cycle_edges.shape[3] * devices)
    tiles2 = rows_of(tiles[0, 0].reshape(blocks * kt, TILE * TILE), kt)
    coup2 = rows_of(coupling[0, 0].reshape(4 * cap, TILE * TILE), 8)
    inv2 = rows_of(inverse_blocks[0, 0], 8)
    send, recv, cols = send_list[0, 0], recv_rows[0, 0], columns[0, 0]

    msg = like(cap, both, LANES)
    *msgs, z, zn, r0, cd, y = call(
        functools.partial(first_kernel, both, blocks, cap),
        [VMEM] * 6 + [SMEM] * 3,
        [msg] * 4 + [like(blocks, both, LANES), like(both, width), like(nf, width), like(cycles, width),
                     like(blocks, 2 * both, LANES, dtype=BF16)],
        [pltpu.VMEM((blocks, both, LANES), F32), pltpu.VMEM((blocks, 2 * both, LANES), BF16)],
        "first",
    )(src, periods, cycle_edges[0, 0], cycle_signs[0, 0], inv2, coup2, send, recv, counts)

    def local(vector, y, n):
        return call(
            functools.partial(local_kernel, n, blocks, kt),
            [SMEM] + [VMEM] * 3,
            like(blocks, n, LANES),
            [pltpu.VMEM((blocks, 4 * n, LANES), BF16), pltpu.VMEM((blocks, 2 * n, LANES), BF16),
             pltpu.VMEM((kt, blocks, n, LANES), F32)],
            "local", flops=2 * 10**9,
        )(cols, tiles2, vector, y)

    incoming = exchange(msgs)
    acc = local(z, y, both)
    msg = like(cap, nf, LANES)
    *msgs, qn, w, wn, y = call(
        functools.partial(second_kernel, nf, blocks, cap),
        [VMEM] * 7 + [SMEM] * 3,
        [msg] * 4 + [like(both, width), like(blocks, nf, LANES), like(nf, width), like(blocks, 2 * nf, LANES, dtype=BF16)],
        [pltpu.VMEM((blocks, both, LANES), F32), pltpu.VMEM((blocks, 2 * nf, LANES), BF16)],
        "second",
    )(acc, *incoming, inv2, coup2, send, recv, counts)
    incoming = exchange(msgs)
    acc = local(w, y, nf)
    sn, pay = call(
        functools.partial(third_kernel, nf, blocks, cap),
        [VMEM] * 6 + [SMEM] * 3 + [VMEM] * 5,
        [like(nf, width), like(nf, LANES)],
        [pltpu.VMEM((blocks, nf, LANES), F32), pltpu.VMEM((24, LANES), F32)],
        "third",
    )(acc, *incoming, coup2, send, recv, counts, zn, qn, wn, r0, cd)
    everyone = lax.all_to_all(jnp.broadcast_to(pay[None], (devices,) + pay.shape), AXES, 0, 0)
    out, res = call(
        functools.partial(last_kernel, nf, rho),
        [VMEM] * 7,
        [like(nf, width), like(nf, width)],
        [],
        "last",
    )(everyone, zn, wn, qn, r0, cd, sn)
    return out[None, None], res[None, None]


def solution(mesh):
    two = P("slab", "sector")
    return jax.shard_map(
        on_device,
        mesh=mesh,
        in_specs=(two, P(), two, two, two, two, two, two, two, two, two),
        out_specs=(two, two),
        check_vma=False,
    )
```

```python
import functools

import jax
import jax.numpy as jnp
from jax import lax
from jax.experimental import pallas as pl
from jax.experimental.pallas import tpu as pltpu
from jax.sharding import PartitionSpec as P

TILE = 64
LANES = 128
F32 = jnp.float32
BF16 = jnp.bfloat16
AXES = ("slab", "sector")
ROWS_STEP = 32
SMOOTH_STEP = 32
SEND_STEP = 32
ABSORB_STEP = 32
LOCAL_STEP = 8


def lane_of(shape):
    return lax.broadcasted_iota(jnp.int32, shape, len(shape) - 1)


def split(x):
    hi = x.astype(BF16)
    lo = x - hi.astype(F32)
    return hi.astype(F32), lo


def turn(x):
    return pltpu.roll(x, 64, x.ndim - 1)


def into_rows():
    row = lax.broadcasted_iota(jnp.int32, (LANES, LANES), 0)
    col = lane_of((LANES, LANES))
    return jnp.where(row == 2 * (col % 32) + (col // 32) % 2, 1.0, 0.0).astype(BF16)


def out_of_rows():
    row = lax.broadcasted_iota(jnp.int32, (LANES, LANES), 0)
    col = lane_of((LANES, LANES))
    return jnp.where(col % 64 == 2 * (row % 32) + (row // 32) % 2, 1.0, 0.0).astype(BF16)


def stacked(x):
    hi, lo = split(x)
    return jnp.concatenate([hi, lo], axis=0).astype(BF16)


def single(ref, start, stride):
    v = ref[pl.ds(start, 32, stride=stride), :]
    t = turn(v)
    low = lane_of(v.shape) < 64
    return stacked(jnp.concatenate([jnp.where(low, v, t), jnp.where(low, t, v)], axis=0))


def pair(ref, start, stride):
    a = ref[pl.ds(start, 32, stride=stride), :]
    b = ref[pl.ds(start + 1, 32, stride=stride), :]
    low = lane_of(a.shape) < 64
    return stacked(jnp.concatenate([jnp.where(low, a, turn(b)), jnp.where(low, turn(a), b)], axis=0))


def dot(a, b):
    return lax.dot_general(a, b, (((1,), (0,)), ((), ())), preferred_element_type=F32)


def dot_nt(a, b):
    return lax.dot_general(a, b, (((1,), (1,)), ((), ())), preferred_element_type=F32)


def halves(out, nf):
    return out[:nf] + out[nf:]


def write_row_form(load, y_ref, nf, blocks, matrix):
    def body(i, carry):
        x = jnp.concatenate([stacked(load(i * ROWS_STEP + j)) for j in range(ROWS_STEP)], axis=0)
        out = dot(x, matrix).astype(BF16)
        for j in range(ROWS_STEP):
            y_ref[i * ROWS_STEP + j] = out[j * 2 * nf : (j + 1) * 2 * nf]
        return carry

    lax.fori_loop(0, blocks // ROWS_STEP, body, 0)


def to_natural(ref, nat_ref, blocks):
    rows = nat_ref.shape[0]
    low = lane_of((rows, LANES)) < 64
    for t in range(blocks // 2):
        a = ref[2 * t]
        b = ref[2 * t + 1]
        nat_ref[:, t * LANES : (t + 1) * LANES] = jnp.where(low, a[:rows], b[:rows])


def smooth_into(inv_ref, y_ref, out_ref, nf, blocks):
    def body(g, carry):
        for c in range(SMOOTH_STEP):
            w = single(inv_ref, g * (32 * SMOOTH_STEP) + (c // 8) * 256 + c % 8, 8)
            out_ref[g * SMOOTH_STEP + c] = halves(dot(y_ref[g * SMOOTH_STEP + c], w), nf)
        return carry

    lax.fori_loop(0, blocks // SMOOTH_STEP, body, 0)


def write_messages(load, y_ref, coup, send_ref, recv_ref, counts_ref, msgs, nf, cap):
    low = lane_of((nf, LANES)) < 64
    for d in range(4):
        coup_ref = coup(d)

        def body(g, carry, d=d, coup_ref=coup_ref):
            for j in range(SEND_STEP):
                c = g * SEND_STEP + j
                w = single(coup_ref, d * cap * 32 + g * (32 * SEND_STEP) + (j // 8) * 256 + j % 8, 8)
                partner = halves(dot(y_ref[recv_ref[d, c]], w), nf)
                weight = jnp.where(c < counts_ref[0, 0, d], 1.0, 0.0)
                msgs[d][c] = jnp.where(low, load(send_ref[d, c]) * weight, partner)
            return carry

        lax.fori_loop(0, cap // SEND_STEP, body, 0)


class Copies:
    def __init__(self, sems, pairs):
        self.copies = [pltpu.make_async_copy(a, b, sems.at[i]) for i, (a, b) in enumerate(pairs)]
        for copy in self.copies:
            copy.start()

    def wait(self, i):
        self.copies[i].wait()


def quarters(hbm, vmem):
    rows = vmem.shape[0] // 4
    return [(hbm.at[pl.ds(d * rows, rows)], vmem.at[pl.ds(d * rows, rows)]) for d in range(4)]


def weighted_rows(coef, rows, at):
    out = None
    for g in range(coef.shape[1]):
        term = coef[:, g : g + 1] * rows[g : g + 1, at]
        out = term if out is None else out + term
    return out


def first_kernel(nf, blocks, cap, src_ref, per_ref, edges_ref, signs_ref, inv_hbm, coup_hbm, send_ref, recv_ref, counts_ref,
                 m0, m1, m2, m3, z_ref, zn_ref, r0_ref, cd_ref, y_ref, x_ref, y0_ref, inv_ref, coup_ref, sems):
    copies = Copies(sems, [(inv_hbm, inv_ref)] + quarters(coup_hbm, coup_ref))
    fields = src_ref.shape[0]
    width = src_ref.shape[1]
    count = edges_ref.shape[0]
    edges = edges_ref[...]
    orient = (2 * signs_ref[...] - 1).astype(F32)
    low = lane_of((fields, LANES)) < 64
    step = 8 * LANES
    place = lane_of((count, step))
    totals = per_ref[...].T

    def cycles(t, carry):
        at = pl.ds(pl.multiple_of(t * step, step), step)
        here = place + t * step
        total = jnp.zeros((count, step), F32)
        for l in range(edges.shape[1]):
            total = jnp.where(edges[:, l : l + 1] == here, orient[:, l : l + 1], total)
        cd_ref[:, at] = total
        r0_ref[:, at] = src_ref[:, at] + weighted_rows(totals, cd_ref, at)
        return carry

    lax.fori_loop(0, width // step, cycles, 0)
    for t in range(width // LANES):
        r = r0_ref[:, t * LANES : (t + 1) * LANES]
        c = cd_ref[:, t * LANES : (t + 1) * LANES]
        rt = turn(r)
        ct = turn(c)
        x_ref[2 * t] = jnp.concatenate([jnp.where(low, r, rt), jnp.where(low, c, ct)], axis=0)
        x_ref[2 * t + 1] = jnp.concatenate([jnp.where(low, rt, r), jnp.where(low, ct, c)], axis=0)
    matrix = into_rows()
    write_row_form(lambda b: x_ref[b], y0_ref, nf, blocks, matrix)
    copies.wait(0)
    smooth_into(inv_ref, y0_ref, z_ref, nf, blocks)
    write_row_form(lambda b: z_ref[b], y_ref, nf, blocks, matrix)

    def coup(d):
        copies.wait(1 + d)
        return coup_ref

    write_messages(lambda b: z_ref[b], y_ref, coup, send_ref, recv_ref, counts_ref, (m0, m1, m2, m3), nf, cap)
    to_natural(z_ref, zn_ref, blocks)


def local_kernel(nf, blocks, kt, cols_ref, tiles_hbm, z_ref, y_ref, acc_ref, x_ref, u_ref, t_ref, tiles_ref, sems):
    rows = LOCAL_STEP * kt * 32

    def copy(i):
        at = pl.ds(pl.multiple_of(i * rows, rows), rows)
        return pltpu.make_async_copy(tiles_hbm.at[at], tiles_ref.at[at], sems.at[i])

    for i in range(blocks // LOCAL_STEP):
        copy(i).start()

    def left(b, carry):
        x_ref[b] = stacked(z_ref[b])
        return carry

    lax.fori_loop(0, blocks, left, 0, unroll=8)
    wide = lane_of((2 * nf, LANES)) < 64

    def body(i, carry):
        copy(i).wait()
        for s in range(LOCAL_STEP):
            b = i * LOCAL_STEP + s
            w = jnp.concatenate([pair(tiles_ref, b * (32 * kt) + k, kt) for k in range(0, kt, 2)], axis=1)
            t_ref[b] = halves(dot(y_ref[b], w), nf)
            x = [x_ref[lax.rem(b + cols_ref[k, 0], blocks)] for k in range(kt)]
            x = jnp.concatenate([jnp.where(wide, x[k], x[k + 1]) for k in range(0, kt, 2)], axis=1)
            u_ref[b] = stacked(halves(dot_nt(x, w), nf))
        return carry

    lax.fori_loop(0, blocks // LOCAL_STEP, body, 0)
    matrix = out_of_rows()
    low = lane_of((nf, LANES)) < 64

    def finish(i, carry):
        out = dot(u_ref[pl.ds(i * 8, 8)].reshape(8 * 2 * nf, LANES), matrix)
        for j in range(8):
            b = i * 8 + j
            t = None
            for k in range(0, kt, 2):
                at = slice(k // 2 * LANES, (k // 2 + 1) * LANES)
                v = jnp.where(low, t_ref[lax.rem(b + blocks - cols_ref[k, 0], blocks), :, at],
                              t_ref[lax.rem(b + blocks - cols_ref[k + 1, 0], blocks), :, at])
                t = v if t is None else t + v
            acc_ref[b] = z_ref[b] + halves(out[j * 2 * nf : (j + 1) * 2 * nf], nf) + t + turn(t)
        return carry

    lax.fori_loop(0, blocks // 8, finish, 0)


def absorb(acc_ref, incs, coup, send_ref, recv_ref, counts_ref, nf, cap):
    matrix = out_of_rows()
    low = lane_of((nf, LANES)) < 64
    for d in range(4):
        coup_ref = coup(d)

        def body(g, carry, d=d, coup_ref=coup_ref):
            rows = []
            back = []
            for j in range(ABSORB_STEP):
                c = g * ABSORB_STEP + j
                arr = incs[d][c]
                hi, lo = split(arr)
                x = jnp.where(low, hi, turn(lo)).astype(BF16)
                w = single(coup_ref, d * cap * 32 + g * (32 * ABSORB_STEP) + (j // 8) * 256 + j % 8, 8)
                rows.append(stacked(dot_nt(x, w)))
                weight = jnp.where(c < counts_ref[0, 0, d], 1.0, 0.0)
                back.append(jnp.where(low, turn(arr), arr) * weight)
            out = dot(jnp.concatenate(rows, axis=0), matrix)
            spots = [recv_ref[d, g * ABSORB_STEP + j] for j in range(ABSORB_STEP)]
            old = [acc_ref[s] for s in spots]
            for j in range(ABSORB_STEP):
                acc_ref[spots[j]] = old[j] + halves(out[j * 2 * nf : (j + 1) * 2 * nf], nf)
            spots = [send_ref[d, g * ABSORB_STEP + j] for j in range(ABSORB_STEP)]
            old = [acc_ref[s] for s in spots]
            for j in range(ABSORB_STEP):
                acc_ref[spots[j]] = old[j] + back[j]
            return carry

        lax.fori_loop(0, cap // ABSORB_STEP, body, 0)


def gathered(copies, coup_ref):
    def coup(d):
        copies.wait(2 * d)
        copies.wait(2 * d + 1)
        return coup_ref

    return coup


def arrivals(incs, inc_ref, coup_hbm, coup_ref):
    pairs = []
    for d, part in enumerate(quarters(coup_hbm, coup_ref)):
        pairs += [(incs[d], inc_ref.at[d]), part]
    return pairs


def second_kernel(nf, blocks, cap, acc_in, i0, i1, i2, i3, inv_hbm, coup_hbm, send_ref, recv_ref, counts_ref,
                  m0, m1, m2, m3, qn_ref, w_ref, wn_ref, y_ref, acc_ref, y0_ref, inv_ref, coup_ref, inc_ref, sems):
    copies = Copies(sems, arrivals((i0, i1, i2, i3), inc_ref, coup_hbm, coup_ref) + [(inv_hbm, inv_ref)])
    acc_ref[...] = acc_in[...]
    incs = [inc_ref.at[d] for d in range(4)]
    absorb(acc_ref, incs, gathered(copies, coup_ref), send_ref, recv_ref, counts_ref, 2 * nf, cap)
    to_natural(acc_ref, qn_ref, blocks)
    matrix = into_rows()
    write_row_form(lambda b: acc_ref[b, 0:nf], y0_ref, nf, blocks, matrix)
    copies.wait(8)
    smooth_into(inv_ref, y0_ref, w_ref, nf, blocks)
    write_row_form(lambda b: w_ref[b], y_ref, nf, blocks, matrix)
    write_messages(lambda b: w_ref[b], y_ref, lambda d: coup_ref, send_ref, recv_ref, counts_ref, (m0, m1, m2, m3), nf, cap)
    to_natural(w_ref, wn_ref, blocks)


def column_of(values, lane, at):
    return jnp.sum(jnp.where(lane == at, values, 0.0), axis=1, keepdims=True)


def third_kernel(nf, blocks, cap, acc_in, i0, i1, i2, i3, coup_hbm, send_ref, recv_ref, counts_ref,
                 zn_ref, qn_ref, wn_ref, r0_ref, cd_ref, sn_ref, pay_ref, acc_ref, g_ref, coup_ref, inc_ref, sems):
    copies = Copies(sems, arrivals((i0, i1, i2, i3), inc_ref, coup_hbm, coup_ref))
    acc_ref[...] = acc_in[...]
    incs = [inc_ref.at[d] for d in range(4)]
    absorb(acc_ref, incs, gathered(copies, coup_ref), send_ref, recv_ref, counts_ref, nf, cap)
    to_natural(acc_ref, sn_ref, blocks)
    z = zn_ref[0:nf, :]
    q = qn_ref[0:nf, :]
    w = wn_ref[...]
    r = r0_ref[...]
    s = sn_ref[...]

    def inner(a, b):
        return jnp.sum(a * b, axis=1, keepdims=True)

    gamma = inner(r, z)
    base = inner(z, q)
    safe = jnp.where(base > 0.0, base, 1.0)
    centre = jnp.where(base > 0.0, jnp.clip(gamma / safe, 0.0, 4.0), 0.0)
    zc = z - centre * w
    kz = q - centre * s
    values = {
        16: gamma,
        17: base,
        24: inner(r - centre * q, zc),
        25: inner(q, zc),
        26: inner(q, w),
        27: inner(zc, kz),
        28: inner(zc, s),
        29: inner(w, s),
    }
    left_hi, left_lo = split(jnp.concatenate([z, w, zn_ref[nf:, :]], axis=0))
    right_hi, right_lo = split(jnp.concatenate([cd_ref[...], qn_ref[nf:, :]], axis=0))
    left = jnp.concatenate([left_hi, left_lo], axis=0).astype(BF16)
    products = dot_nt(left, right_hi.astype(BF16)) + dot_nt(left, right_lo.astype(BF16))
    g_ref[...] = jnp.zeros_like(g_ref)
    g_ref[:, 0:16] = products[:24] + products[24:]
    lane = lane_of((nf, LANES))
    pay = g_ref[0:8, :] + pltpu.roll(g_ref[8:16, :], 32, 1) + pltpu.roll(g_ref[16:24, :], 64, 1)
    for at, value in values.items():
        pay = jnp.where(lane == at, value, pay)
    pay = jnp.where((lane >= 56) & (lane < 62), centre, pay)
    pay_ref[...] = jnp.broadcast_to(pay[None], pay_ref.shape)


def last_kernel(nf, rho, all_ref, zn_ref, wn_ref, qn_ref, r0_ref, cd_ref, sn_ref, x_ref, res_ref):
    lane = lane_of((nf, LANES))
    total = lax.fori_loop(0, all_ref.shape[0], lambda d, t: t + all_ref[d], jnp.zeros((nf, LANES), F32), unroll=16)

    def mat(a, b):
        out = None
        for g in range(a.shape[1]):
            term = a[:, g : g + 1] * b[g : g + 1, :]
            out = term if out is None else out + term
        return out

    t0 = total[:, 0:8]
    z_h = total[:, 8:16]
    cw = total[:, 32:40]
    w_h = total[:, 40:48]
    b = total[:, 64:72]
    d_h = total[:, 72:80]
    gamma0 = column_of(total, lane, 16)
    base = column_of(total, lane, 17) + rho * jnp.sum(t0 * t0, axis=1, keepdims=True)
    alpha0 = gamma0 / base
    wide = jnp.broadcast_to(alpha0, (nf, LANES))
    constant = (lane == 24) | (lane == 27)
    linear = (lane == 25) | (lane == 28)

    def about(d, carry):
        part = all_ref[d]
        off = wide - pltpu.roll(part, LANES - 32, 1)
        return carry + part * jnp.where(constant, 1.0, jnp.where(linear, -2.0 * off, off * off))

    sums = lax.fori_loop(0, all_ref.shape[0], about, jnp.zeros((nf, LANES), F32), unroll=16)
    gamma1 = jnp.sum(jnp.where((lane >= 24) & (lane < 27), sums, 0.0), axis=1, keepdims=True)
    delta = jnp.sum(jnp.where((lane >= 27) & (lane < 30), sums, 0.0), axis=1, keepdims=True)
    t0b = mat(t0, b)
    t0d = mat(t0, d_h)
    tw = cw + rho * t0b
    cz = t0 - alpha0 * tw
    step = alpha0 * rho
    gamma1 = gamma1 + step * jnp.sum(t0 * (step * t0b - 2.0 * (t0 - alpha0 * cw)), axis=1, keepdims=True)
    delta = delta + jnp.sum(step * t0 * (step * t0d - 2.0 * (z_h - alpha0 * w_h)) + rho * cz * cz, axis=1, keepdims=True)
    beta = gamma1 / gamma0
    alpha1 = gamma1 / (delta - beta * (gamma1 / alpha0))
    both = alpha0 * alpha1
    lead = alpha0 + alpha1 * (1.0 + beta)
    on_d = -(both * rho) * t0
    on_c = rho * (both * tw - lead * t0)
    chunk = 8 * LANES

    def body(i, carry):
        at = pl.ds(pl.multiple_of(i * chunk, chunk), chunk)
        x_ref[:, at] = lead * zn_ref[0:nf, at] - both * wn_ref[:, at] + weighted_rows(on_d, zn_ref.at[nf:], at)
        res_ref[:, at] = (
            r0_ref[:, at] - lead * qn_ref[0:nf, at] + both * sn_ref[:, at]
            + (weighted_rows(on_c, cd_ref, at) - weighted_rows(on_d, qn_ref.at[nf:], at))
        )
        return carry

    lax.fori_loop(0, x_ref.shape[1] // chunk, body, 0)


SMEM = pl.BlockSpec(memory_space=pltpu.SMEM)
VMEM = pl.BlockSpec(memory_space=pltpu.VMEM)
ANY = pl.BlockSpec(memory_space=pl.ANY)
PARAMS = pltpu.CompilerParams(vmem_limit_bytes=56 * 1024 * 1024)


def like(*shape, dtype=F32):
    return jax.ShapeDtypeStruct(shape, dtype)


def call(kernel, ins, outs, scratch, name, flops=0):
    return pl.pallas_call(
        kernel, in_specs=ins, out_shape=outs, out_specs=jax.tree.map(lambda _: VMEM, outs), scratch_shapes=scratch,
        compiler_params=PARAMS, name=name,
        cost_estimate=pl.CostEstimate(flops=flops, transcendentals=0, bytes_accessed=8 << 20) if flops else None)


def exchange(msgs):
    slabs = lax.axis_size("slab")
    sectors = lax.axis_size("sector")
    up = [(i, i + 1) for i in range(slabs - 1)]
    down = [(i + 1, i) for i in range(slabs - 1)]
    right = [(i, (i + 1) % sectors) for i in range(sectors)]
    left = [((i + 1) % sectors, i) for i in range(sectors)]
    return (
        lax.ppermute(msgs[1], "slab", up),
        lax.ppermute(msgs[0], "slab", down),
        lax.ppermute(msgs[3], "sector", right),
        lax.ppermute(msgs[2], "sector", left),
    )


def rows_of(x, group):
    n = x.shape[0]
    return x.reshape(n // group, group, 32, LANES).transpose(0, 2, 1, 3).reshape(n * 32, LANES)


def on_device(source, periods, tiles, columns, coupling, send_list, recv_rows, counts, cycle_edges, cycle_signs, inverse_blocks):
    src = source[0, 0]
    nf, width = src.shape
    blocks = width // TILE
    kt = tiles.shape[3]
    cap = coupling.shape[3]
    cycles = periods.shape[0]
    both = nf + cycles
    devices = lax.axis_size("slab") * lax.axis_size("sector")
    rho = 1.0 / (cycle_edges.shape[3] * devices)
    tiles2 = rows_of(tiles[0, 0].reshape(blocks * kt, TILE * TILE), kt)
    coup2 = rows_of(coupling[0, 0].reshape(4 * cap, TILE * TILE), 8)
    inv2 = rows_of(inverse_blocks[0, 0], 8)
    send, recv, cols = send_list[0, 0], recv_rows[0, 0], columns[0, 0].T
    coup_buf = pltpu.VMEM(coup2.shape, F32)
    inv_buf = pltpu.VMEM(inv2.shape, F32)

    msg = like(cap, both, LANES)
    *msgs, z, zn, r0, cd, y = call(
        functools.partial(first_kernel, both, blocks, cap),
        [VMEM] * 4 + [ANY] * 2 + [SMEM] * 3,
        [msg] * 4 + [like(blocks, both, LANES), like(both, width), like(nf, width), like(cycles, width),
                     like(blocks, 2 * both, LANES, dtype=BF16)],
        [pltpu.VMEM((blocks, both, LANES), F32), pltpu.VMEM((blocks, 2 * both, LANES), BF16), inv_buf, coup_buf,
         pltpu.SemaphoreType.DMA((5,))],
        "first",
    )(src, periods, cycle_edges[0, 0], cycle_signs[0, 0], inv2, coup2, send, recv, counts)

    def local(vector, y, n):
        return call(
            functools.partial(local_kernel, n, blocks, kt),
            [SMEM, ANY, VMEM, VMEM],
            like(blocks, n, LANES),
            [pltpu.VMEM((blocks, 2 * n, LANES), BF16), pltpu.VMEM((blocks, 2 * n, LANES), BF16),
             pltpu.VMEM((blocks, n, kt // 2 * LANES), F32), pltpu.VMEM(tiles2.shape, F32),
             pltpu.SemaphoreType.DMA((blocks // LOCAL_STEP,))],
            "local", flops=2 * 10**9,
        )(cols, tiles2, vector, y)

    incoming = exchange(msgs)
    acc = local(z, y, both)
    msg = like(cap, nf, LANES)
    *msgs, qn, w, wn, y = call(
        functools.partial(second_kernel, nf, blocks, cap),
        [VMEM] + [ANY] * 6 + [SMEM] * 3,
        [msg] * 4 + [like(both, width), like(blocks, nf, LANES), like(nf, width), like(blocks, 2 * nf, LANES, dtype=BF16)],
        [pltpu.VMEM((blocks, both, LANES), F32), pltpu.VMEM((blocks, 2 * nf, LANES), BF16), inv_buf, coup_buf,
         pltpu.VMEM((4, cap, both, LANES), F32), pltpu.SemaphoreType.DMA((9,))],
        "second",
    )(acc, *incoming, inv2, coup2, send, recv, counts)
    incoming = exchange(msgs)
    acc = local(w, y, nf)
    sn, pay = call(
        functools.partial(third_kernel, nf, blocks, cap),
        [VMEM] + [ANY] * 5 + [SMEM] * 3 + [VMEM] * 5,
        [like(nf, width), like(devices, nf, LANES)],
        [pltpu.VMEM((blocks, nf, LANES), F32), pltpu.VMEM((24, LANES), F32), coup_buf,
         pltpu.VMEM((4, cap, nf, LANES), F32), pltpu.SemaphoreType.DMA((8,))],
        "third",
    )(acc, *incoming, coup2, send, recv, counts, zn, qn, wn, r0, cd)
    everyone = lax.all_to_all(pay, AXES, 0, 0)
    out, res = call(
        functools.partial(last_kernel, nf, rho),
        [VMEM] * 7,
        [like(nf, width), like(nf, width)],
        [],
        "last",
    )(everyone, zn, wn, qn, r0, cd, sn)
    return out[None, None], res[None, None]


def solution(mesh):
    two = P("slab", "sector")
    return jax.shard_map(
        on_device,
        mesh=mesh,
        in_specs=(two, P(), two, two, two, two, two, two, two, two, two),
        out_specs=(two, two),
        check_vma=False,
    )
```

```python
import functools

import jax
import jax.numpy as jnp
from jax import lax
from jax.experimental import pallas as pl
from jax.experimental.pallas import tpu as pltpu
from jax.sharding import PartitionSpec as P

TILE = 64
LANES = 128
F32 = jnp.float32
BF16 = jnp.bfloat16
AXES = ("slab", "sector")
ROWS_STEP = 32
SMOOTH_STEP = 32
SEND_STEP = 32
ABSORB_STEP = 32
LOCAL_STEP = 16


def lane_of(shape):
    return lax.broadcasted_iota(jnp.int32, shape, len(shape) - 1)


def split(x):
    hi = x.astype(BF16)
    lo = x - hi.astype(F32)
    return hi.astype(F32), lo


def turn(x):
    return pltpu.roll(x, 64, x.ndim - 1)


def into_rows():
    row = lax.broadcasted_iota(jnp.int32, (LANES, LANES), 0)
    col = lane_of((LANES, LANES))
    return jnp.where(row == 2 * (col % 32) + (col // 32) % 2, 1.0, 0.0).astype(BF16)


def out_of_rows():
    row = lax.broadcasted_iota(jnp.int32, (LANES, LANES), 0)
    col = lane_of((LANES, LANES))
    return jnp.where(col % 64 == 2 * (row % 32) + (row // 32) % 2, 1.0, 0.0).astype(BF16)


def stacked(x):
    hi, lo = split(x)
    return jnp.concatenate([hi, lo], axis=0).astype(BF16)


def single(ref, start, stride):
    v = ref[pl.ds(start, 32, stride=stride), :]
    t = turn(v)
    low = lane_of(v.shape) < 64
    return stacked(jnp.concatenate([jnp.where(low, v, t), jnp.where(low, t, v)], axis=0))


def pair(ref, start, stride):
    a = ref[pl.ds(start, 32, stride=stride), :]
    b = ref[pl.ds(start + 1, 32, stride=stride), :]
    low = lane_of(a.shape) < 64
    return stacked(jnp.concatenate([jnp.where(low, a, turn(b)), jnp.where(low, turn(a), b)], axis=0))


def dot(a, b):
    return lax.dot_general(a, b, (((1,), (0,)), ((), ())), preferred_element_type=F32)


def dot_nt(a, b):
    return lax.dot_general(a, b, (((1,), (1,)), ((), ())), preferred_element_type=F32)


def halves(out, nf):
    return out[:nf] + out[nf:]


def write_row_form(load, y_ref, nf, blocks, matrix):
    def body(i, carry):
        x = jnp.concatenate([stacked(load(i * ROWS_STEP + j)) for j in range(ROWS_STEP)], axis=0)
        out = dot(x, matrix).astype(BF16)
        for j in range(ROWS_STEP):
            y_ref[i * ROWS_STEP + j] = out[j * 2 * nf : (j + 1) * 2 * nf]
        return carry

    lax.fori_loop(0, blocks // ROWS_STEP, body, 0)


def to_natural(ref, nat_ref, blocks):
    rows = nat_ref.shape[0]
    low = lane_of((rows, LANES)) < 64
    for t in range(blocks // 2):
        a = ref[2 * t]
        b = ref[2 * t + 1]
        nat_ref[:, t * LANES : (t + 1) * LANES] = jnp.where(low, a[:rows], b[:rows])


def made(ref, keep_ref):
    def tile(first, j):
        w = single(ref, first * 32 + (j // 8) * 256 + j % 8, 8)
        keep_ref[first + j] = w
        return w

    return tile


def kept(keep_ref):
    return lambda first, j: keep_ref[first + j]


def smooth_into(tile, y_ref, out_ref, nf, blocks):
    def body(g, carry):
        for c in range(SMOOTH_STEP):
            w = tile(g * SMOOTH_STEP, c)
            out_ref[g * SMOOTH_STEP + c] = halves(dot(y_ref[g * SMOOTH_STEP + c], w), nf)
        return carry

    lax.fori_loop(0, blocks // SMOOTH_STEP, body, 0)


def write_messages(load, y_ref, ready, tile, send_ref, recv_ref, counts_ref, msgs, nf, cap):
    low = lane_of((nf, LANES)) < 64
    for d in range(4):
        ready(d)

        def body(g, carry, d=d):
            for j in range(SEND_STEP):
                c = g * SEND_STEP + j
                w = tile(d * cap + g * SEND_STEP, j)
                partner = halves(dot(y_ref[recv_ref[d, c]], w), nf)
                weight = jnp.where(c < counts_ref[0, 0, d], 1.0, 0.0)
                msgs[d][c] = jnp.where(low, load(send_ref[d, c]) * weight, partner)
            return carry

        lax.fori_loop(0, cap // SEND_STEP, body, 0)


class Copies:
    def __init__(self, sems, pairs):
        self.copies = [pltpu.make_async_copy(a, b, sems.at[i]) for i, (a, b) in enumerate(pairs)]
        for copy in self.copies:
            copy.start()

    def wait(self, i):
        self.copies[i].wait()


def quarters(hbm, vmem):
    rows = vmem.shape[0] // 4
    return [(hbm.at[pl.ds(d * rows, rows)], vmem.at[pl.ds(d * rows, rows)]) for d in range(4)]


def weighted_rows(coef, rows, at):
    out = None
    for g in range(coef.shape[1]):
        term = coef[:, g : g + 1] * rows[g : g + 1, at]
        out = term if out is None else out + term
    return out


def first_kernel(nf, blocks, cap, src_ref, per_ref, edges_ref, signs_ref, inv_hbm, coup_hbm, send_ref, recv_ref, counts_ref,
                 m0, m1, m2, m3, z_ref, zn_ref, r0_ref, cd_ref, y_ref, winv_ref, wcoup_ref,
                 x_ref, y0_ref, inv_ref, coup_ref, sems):
    copies = Copies(sems, [(inv_hbm, inv_ref)] + quarters(coup_hbm, coup_ref))
    fields = src_ref.shape[0]
    width = src_ref.shape[1]
    count = edges_ref.shape[0]
    edges = edges_ref[...]
    orient = (2 * signs_ref[...] - 1).astype(F32)
    low = lane_of((fields, LANES)) < 64
    step = 8 * LANES
    place = lane_of((count, step))
    totals = per_ref[...].T

    def cycles(t, carry):
        at = pl.ds(pl.multiple_of(t * step, step), step)
        here = place + t * step
        total = jnp.zeros((count, step), F32)
        for l in range(edges.shape[1]):
            total = jnp.where(edges[:, l : l + 1] == here, orient[:, l : l + 1], total)
        cd_ref[:, at] = total
        r0_ref[:, at] = src_ref[:, at] + weighted_rows(totals, cd_ref, at)
        return carry

    lax.fori_loop(0, width // step, cycles, 0)
    for t in range(width // LANES):
        r = r0_ref[:, t * LANES : (t + 1) * LANES]
        c = cd_ref[:, t * LANES : (t + 1) * LANES]
        rt = turn(r)
        ct = turn(c)
        x_ref[2 * t] = jnp.concatenate([jnp.where(low, r, rt), jnp.where(low, c, ct)], axis=0)
        x_ref[2 * t + 1] = jnp.concatenate([jnp.where(low, rt, r), jnp.where(low, ct, c)], axis=0)
    matrix = into_rows()
    write_row_form(lambda b: x_ref[b], y0_ref, nf, blocks, matrix)
    copies.wait(0)
    smooth_into(made(inv_ref, winv_ref), y0_ref, z_ref, nf, blocks)
    write_row_form(lambda b: z_ref[b], y_ref, nf, blocks, matrix)

    write_messages(lambda b: z_ref[b], y_ref, lambda d: copies.wait(1 + d), made(coup_ref, wcoup_ref),
                   send_ref, recv_ref, counts_ref, (m0, m1, m2, m3), nf, cap)
    to_natural(z_ref, zn_ref, blocks)


def local_kernel(nf, blocks, kt, fresh, cols_ref, tiles_hbm, z_ref, y_ref, acc_ref, *rest):
    if fresh:
        w_ref, x_ref, u_ref, t_ref, tiles_ref, sems = rest
    else:
        x_ref, u_ref, t_ref = rest
        w_ref = tiles_hbm
    rows = LOCAL_STEP * kt * 32

    def copy(i):
        at = pl.ds(pl.multiple_of(i * rows, rows), rows)
        return pltpu.make_async_copy(tiles_hbm.at[at], tiles_ref.at[at], sems.at[i])

    if fresh:
        for i in range(blocks // LOCAL_STEP):
            copy(i).start()

    def left(b, carry):
        x_ref[b] = stacked(z_ref[b])
        return carry

    lax.fori_loop(0, blocks, left, 0, unroll=8)
    wide = lane_of((2 * nf, LANES)) < 64

    def body(i, carry):
        if fresh:
            copy(i).wait()
        for s in range(LOCAL_STEP):
            b = i * LOCAL_STEP + s
            if fresh:
                w = jnp.concatenate([pair(tiles_ref, b * (32 * kt) + k, kt) for k in range(0, kt, 2)], axis=1)
                w_ref[b] = w
            else:
                w = w_ref[b]
            t_ref[b] = halves(dot(y_ref[b], w), nf)
            x = [x_ref[lax.rem(b + cols_ref[k, 0], blocks)] for k in range(kt)]
            x = jnp.concatenate([jnp.where(wide, x[k], x[k + 1]) for k in range(0, kt, 2)], axis=1)
            u_ref[b] = stacked(halves(dot_nt(x, w), nf))
        return carry

    lax.fori_loop(0, blocks // LOCAL_STEP, body, 0)
    matrix = out_of_rows()
    low = lane_of((nf, LANES)) < 64

    def finish(i, carry):
        out = dot(u_ref[pl.ds(i * 16, 16)].reshape(16 * 2 * nf, LANES), matrix)
        for j in range(16):
            b = i * 16 + j
            t = None
            for k in range(0, kt, 2):
                at = slice(k // 2 * LANES, (k // 2 + 1) * LANES)
                v = jnp.where(low, t_ref[lax.rem(b + blocks - cols_ref[k, 0], blocks), :, at],
                              t_ref[lax.rem(b + blocks - cols_ref[k + 1, 0], blocks), :, at])
                t = v if t is None else t + v
            acc_ref[b] = z_ref[b] + halves(out[j * 2 * nf : (j + 1) * 2 * nf], nf) + t + turn(t)
        return carry

    lax.fori_loop(0, blocks // 16, finish, 0)


def present(d):
    if d > 1:
        return None
    end = 0 if d == 0 else lax.axis_size("slab") - 1
    return jnp.where(lax.axis_index("slab") == end, 0.0, 1.0)


def absorb(acc_ref, incs, tile, send_ref, recv_ref, counts_ref, nf, cap):
    matrix = out_of_rows()
    low = lane_of((nf, LANES)) < 64
    for d in range(4):
        there = present(d)

        def body(g, carry, d=d, there=there):
            rows = []
            back = []
            for j in range(ABSORB_STEP):
                c = g * ABSORB_STEP + j
                arr = incs[d][c]
                if there is not None:
                    arr = arr * there
                hi, lo = split(arr)
                x = jnp.where(low, hi, turn(lo)).astype(BF16)
                w = tile(d * cap + g * ABSORB_STEP, j)
                rows.append(stacked(dot_nt(x, w)))
                weight = jnp.where(c < counts_ref[0, 0, d], 1.0, 0.0)
                back.append(jnp.where(low, turn(arr), arr) * weight)
            out = dot(jnp.concatenate(rows, axis=0), matrix)
            spots = [recv_ref[d, g * ABSORB_STEP + j] for j in range(ABSORB_STEP)]
            old = [acc_ref[s] for s in spots]
            for j in range(ABSORB_STEP):
                acc_ref[spots[j]] = old[j] + halves(out[j * 2 * nf : (j + 1) * 2 * nf], nf)
            spots = [send_ref[d, g * ABSORB_STEP + j] for j in range(ABSORB_STEP)]
            old = [acc_ref[s] for s in spots]
            for j in range(ABSORB_STEP):
                acc_ref[spots[j]] = old[j] + back[j]
            return carry

        lax.fori_loop(0, cap // ABSORB_STEP, body, 0)


def second_kernel(nf, blocks, cap, acc_in, i0, i1, i2, i3, winv_ref, wcoup_ref, send_ref, recv_ref, counts_ref,
                  m0, m1, m2, m3, qn_ref, w_ref, wn_ref, y_ref, acc_ref, y0_ref):
    acc_ref[...] = acc_in[...]
    coup = kept(wcoup_ref)
    absorb(acc_ref, (i0, i1, i2, i3), coup, send_ref, recv_ref, counts_ref, 2 * nf, cap)
    to_natural(acc_ref, qn_ref, blocks)
    matrix = into_rows()
    write_row_form(lambda b: acc_ref[b, 0:nf], y0_ref, nf, blocks, matrix)
    smooth_into(kept(winv_ref), y0_ref, w_ref, nf, blocks)
    write_row_form(lambda b: w_ref[b], y_ref, nf, blocks, matrix)
    write_messages(lambda b: w_ref[b], y_ref, lambda d: None, coup, send_ref, recv_ref, counts_ref, (m0, m1, m2, m3), nf, cap)
    to_natural(w_ref, wn_ref, blocks)


def column_of(values, lane, at):
    return jnp.sum(jnp.where(lane == at, values, 0.0), axis=1, keepdims=True)


def third_kernel(nf, blocks, cap, acc_in, i0, i1, i2, i3, wcoup_ref, send_ref, recv_ref, counts_ref,
                 zn_ref, qn_ref, wn_ref, r0_ref, cd_ref, sn_ref, pay_ref, acc_ref, g_ref):
    acc_ref[...] = acc_in[...]
    absorb(acc_ref, (i0, i1, i2, i3), kept(wcoup_ref), send_ref, recv_ref, counts_ref, nf, cap)
    to_natural(acc_ref, sn_ref, blocks)
    z = zn_ref[0:nf, :]
    q = qn_ref[0:nf, :]
    w = wn_ref[...]
    r = r0_ref[...]
    s = sn_ref[...]

    def inner(a, b):
        return jnp.sum(a * b, axis=1, keepdims=True)

    gamma = inner(r, z)
    base = inner(z, q)
    safe = jnp.where(base > 0.0, base, 1.0)
    centre = jnp.where(base > 0.0, jnp.clip(gamma / safe, 0.0, 4.0), 0.0)
    zc = z - centre * w
    kz = q - centre * s
    values = {
        16: gamma,
        17: base,
        24: inner(r - centre * q, zc),
        25: inner(q, zc),
        26: inner(q, w),
        27: inner(zc, kz),
        28: inner(zc, s),
        29: inner(w, s),
    }
    left_hi, left_lo = split(jnp.concatenate([z, w, zn_ref[nf:, :]], axis=0))
    right_hi, right_lo = split(jnp.concatenate([cd_ref[...], qn_ref[nf:, :]], axis=0))
    left = jnp.concatenate([left_hi, left_lo], axis=0).astype(BF16)
    products = dot_nt(left, right_hi.astype(BF16)) + dot_nt(left, right_lo.astype(BF16))
    g_ref[...] = jnp.zeros_like(g_ref)
    g_ref[:, 0:16] = products[:24] + products[24:]
    lane = lane_of((nf, LANES))
    pay = g_ref[0:8, :] + pltpu.roll(g_ref[8:16, :], 32, 1) + pltpu.roll(g_ref[16:24, :], 64, 1)
    for at, value in values.items():
        pay = jnp.where(lane == at, value, pay)
    pay = jnp.where((lane >= 56) & (lane < 62), centre, pay)
    pay_ref[...] = jnp.broadcast_to(pay[None], pay_ref.shape)


def last_kernel(nf, rho, all_ref, zn_ref, wn_ref, qn_ref, r0_ref, cd_ref, sn_ref, x_ref, res_ref):
    lane = lane_of((nf, LANES))
    total = lax.fori_loop(0, all_ref.shape[0], lambda d, t: t + all_ref[d], jnp.zeros((nf, LANES), F32), unroll=16)

    def mat(a, b):
        out = None
        for g in range(a.shape[1]):
            term = a[:, g : g + 1] * b[g : g + 1, :]
            out = term if out is None else out + term
        return out

    t0 = total[:, 0:8]
    z_h = total[:, 8:16]
    cw = total[:, 32:40]
    w_h = total[:, 40:48]
    b = total[:, 64:72]
    d_h = total[:, 72:80]
    gamma0 = column_of(total, lane, 16)
    base = column_of(total, lane, 17) + rho * jnp.sum(t0 * t0, axis=1, keepdims=True)
    alpha0 = gamma0 / base
    wide = jnp.broadcast_to(alpha0, (nf, LANES))
    constant = (lane == 24) | (lane == 27)
    linear = (lane == 25) | (lane == 28)

    def about(d, carry):
        part = all_ref[d]
        off = wide - pltpu.roll(part, LANES - 32, 1)
        return carry + part * jnp.where(constant, 1.0, jnp.where(linear, -2.0 * off, off * off))

    sums = lax.fori_loop(0, all_ref.shape[0], about, jnp.zeros((nf, LANES), F32), unroll=16)
    gamma1 = jnp.sum(jnp.where((lane >= 24) & (lane < 27), sums, 0.0), axis=1, keepdims=True)
    delta = jnp.sum(jnp.where((lane >= 27) & (lane < 30), sums, 0.0), axis=1, keepdims=True)
    t0b = mat(t0, b)
    t0d = mat(t0, d_h)
    tw = cw + rho * t0b
    cz = t0 - alpha0 * tw
    step = alpha0 * rho
    gamma1 = gamma1 + step * jnp.sum(t0 * (step * t0b - 2.0 * (t0 - alpha0 * cw)), axis=1, keepdims=True)
    delta = delta + jnp.sum(step * t0 * (step * t0d - 2.0 * (z_h - alpha0 * w_h)) + rho * cz * cz, axis=1, keepdims=True)
    beta = gamma1 / gamma0
    alpha1 = gamma1 / (delta - beta * (gamma1 / alpha0))
    both = alpha0 * alpha1
    lead = alpha0 + alpha1 * (1.0 + beta)
    on_d = -(both * rho) * t0
    on_c = rho * (both * tw - lead * t0)
    chunk = 8 * LANES

    def body(i, carry):
        at = pl.ds(pl.multiple_of(i * chunk, chunk), chunk)
        x_ref[:, at] = lead * zn_ref[0:nf, at] - both * wn_ref[:, at] + weighted_rows(on_d, zn_ref.at[nf:], at)
        res_ref[:, at] = (
            r0_ref[:, at] - lead * qn_ref[0:nf, at] + both * sn_ref[:, at]
            + (weighted_rows(on_c, cd_ref, at) - weighted_rows(on_d, qn_ref.at[nf:], at))
        )
        return carry

    lax.fori_loop(0, x_ref.shape[1] // chunk, body, 0)


SMEM = pl.BlockSpec(memory_space=pltpu.SMEM)
VMEM = pl.BlockSpec(memory_space=pltpu.VMEM)
ANY = pl.BlockSpec(memory_space=pltpu.HBM)
PARAMS = pltpu.CompilerParams(vmem_limit_bytes=20 * 1024 * 1024)


def like(*shape, dtype=F32):
    return pltpu.VMEM(shape, dtype)


def in_hbm(x):
    return pltpu.with_memory_space_constraint(x, pltpu.HBM)


def call(kernel, ins, outs, scratch, name, flops=0):
    return pl.pallas_call(
        kernel, in_specs=ins, out_shape=outs, out_specs=jax.tree.map(lambda _: VMEM, outs), scratch_shapes=scratch,
        compiler_params=PARAMS, name=name,
        cost_estimate=pl.CostEstimate(flops=flops, transcendentals=0, bytes_accessed=8 << 20) if flops else None)


def exchange(msgs):
    slabs = lax.axis_size("slab")
    sectors = lax.axis_size("sector")
    up = [(i, (i + 1) % slabs) for i in range(slabs)]
    down = [((i + 1) % slabs, i) for i in range(slabs)]
    right = [(i, (i + 1) % sectors) for i in range(sectors)]
    left = [((i + 1) % sectors, i) for i in range(sectors)]
    return (
        lax.ppermute(msgs[1], "slab", up),
        lax.ppermute(msgs[0], "slab", down),
        lax.ppermute(msgs[3], "sector", right),
        lax.ppermute(msgs[2], "sector", left),
    )


def rows_of(x, group):
    n = x.shape[0]
    return x.reshape(n // group, group, 32, LANES).transpose(0, 2, 1, 3).reshape(n * 32, LANES)


def on_device(source, periods, tiles, columns, coupling, send_list, recv_rows, counts, cycle_edges, cycle_signs, inverse_blocks):
    src = source[0, 0]
    nf, width = src.shape
    blocks = width // TILE
    kt = tiles.shape[3]
    cap = coupling.shape[3]
    cycles = periods.shape[0]
    both = nf + cycles
    devices = lax.axis_size("slab") * lax.axis_size("sector")
    rho = 1.0 / (cycle_edges.shape[3] * devices)
    tiles2 = in_hbm(rows_of(tiles[0, 0].reshape(blocks * kt, TILE * TILE), kt))
    coup2 = in_hbm(rows_of(coupling[0, 0].reshape(4 * cap, TILE * TILE), 8))
    inv2 = in_hbm(rows_of(inverse_blocks[0, 0], 8))
    send, recv, cols = in_hbm(send_list[0, 0]), in_hbm(recv_rows[0, 0]), in_hbm(columns[0, 0].T)
    counts, periods, src = in_hbm(counts), in_hbm(periods), in_hbm(src)
    edges, signs = in_hbm(cycle_edges[0, 0]), in_hbm(cycle_signs[0, 0])
    msg = like(cap, both, LANES)
    *msgs, z, zn, r0, cd, y, winv, wcoup = call(
        functools.partial(first_kernel, both, blocks, cap),
        [VMEM] * 4 + [ANY] * 2 + [SMEM] * 3,
        [msg] * 4 + [like(blocks, both, LANES), like(both, width), like(nf, width), like(cycles, width),
                     like(blocks, 2 * both, LANES, dtype=BF16), like(blocks, LANES, LANES, dtype=BF16),
                     like(4 * cap, LANES, LANES, dtype=BF16)],
        [pltpu.VMEM((blocks, both, LANES), F32), pltpu.VMEM((blocks, 2 * both, LANES), BF16), pltpu.VMEM(inv2.shape, F32),
         pltpu.VMEM(coup2.shape, F32), pltpu.SemaphoreType.DMA((5,))],
        "first",
    )(src, periods, edges, signs, inv2, coup2, send, recv, counts)

    def local(vector, y, n, forms):
        fresh = forms is None
        out = [like(blocks, n, LANES)]
        scratch = [pltpu.VMEM((blocks, 2 * n, LANES), BF16), pltpu.VMEM((blocks, 2 * n, LANES), BF16),
                   pltpu.VMEM((blocks, n, kt // 2 * LANES), F32)]
        if fresh:
            out.append(like(blocks, LANES, kt // 2 * LANES, dtype=BF16))
            scratch += [pltpu.VMEM(tiles2.shape, F32), pltpu.SemaphoreType.DMA((blocks // LOCAL_STEP,))]
        return call(
            functools.partial(local_kernel, n, blocks, kt, fresh),
            [SMEM, ANY if fresh else VMEM, VMEM, VMEM], out, scratch, "local", flops=2 * 10**9,
        )(cols, tiles2 if fresh else forms, vector, y)

    incoming = exchange(msgs)
    acc, forms = local(z, y, both, None)
    msg = like(cap, nf, LANES)
    *msgs, qn, w, wn, y = call(
        functools.partial(second_kernel, nf, blocks, cap),
        [VMEM] * 7 + [SMEM] * 3,
        [msg] * 4 + [like(both, width), like(blocks, nf, LANES), like(nf, width), like(blocks, 2 * nf, LANES, dtype=BF16)],
        [pltpu.VMEM((blocks, both, LANES), F32), pltpu.VMEM((blocks, 2 * nf, LANES), BF16)],
        "second",
    )(acc, *incoming, winv, wcoup, send, recv, counts)
    incoming = exchange(msgs)
    (acc,) = local(w, y, nf, forms)
    sn, pay = call(
        functools.partial(third_kernel, nf, blocks, cap),
        [VMEM] * 6 + [SMEM] * 3 + [VMEM] * 5,
        [like(nf, width), like(devices, nf, LANES)],
        [pltpu.VMEM((blocks, nf, LANES), F32), pltpu.VMEM((24, LANES), F32)],
        "third",
    )(acc, *incoming, wcoup, send, recv, counts, zn, qn, wn, r0, cd)
    everyone = lax.all_to_all(pay, AXES, 0, 0)
    out, res = call(
        functools.partial(last_kernel, nf, rho),
        [VMEM] * 7,
        [jax.ShapeDtypeStruct((nf, width), F32)] * 2,
        [],
        "last",
    )(everyone, zn, wn, qn, r0, cd, sn)
    return out[None, None], res[None, None]


def solution(mesh):
    two = P("slab", "sector")
    return jax.shard_map(
        on_device,
        mesh=mesh,
        in_specs=(two, P(), two, two, two, two, two, two, two, two, two),
        out_specs=(two, two),
        check_vma=False,
    )
```

```python
import functools

import jax
import jax.numpy as jnp
from jax import lax
from jax.experimental import pallas as pl
from jax.experimental.pallas import tpu as pltpu
from jax.sharding import PartitionSpec as P

TILE = 64
LANES = 128
F32 = jnp.float32
BF16 = jnp.bfloat16
AXES = ("slab", "sector")
ROWS_STEP = 32
SMOOTH_STEP = 32
SEND_STEP = 32
ABSORB_STEP = 32
LOCAL_STEP = 16


def lane_of(shape):
    return lax.broadcasted_iota(jnp.int32, shape, len(shape) - 1)


def split(x):
    hi = x.astype(BF16)
    lo = x - hi.astype(F32)
    return hi.astype(F32), lo


def turn(x):
    return pltpu.roll(x, 64, x.ndim - 1)


def into_rows():
    row = lax.broadcasted_iota(jnp.int32, (LANES, LANES), 0)
    col = lane_of((LANES, LANES))
    return jnp.where(row == 2 * (col % 32) + (col // 32) % 2, 1.0, 0.0).astype(BF16)


def out_of_rows():
    row = lax.broadcasted_iota(jnp.int32, (LANES, LANES), 0)
    col = lane_of((LANES, LANES))
    return jnp.where(col % 64 == 2 * (row % 32) + (row // 32) % 2, 1.0, 0.0).astype(BF16)


def stacked(x):
    hi, lo = split(x)
    return jnp.concatenate([hi, lo], axis=0).astype(BF16)


def single(ref, start, stride):
    v = ref[pl.ds(start, 32, stride=stride), :]
    t = turn(v)
    low = lane_of(v.shape) < 64
    return stacked(jnp.concatenate([jnp.where(low, v, t), jnp.where(low, t, v)], axis=0))


def pair(ref, start, stride):
    a = ref[pl.ds(start, 32, stride=stride), :]
    b = ref[pl.ds(start + 1, 32, stride=stride), :]
    low = lane_of(a.shape) < 64
    return stacked(jnp.concatenate([jnp.where(low, a, turn(b)), jnp.where(low, turn(a), b)], axis=0))


def dot(a, b):
    return lax.dot_general(a, b, (((1,), (0,)), ((), ())), preferred_element_type=F32)


def dot_nt(a, b):
    return lax.dot_general(a, b, (((1,), (1,)), ((), ())), preferred_element_type=F32)


def rows_and_lanes(parts):
    return jnp.concatenate([jnp.concatenate(row, axis=1) for row in parts], axis=0)


def turned_products(ys, ws, nf):
    none = jnp.zeros_like(ys[0])
    left = rows_and_lanes([[ys[0], none], [ys[1], none], [none, ys[2]], [none, ys[3]]])
    out = dot(left, rows_and_lanes([ws[:2], ws[2:]]))
    n = 2 * nf
    return [halves(out[i * n : (i + 1) * n, i % 2 * LANES : (i % 2 + 1) * LANES], nf) for i in range(4)]


def straight_products(xs, ws, nf):
    none = jnp.zeros_like(xs[0])
    left = rows_and_lanes([[xs[0], none], [none, xs[1]], [xs[2], none], [none, xs[3]]]).astype(BF16)
    out = dot_nt(left, rows_and_lanes([ws[:2], ws[2:]]))
    return [out[i * nf : (i + 1) * nf, i // 2 * LANES : (i // 2 + 1) * LANES] for i in range(4)]


def halves(out, nf):
    return out[:nf] + out[nf:]


def write_row_form(load, y_ref, nf, blocks, matrix, narrow_ref=None):
    def body(i, carry):
        x = jnp.concatenate([stacked(load(i * ROWS_STEP + j)) for j in range(ROWS_STEP)], axis=0)
        out = dot(x, matrix)
        for j in range(ROWS_STEP):
            o = out[j * 2 * nf : (j + 1) * 2 * nf]
            y_ref[i * ROWS_STEP + j] = o.astype(BF16)
            if narrow_ref is not None:
                half = nf // 2
                narrow_ref[i * ROWS_STEP + j] = jnp.concatenate([o[:half], o[nf : nf + half]], axis=0).astype(BF16)
        return carry

    lax.fori_loop(0, blocks // ROWS_STEP, body, 0)


def to_natural(ref, nat_ref, blocks):
    rows = nat_ref.shape[0]
    low = lane_of((rows, LANES)) < 64
    for t in range(blocks // 2):
        a = ref[2 * t]
        b = ref[2 * t + 1]
        nat_ref[:, t * LANES : (t + 1) * LANES] = jnp.where(low, a[:rows], b[:rows])


def made(ref, keep_ref):
    def tile(first, j):
        w = single(ref, first * 32 + (j // 8) * 256 + j % 8, 8)
        keep_ref[first + j] = w
        return w

    return tile


def kept(keep_ref):
    return lambda first, j: keep_ref[first + j]


def smooth_into(tile, y_ref, out_ref, nf, blocks):
    def body(g, carry):
        for c in range(0, SMOOTH_STEP, 4):
            ws = [tile(g * SMOOTH_STEP, c + i) for i in range(4)]
            at = g * SMOOTH_STEP + c
            for i, value in enumerate(turned_products([y_ref[at + i] for i in range(4)], ws, nf)):
                out_ref[at + i] = value
        return carry

    lax.fori_loop(0, blocks // SMOOTH_STEP, body, 0)


def write_messages(load, y_ref, ready, tile, send_ref, recv_ref, counts_ref, msgs, nf, cap):
    low = lane_of((nf, LANES)) < 64
    for way in range(4):
        ready(way)
        d = sends(way)

        def body(g, carry, d=d, way=way):
            for j in range(0, SEND_STEP, 4):
                c = g * SEND_STEP + j
                ws = [tile(d * cap + g * SEND_STEP, j + i) for i in range(4)]
                ys = [y_ref[recv_ref[d, c + i]] for i in range(4)]
                for i, partner in enumerate(turned_products(ys, ws, nf)):
                    weight = jnp.where(c + i < counts_ref[0, 0, d], 1.0, 0.0)
                    value = jnp.where(low, load(send_ref[d, c + i]) * weight, partner)
                    at = 0
                    for msg in msgs[way]:
                        msg[c + i] = value[at : at + msg.shape[1]]
                        at += msg.shape[1]
            return carry

        lax.fori_loop(0, cap // SEND_STEP, body, 0)


class Copies:
    def __init__(self, sems, pairs):
        self.copies = [pltpu.make_async_copy(a, b, sems.at[i]) for i, (a, b) in enumerate(pairs)]
        for copy in self.copies:
            copy.start()

    def wait(self, i):
        self.copies[i].wait()


def quarters(hbm, vmem):
    rows = vmem.shape[0] // 4
    return [(hbm.at[pl.ds(d * rows, rows)], vmem.at[pl.ds(d * rows, rows)]) for d in range(4)]


def weighted_rows(coef, rows, at):
    out = None
    for g in range(coef.shape[1]):
        term = coef[:, g : g + 1] * rows[g : g + 1, at]
        out = term if out is None else out + term
    return out


def first_kernel(nf, blocks, cap, src_ref, per_ref, edges_ref, signs_ref, inv_hbm, coup_hbm, send_ref, recv_ref, counts_ref,
                 m0, m1, m2, m3, d0, d1, z_ref, zn_ref, r0_ref, cd_ref, narrow_ref, winv_ref, wcoup_ref,
                 x_ref, y0_ref, y_ref, inv_ref, coup_ref, sems):
    copies = Copies(sems, [(inv_hbm, inv_ref)] + quarters(coup_hbm, coup_ref))
    fields = src_ref.shape[0]
    width = src_ref.shape[1]
    count = edges_ref.shape[0]
    edges = edges_ref[...]
    orient = (2 * signs_ref[...] - 1).astype(F32)
    low = lane_of((fields, LANES)) < 64
    step = 8 * LANES
    place = lane_of((count, step))
    totals = per_ref[...].T

    def cycles(t, carry):
        at = pl.ds(pl.multiple_of(t * step, step), step)
        here = place + t * step
        total = jnp.zeros((count, step), F32)
        for l in range(edges.shape[1]):
            total = jnp.where(edges[:, l : l + 1] == here, orient[:, l : l + 1], total)
        cd_ref[:, at] = total
        r0_ref[:, at] = src_ref[:, at] + weighted_rows(totals, cd_ref, at)
        return carry

    lax.fori_loop(0, width // step, cycles, 0)
    for t in range(width // LANES):
        r = r0_ref[:, t * LANES : (t + 1) * LANES]
        c = cd_ref[:, t * LANES : (t + 1) * LANES]
        rt = turn(r)
        ct = turn(c)
        x_ref[2 * t] = jnp.concatenate([jnp.where(low, r, rt), jnp.where(low, c, ct)], axis=0)
        x_ref[2 * t + 1] = jnp.concatenate([jnp.where(low, rt, r), jnp.where(low, ct, c)], axis=0)
    matrix = into_rows()
    write_row_form(lambda b: x_ref[b], y0_ref, nf, blocks, matrix)
    copies.wait(0)
    smooth_into(made(inv_ref, winv_ref), y0_ref, z_ref, nf, blocks)
    write_row_form(lambda b: z_ref[b], y_ref, nf, blocks, matrix, narrow_ref)


    def ready(way):
        for part in ((0, 1), (), (3,), (2,))[way]:
            copies.wait(1 + part)

    write_messages(lambda b: z_ref[b], y_ref, ready, made(coup_ref, wcoup_ref),
                   send_ref, recv_ref, counts_ref, ((m0, d0), (m1, d1), (m2,), (m3,)), nf, cap)
    to_natural(z_ref, zn_ref, blocks)


def local_kernel(nf, blocks, kt, fresh, cols_ref, tiles_hbm, z_ref, y_ref, acc_ref, *rest):
    if fresh:
        w_ref, x_ref, u_ref, t_ref, tiles_ref, sems = rest
    else:
        x_ref, u_ref, t_ref = rest
        w_ref = tiles_hbm
    rows = LOCAL_STEP * kt * 32

    def copy(i):
        at = pl.ds(pl.multiple_of(i * rows, rows), rows)
        return pltpu.make_async_copy(tiles_hbm.at[at], tiles_ref.at[at], sems.at[i])

    if fresh:
        for i in range(blocks // LOCAL_STEP):
            copy(i).start()

    def left(b, carry):
        x_ref[b] = stacked(z_ref[b, 0:nf])
        return carry

    lax.fori_loop(0, blocks, left, 0, unroll=8)
    wide = lane_of((2 * nf, LANES)) < 64

    def body(i, carry):
        if fresh:
            copy(i).wait()
        for s in range(0, LOCAL_STEP, 2):
            xs, ws = [], []
            b = i * LOCAL_STEP + s
            for at in (b, b + 1):
                if fresh:
                    w = jnp.concatenate([pair(tiles_ref, at * (32 * kt) + k, kt) for k in range(0, kt, 2)], axis=1)
                    w_ref[at] = w
                    ws.append(w)
                else:
                    ws.append(w_ref[at])
                x = [x_ref[lax.rem(at + cols_ref[k, 0], blocks)] for k in range(kt)]
                xs.append(jnp.concatenate([jnp.where(wide, x[k], x[k + 1]) for k in range(0, kt, 2)], axis=1))
            w = jnp.concatenate(ws, axis=0)
            none = jnp.zeros_like(y_ref[b])
            out = dot(rows_and_lanes([[y_ref[b], none], [none, y_ref[b + 1]]]), w)
            t_ref[b] = halves(out[: 2 * nf], nf)
            t_ref[b + 1] = halves(out[2 * nf :], nf)
            out = dot_nt(jnp.concatenate(xs, axis=0), w)
            u_ref[b] = stacked(halves(out[: 2 * nf, :LANES], nf))
            u_ref[b + 1] = stacked(halves(out[2 * nf :, LANES:], nf))
        return carry

    lax.fori_loop(0, blocks // LOCAL_STEP, body, 0)
    matrix = out_of_rows()
    low = lane_of((nf, LANES)) < 64

    def finish(i, carry):
        out = dot(u_ref[pl.ds(i * 32, 32)].reshape(32 * 2 * nf, LANES), matrix)
        for j in range(32):
            b = i * 32 + j
            t = None
            for k in range(0, kt, 2):
                at = slice(k // 2 * LANES, (k // 2 + 1) * LANES)
                v = jnp.where(low, t_ref[lax.rem(b + blocks - cols_ref[k, 0], blocks), :, at],
                              t_ref[lax.rem(b + blocks - cols_ref[k + 1, 0], blocks), :, at])
                t = v if t is None else t + v
            acc_ref[b] = z_ref[b, 0:nf] + halves(out[j * 2 * nf : (j + 1) * 2 * nf], nf) + t + turn(t)
        return carry

    lax.fori_loop(0, blocks // 32, finish, 0)


def odd_sector():
    return lax.rem(lax.axis_index("sector"), 2)


def sends(way):
    return 1 - odd_sector() if way == 0 else odd_sector() if way == 1 else 5 - way


def receives(way):
    return odd_sector() if way == 0 else 1 - odd_sector() if way == 1 else way


def present(way, d):
    if way > 1:
        return None
    end = d * (lax.axis_size("slab") - 1)
    return jnp.where(lax.axis_index("slab") == end, 0.0, 1.0)


def absorb(acc_ref, incs, tile, send_ref, recv_ref, counts_ref, nf, cap):
    matrix = out_of_rows()
    low = lane_of((nf, LANES)) < 64
    for way in range(4):
        d = receives(way)
        there = present(way, d)

        def body(g, carry, d=d, way=way, there=there):
            rows = []
            back = []
            for j in range(0, ABSORB_STEP, 4):
                xs = []
                for i in range(4):
                    c = g * ABSORB_STEP + j + i
                    arr = jnp.concatenate([inc[c, at : at + nf // len(incs[way])] for inc, at in incs[way]], axis=0)
                    if there is not None:
                        arr = arr * there
                    hi, lo = split(arr)
                    xs.append(jnp.where(low, hi, turn(lo)))
                    weight = jnp.where(c < counts_ref[0, 0, d], 1.0, 0.0)
                    back.append(jnp.where(low, turn(arr), arr) * weight)
                ws = [tile(d * cap + g * ABSORB_STEP, j + i) for i in range(4)]
                rows += [stacked(u) for u in straight_products(xs, ws, nf)]
            out = dot(jnp.concatenate(rows, axis=0), matrix)
            spots = [recv_ref[d, g * ABSORB_STEP + j] for j in range(ABSORB_STEP)]
            old = [acc_ref[s] for s in spots]
            for j in range(ABSORB_STEP):
                acc_ref[spots[j]] = old[j] + halves(out[j * 2 * nf : (j + 1) * 2 * nf], nf)
            spots = [send_ref[d, g * ABSORB_STEP + j] for j in range(ABSORB_STEP)]
            old = [acc_ref[s] for s in spots]
            for j in range(ABSORB_STEP):
                acc_ref[spots[j]] = old[j] + back[j]
            return carry

        lax.fori_loop(0, cap // ABSORB_STEP, body, 0)


def second_kernel(nf, blocks, cap, acc_in, i0, i1, i2, i3, z_ref, winv_ref, wcoup_ref, send_ref, recv_ref, counts_ref,
                  m0, m1, m2, m3, qn_ref, wd_ref, wn_ref, y_ref, acc_ref, y0_ref, w_ref, narrow_ref):
    acc_ref[...] = acc_in[...]
    coup = kept(wcoup_ref)
    absorb(acc_ref, [[(inc, 0)] for inc in (i0, i1, i2, i3)], coup, send_ref, recv_ref, counts_ref, nf, cap)
    matrix = into_rows()
    write_row_form(lambda b: acc_ref[b], y0_ref, nf, blocks, matrix)
    smooth_into(kept(winv_ref), y0_ref, w_ref, nf, blocks)
    for b in range(blocks):
        wd_ref[b] = jnp.concatenate([w_ref[b], z_ref[b, nf:]], axis=0)
    write_row_form(lambda b: wd_ref[b], y_ref, wd_ref.shape[1], blocks, matrix, narrow_ref)
    write_messages(lambda b: w_ref[b], narrow_ref, lambda d: None, coup, send_ref, recv_ref, counts_ref,
                   ((m0,), (m1,), (m2,), (m3,)), nf, cap)
    to_natural(acc_ref, qn_ref, blocks)
    to_natural(w_ref, wn_ref, blocks)


def column_of(values, lane, at):
    return jnp.sum(jnp.where(lane == at, values, 0.0), axis=1, keepdims=True)


def packed(x):
    return jnp.where(lane_of((4, LANES)) < 64, x[0:4], turn(x[4:8]))


def third_kernel(nf, blocks, cap, acc_in, i0, i1, i2, i3, d0, d1, e2, e3, wcoup_ref, send_ref, recv_ref, counts_ref,
                 zn_ref, qn_ref, wn_ref, r0_ref, cd_ref, sn_ref, pay_ref, acc_ref, g_ref):
    acc_ref[...] = acc_in[...]
    incs = [[(i0, 0), (d0, 0)], [(i1, 0), (d1, 0)], [(i2, 0), (e2, nf)], [(i3, 0), (e3, nf)]]
    absorb(acc_ref, incs, kept(wcoup_ref), send_ref, recv_ref, counts_ref,
           acc_ref.shape[1], cap)
    to_natural(acc_ref, sn_ref, blocks)
    z = zn_ref[0:nf, :]
    q = qn_ref[...]
    w = wn_ref[...]
    r = r0_ref[...]
    s = sn_ref[0:nf, :]

    def inner(a, b):
        return jnp.sum(a * b, axis=1, keepdims=True)

    gamma = inner(r, z)
    base = inner(z, q)
    safe = jnp.where(base > 0.0, base, 1.0)
    centre = jnp.where(base > 0.0, jnp.clip(gamma / safe, 0.0, 4.0), 0.0)
    zc = z - centre * w
    kz = q - centre * s
    values = {
        16: gamma,
        17: base,
        18: inner(r - centre * q, zc),
        19: inner(q, zc),
        20: inner(q, w),
        21: inner(zc, kz),
        22: inner(zc, s),
        23: inner(w, s),
    }
    left_hi, left_lo = split(jnp.concatenate([z, w, zn_ref[nf:, :]], axis=0))
    right_hi, right_lo = split(jnp.concatenate([cd_ref[...], sn_ref[nf:, :]], axis=0))
    left = jnp.concatenate([left_hi, left_lo], axis=0).astype(BF16)
    products = dot_nt(left, right_hi.astype(BF16)) + dot_nt(left, right_lo.astype(BF16))
    g_ref[...] = jnp.zeros_like(g_ref)
    g_ref[:, 0:16] = products[:24] + products[24:]
    lane = lane_of((nf, LANES))
    pay = g_ref[0:8, :] + pltpu.roll(g_ref[8:16, :], 32, 1) + pltpu.roll(g_ref[16:24, :], 48, 1)
    for at, value in values.items():
        pay = jnp.where(lane == at, value, pay)
    pay = jnp.where((lane >= 24) & (lane < 30), centre, pay)
    pay_ref[...] = jnp.broadcast_to(packed(pay)[None], pay_ref.shape)


def last_kernel(nf, rho, all_ref, zn_ref, wn_ref, qn_ref, r0_ref, cd_ref, sn_ref, x_ref, res_ref):
    lane = lane_of((nf, LANES))
    total = lax.fori_loop(0, all_ref.shape[0], lambda d, t: t + all_ref[d], jnp.zeros((nf // 2, LANES), F32), unroll=16)
    total = jnp.concatenate([total, turn(total)], axis=0)

    def mat(a, b):
        out = None
        for g in range(a.shape[1]):
            term = a[:, g : g + 1] * b[g : g + 1, :]
            out = term if out is None else out + term
        return out

    t0 = total[:, 0:8]
    z_h = total[:, 8:16]
    cw = total[:, 32:40]
    w_h = total[:, 40:48]
    b = total[:, 48:56]
    d_h = total[:, 56:64]
    gamma0 = column_of(total, lane, 16)
    base = column_of(total, lane, 17) + rho * jnp.sum(t0 * t0, axis=1, keepdims=True)
    alpha0 = gamma0 / base
    wide = packed(jnp.broadcast_to(alpha0, (nf, LANES)))
    spot = lane_of((nf // 2, LANES)) % 64
    constant = (spot == 18) | (spot == 21)
    linear = (spot == 19) | (spot == 22)

    def about(d, carry):
        part = all_ref[d]
        off = wide - pltpu.roll(part, LANES - 6, 1)
        return carry + part * jnp.where(constant, 1.0, jnp.where(linear, -2.0 * off, off * off))

    sums = lax.fori_loop(0, all_ref.shape[0], about, jnp.zeros((nf // 2, LANES), F32), unroll=16)
    sums = jnp.concatenate([sums, turn(sums)], axis=0)
    gamma1 = jnp.sum(jnp.where((lane >= 18) & (lane < 21), sums, 0.0), axis=1, keepdims=True)
    delta = jnp.sum(jnp.where((lane >= 21) & (lane < 24), sums, 0.0), axis=1, keepdims=True)
    t0b = mat(t0, b)
    t0d = mat(t0, d_h)
    tw = cw + rho * t0b
    cz = t0 - alpha0 * tw
    step = alpha0 * rho
    gamma1 = gamma1 + step * jnp.sum(t0 * (step * t0b - 2.0 * (t0 - alpha0 * cw)), axis=1, keepdims=True)
    delta = delta + jnp.sum(step * t0 * (step * t0d - 2.0 * (z_h - alpha0 * w_h)) + rho * cz * cz, axis=1, keepdims=True)
    beta = gamma1 / gamma0
    alpha1 = gamma1 / (delta - beta * (gamma1 / alpha0))
    both = alpha0 * alpha1
    lead = alpha0 + alpha1 * (1.0 + beta)
    on_d = -(both * rho) * t0
    on_c = rho * (both * tw - lead * t0)
    chunk = 8 * LANES

    def body(i, carry):
        at = pl.ds(pl.multiple_of(i * chunk, chunk), chunk)
        x_ref[:, at] = lead * zn_ref[0:nf, at] - both * wn_ref[:, at] + weighted_rows(on_d, zn_ref.at[nf:], at)
        res_ref[:, at] = (
            r0_ref[:, at] - lead * qn_ref[:, at] + both * sn_ref[0:nf, at]
            + (weighted_rows(on_c, cd_ref, at) - weighted_rows(on_d, sn_ref.at[nf:], at))
        )
        return carry

    lax.fori_loop(0, x_ref.shape[1] // chunk, body, 0)


SMEM = pl.BlockSpec(memory_space=pltpu.SMEM)
VMEM = pl.BlockSpec(memory_space=pltpu.VMEM)
ANY = pl.BlockSpec(memory_space=pltpu.HBM)
PARAMS = pltpu.CompilerParams(vmem_limit_bytes=20 * 1024 * 1024)


def like(*shape, dtype=F32):
    return pltpu.VMEM(shape, dtype)


def in_hbm(x):
    return pltpu.with_memory_space_constraint(x, pltpu.HBM)


def call(kernel, ins, outs, scratch, name, flops=0):
    return pl.pallas_call(
        kernel, in_specs=ins, out_shape=outs, out_specs=jax.tree.map(lambda _: VMEM, outs), scratch_shapes=scratch,
        compiler_params=PARAMS, name=name,
        cost_estimate=pl.CostEstimate(flops=flops, transcendentals=0, bytes_accessed=8 << 20) if flops else None)


def along_slabs(one, two):
    slabs, sectors = lax.axis_size("slab"), lax.axis_size("sector")

    def steps(way):
        pairs = []
        for s in range(slabs):
            for e in range(sectors):
                to = s + 1 if (e + way) % 2 == 0 else s - 1
                target = (to, e) if 0 <= to < slabs else (s, e ^ 1)
                pairs.append((s * sectors + e, target[0] * sectors + target[1]))
        return pairs

    return lax.ppermute(one, AXES, steps(0)), lax.ppermute(two, AXES, steps(1))


def along_sectors(one, two):
    count = lax.axis_size("sector")
    up = [(i, (i + 1) % count) for i in range(count)]
    down = [((i + 1) % count, i) for i in range(count)]
    return lax.ppermute(one, "sector", up), lax.ppermute(two, "sector", down)


def exchange(msgs):
    return along_slabs(msgs[0], msgs[1]) + along_sectors(msgs[2], msgs[3])


def rows_of(x, group):
    n = x.shape[0]
    return x.reshape(n // group, group, 32, LANES).transpose(0, 2, 1, 3).reshape(n * 32, LANES)


def on_device(source, periods, tiles, columns, coupling, send_list, recv_rows, counts, cycle_edges, cycle_signs, inverse_blocks):
    src = source[0, 0]
    nf, width = src.shape
    blocks = width // TILE
    kt = tiles.shape[3]
    cap = coupling.shape[3]
    cycles = periods.shape[0]
    both = nf + cycles
    devices = lax.axis_size("slab") * lax.axis_size("sector")
    rho = 1.0 / (cycle_edges.shape[3] * devices)
    tiles2 = in_hbm(rows_of(tiles[0, 0].reshape(blocks * kt, TILE * TILE), kt))
    coup2 = in_hbm(rows_of(coupling[0, 0].reshape(4 * cap, TILE * TILE), 8))
    inv2 = in_hbm(rows_of(inverse_blocks[0, 0], 8))
    send, recv, cols = in_hbm(send_list[0, 0]), in_hbm(recv_rows[0, 0]), in_hbm(columns[0, 0].T)
    counts, periods, src = in_hbm(counts), in_hbm(periods), in_hbm(src)
    edges, signs = in_hbm(cycle_edges[0, 0]), in_hbm(cycle_signs[0, 0])
    msg = like(cap, nf, LANES)
    *msgs, z, zn, r0, cd, y, winv, wcoup = call(
        functools.partial(first_kernel, both, blocks, cap),
        [VMEM] * 4 + [ANY] * 2 + [SMEM] * 3,
        [msg] * 2 + [like(cap, both, LANES)] * 2 + [msg] * 2 + [like(blocks, both, LANES), like(both, width), like(nf, width), like(cycles, width),
                     like(blocks, 2 * nf, LANES, dtype=BF16), like(blocks, LANES, LANES, dtype=BF16),
                     like(4 * cap, LANES, LANES, dtype=BF16)],
        [pltpu.VMEM((blocks, both, LANES), F32), pltpu.VMEM((blocks, 2 * both, LANES), BF16),
         pltpu.VMEM((blocks, 2 * both, LANES), BF16), pltpu.VMEM(inv2.shape, F32), pltpu.VMEM(coup2.shape, F32),
         pltpu.SemaphoreType.DMA((5,))],
        "first",
    )(src, periods, edges, signs, inv2, coup2, send, recv, counts)

    def local(vector, y, n, forms):
        fresh = forms is None
        out = [like(blocks, n, LANES)]
        scratch = [pltpu.VMEM((blocks, 2 * n, LANES), BF16), pltpu.VMEM((blocks, 2 * n, LANES), BF16),
                   pltpu.VMEM((blocks, n, kt // 2 * LANES), F32)]
        if fresh:
            out.append(like(blocks, LANES, kt // 2 * LANES, dtype=BF16))
            scratch += [pltpu.VMEM(tiles2.shape, F32), pltpu.SemaphoreType.DMA((blocks // LOCAL_STEP,))]
        return call(
            functools.partial(local_kernel, n, blocks, kt, fresh),
            [SMEM, ANY if fresh else VMEM, VMEM, VMEM], out, scratch, "local", flops=2 * 10**9,
        )(cols, tiles2 if fresh else forms, vector, y)

    incoming = exchange(msgs[:4])
    acc, forms = local(z, y, nf, None)
    acc, incoming, last = lax.optimization_barrier((acc, incoming, msgs[4:]))
    later = along_slabs(*last) + incoming[2:]
    *msgs, qn, wd, wn, y = call(
        functools.partial(second_kernel, nf, blocks, cap),
        [VMEM] * 8 + [SMEM] * 3,
        [msg] * 4 + [like(nf, width), like(blocks, both, LANES), like(nf, width), like(blocks, 2 * both, LANES, dtype=BF16)],
        [pltpu.VMEM((blocks, nf, LANES), F32), pltpu.VMEM((blocks, 2 * nf, LANES), BF16),
         pltpu.VMEM((blocks, nf, LANES), F32), pltpu.VMEM((blocks, 2 * nf, LANES), BF16)],
        "second",
    )(acc, *incoming, z, winv, wcoup, send, recv, counts)
    msgs, later = lax.optimization_barrier((msgs, later))
    incoming = exchange(msgs)
    (acc,) = local(wd, y, both, forms)
    sn, pay = call(
        functools.partial(third_kernel, nf, blocks, cap),
        [VMEM] * 10 + [SMEM] * 3 + [VMEM] * 5,
        [like(both, width), like(devices, nf // 2, LANES)],
        [pltpu.VMEM((blocks, both, LANES), F32), pltpu.VMEM((nf + both, LANES), F32)],
        "third",
    )(acc, *incoming, *later, wcoup, send, recv, counts, zn, qn, wn, r0, cd)
    everyone = lax.all_to_all(pay, AXES, 0, 0)
    out, res = call(
        functools.partial(last_kernel, nf, rho),
        [VMEM] * 7,
        [jax.ShapeDtypeStruct((nf, width), F32)] * 2,
        [],
        "last",
    )(everyone, zn, wn, qn, r0, cd, sn)
    return out[None, None], res[None, None]


def solution(mesh):
    two = P("slab", "sector")
    return jax.shard_map(
        on_device,
        mesh=mesh,
        in_specs=(two, P(), two, two, two, two, two, two, two, two, two),
        out_specs=(two, two),
        check_vma=False,
    )
```

```python
import functools

import jax
import jax.numpy as jnp
from jax import lax
from jax.experimental import pallas as pl
from jax.experimental.pallas import tpu as pltpu
from jax.sharding import PartitionSpec as P

TILE = 64
LANES = 128
F32 = jnp.float32
BF16 = jnp.bfloat16
AXES = ("slab", "sector")
ROWS_STEP = 64
SMOOTH_STEP = 64
SEND_STEP = 32
ABSORB_STEP = 32
LOCAL_STEP = 16


def lane_of(shape):
    return lax.broadcasted_iota(jnp.int32, shape, len(shape) - 1)


def split(x):
    hi = x.astype(BF16)
    lo = x - hi.astype(F32)
    return hi.astype(F32), lo


def turn(x):
    return pltpu.roll(x, 64, x.ndim - 1)


def into_rows():
    row = lax.broadcasted_iota(jnp.int32, (LANES, LANES), 0)
    col = lane_of((LANES, LANES))
    return jnp.where(row == 2 * (col % 32) + (col // 32) % 2, 1.0, 0.0).astype(BF16)


def out_of_rows():
    row = lax.broadcasted_iota(jnp.int32, (LANES, LANES), 0)
    col = lane_of((LANES, LANES))
    return jnp.where(col % 64 == 2 * (row % 32) + (row // 32) % 2, 1.0, 0.0).astype(BF16)


def stacked(x):
    hi, lo = split(x)
    return jnp.concatenate([hi, lo], axis=0).astype(BF16)


def single(ref, start, stride):
    v = ref[pl.ds(start, 32, stride=stride), :]
    t = turn(v)
    low = lane_of(v.shape) < 64
    return stacked(jnp.concatenate([jnp.where(low, v, t), jnp.where(low, t, v)], axis=0))


def pair(ref, start, stride):
    a = ref[pl.ds(start, 32, stride=stride), :]
    b = ref[pl.ds(start + 1, 32, stride=stride), :]
    low = lane_of(a.shape) < 64
    return stacked(jnp.concatenate([jnp.where(low, a, turn(b)), jnp.where(low, turn(a), b)], axis=0))


def dot(a, b):
    return lax.dot_general(a, b, (((1,), (0,)), ((), ())), preferred_element_type=F32)


def dot_nt(a, b):
    return lax.dot_general(a, b, (((1,), (1,)), ((), ())), preferred_element_type=F32)


def rows_and_lanes(parts):
    return jnp.concatenate([jnp.concatenate(row, axis=1) for row in parts], axis=0)


def turned_products(ys, ws, nf):
    none = jnp.zeros_like(ys[0])
    left = rows_and_lanes([[ys[0], none], [ys[1], none], [none, ys[2]], [none, ys[3]]])
    out = dot(left, rows_and_lanes([ws[:2], ws[2:]]))
    n = 2 * nf
    return [halves(out[i * n : (i + 1) * n, i % 2 * LANES : (i % 2 + 1) * LANES], nf) for i in range(4)]


def straight_products(xs, ws, nf):
    none = jnp.zeros_like(xs[0])
    left = rows_and_lanes([[xs[0], none], [none, xs[1]], [xs[2], none], [none, xs[3]]]).astype(BF16)
    out = dot_nt(left, rows_and_lanes([ws[:2], ws[2:]]))
    return [out[i * nf : (i + 1) * nf, i // 2 * LANES : (i // 2 + 1) * LANES] for i in range(4)]


def halves(out, nf):
    return out[:nf] + out[nf:]


def write_row_form(load, y_ref, nf, blocks, matrix):
    def body(i, carry):
        x = jnp.concatenate([stacked(load(i * ROWS_STEP + j)) for j in range(ROWS_STEP)], axis=0)
        out = dot(x, matrix).astype(BF16)
        for j in range(ROWS_STEP):
            y_ref[i * ROWS_STEP + j] = out[j * 2 * nf : (j + 1) * 2 * nf]
        return carry

    lax.fori_loop(0, blocks // ROWS_STEP, body, 0)


def to_natural(ref, nat_ref, blocks):
    rows = nat_ref.shape[0]
    low = lane_of((rows, LANES)) < 64
    for t in range(blocks // 2):
        a = ref[2 * t]
        b = ref[2 * t + 1]
        nat_ref[:, t * LANES : (t + 1) * LANES] = jnp.where(low, a[:rows], b[:rows])


def made(ref, keep_ref):
    def tile(first, j):
        w = single(ref, first * 32 + (j // 8) * 256 + j % 8, 8)
        keep_ref[first + j] = w
        return w

    return tile


def kept(keep_ref):
    return lambda first, j: keep_ref[first + j]


def smooth_into(tile, y_ref, out_ref, nf, blocks):
    def body(g, carry):
        for c in range(0, SMOOTH_STEP, 4):
            ws = [tile(g * SMOOTH_STEP, c + i) for i in range(4)]
            at = g * SMOOTH_STEP + c
            for i, value in enumerate(turned_products([y_ref[at + i] for i in range(4)], ws, nf)):
                out_ref[at + i, 0:nf] = value
        return carry

    lax.fori_loop(0, blocks // SMOOTH_STEP, body, 0)


def write_messages(load, y_ref, ready, tile, send_ref, recv_ref, counts_ref, msgs, nf, cap):
    low = lane_of((nf, LANES)) < 64
    for way in range(4):
        ready(way)
        d = sends(way)

        def body(g, carry, d=d, way=way):
            for j in range(0, SEND_STEP, 4):
                c = g * SEND_STEP + j
                ws = [tile(d * cap + g * SEND_STEP, j + i) for i in range(4)]
                ys = [y_ref[recv_ref[d, c + i]] for i in range(4)]
                for i, partner in enumerate(turned_products(ys, ws, nf)):
                    weight = jnp.where(c + i < counts_ref[0, 0, d], 1.0, 0.0)
                    value = jnp.where(low, load(send_ref[d, c + i]) * weight, partner)
                    at = 0
                    for msg in msgs[way]:
                        msg[c + i] = value[at : at + msg.shape[1]]
                        at += msg.shape[1]
            return carry

        lax.fori_loop(0, cap // SEND_STEP, body, 0)


class Copies:
    def __init__(self, sems, pairs):
        self.copies = [pltpu.make_async_copy(a, b, sems.at[i]) for i, (a, b) in enumerate(pairs)]
        for copy in self.copies:
            copy.start()

    def wait(self, i):
        self.copies[i].wait()


def lists(hbm, smem, sems):
    return Copies(sems, list(zip(hbm, smem)))


def quarters(hbm, vmem):
    rows = vmem.shape[0] // 4
    return [(hbm.at[pl.ds(d * rows, rows)], vmem.at[pl.ds(d * rows, rows)]) for d in range(4)]


def weighted_rows(coef, rows, at):
    out = None
    for g in range(coef.shape[1]):
        term = coef[:, g : g + 1] * rows[g : g + 1, at]
        out = term if out is None else out + term
    return out


def first_kernel(nf, blocks, cap, src_hbm, per_hbm, edges_hbm, signs_hbm, inv_hbm, coup_hbm, send_hbm, recv_hbm,
                 counts_hbm, m0, m1, m2, m3, d0, d1, z_ref, r0_ref, cd_ref, winv_ref, wcoup_ref,
                 x_ref, y0_ref, y_ref, inv_ref, coup_ref, src_ref, per_ref, edges_ref, signs_ref, send_ref, recv_ref,
                 counts_ref, sems):
    small = [(edges_hbm, edges_ref), (signs_hbm, signs_ref), (per_hbm, per_ref), (src_hbm, src_ref), (send_hbm, send_ref),
             (recv_hbm, recv_ref), (counts_hbm, counts_ref)]
    large = [(inv_hbm, inv_ref)] + quarters(coup_hbm, coup_ref)
    copies = Copies(sems, small + large)
    for i in range(len(small)):
        copies.wait(i)
    fields = src_ref.shape[0]
    width = src_ref.shape[1]
    count = edges_ref.shape[0]
    edges = edges_ref[...]
    orient = (2 * signs_ref[...] - 1).astype(F32)
    low = lane_of((fields, LANES)) < 64
    step = 16 * LANES
    place = lane_of((count, step))
    totals = per_ref[...].T

    def cycles(t, carry):
        at = pl.ds(pl.multiple_of(t * step, step), step)
        here = place + t * step
        total = jnp.zeros((count, step), F32)
        for l in range(edges.shape[1]):
            total = jnp.where(edges[:, l : l + 1] == here, orient[:, l : l + 1], total)
        cd_ref[:, at] = total
        r0_ref[:, at] = src_ref[:, at] + weighted_rows(totals, cd_ref, at)
        return carry

    lax.fori_loop(0, width // step, cycles, 0)
    for t in range(width // LANES):
        r = r0_ref[:, t * LANES : (t + 1) * LANES]
        c = cd_ref[:, t * LANES : (t + 1) * LANES]
        rt = turn(r)
        ct = turn(c)
        x_ref[2 * t] = jnp.concatenate([jnp.where(low, r, rt), jnp.where(low, c, ct)], axis=0)
        x_ref[2 * t + 1] = jnp.concatenate([jnp.where(low, rt, r), jnp.where(low, ct, c)], axis=0)
    matrix = into_rows()
    write_row_form(lambda b: x_ref[b], y0_ref, nf, blocks, matrix)
    copies.wait(len(small))
    smooth_into(made(inv_ref, winv_ref), y0_ref, z_ref, nf, blocks)
    write_row_form(lambda b: z_ref[b], y_ref, nf, blocks, matrix)


    def ready(way):
        for part in ((0, 1), (), (3,), (2,))[way]:
            copies.wait(len(small) + 1 + part)

    write_messages(lambda b: z_ref[b], y_ref, ready, made(coup_ref, wcoup_ref),
                   send_ref, recv_ref, counts_ref, ((m0, d0), (m1, d1), (m2,), (m3,)), nf, cap)


def local_kernel(nf, blocks, kt, fresh, plain, cols_hbm, tiles_in, *rest):
    vectors, rest = rest[:plain], rest[plain:]
    z_ref = vectors[0]
    acc_ref, rest = rest[0], rest[1:]
    w_ref, rest = (rest[0], rest[1:]) if fresh else (tiles_in, rest)
    naturals, (x_ref, y_ref, u_ref, t_ref, cols_ref, col_sem) = rest[:plain], rest[plain : plain + 6]
    listed = lists([cols_hbm], [cols_ref], col_sem)
    if fresh:
        tiles_ref, sems = rest[plain + 6 :]
        rows = LOCAL_STEP * kt * 32

        def copy(i):
            at = pl.ds(pl.multiple_of(i * rows, rows), rows)
            return pltpu.make_async_copy(tiles_in.at[at], tiles_ref.at[at], sems.at[i])

        for i in range(blocks // LOCAL_STEP):
            copy(i).start()
    write_row_form(lambda b: z_ref[b, 0:nf], y_ref, nf, blocks, into_rows())

    def left(b, carry):
        x_ref[b] = stacked(z_ref[b, 0:nf])
        return carry

    lax.fori_loop(0, blocks, left, 0, unroll=8)
    listed.wait(0)
    wide = lane_of((2 * nf, LANES)) < 64

    def body(i, carry):
        if fresh:
            copy(i).wait()
        for s in range(0, LOCAL_STEP, 2):
            xs, ws = [], []
            b = i * LOCAL_STEP + s
            for at in (b, b + 1):
                if fresh:
                    w = jnp.concatenate([pair(tiles_ref, at * (32 * kt) + k, kt) for k in range(0, kt, 2)], axis=1)
                    w_ref[at] = w
                    ws.append(w)
                else:
                    ws.append(w_ref[at])
                x = [x_ref[lax.rem(at + cols_ref[k, 0], blocks)] for k in range(kt)]
                xs.append(jnp.concatenate([jnp.where(wide, x[k], x[k + 1]) for k in range(0, kt, 2)], axis=1))
            w = jnp.concatenate(ws, axis=0)
            none = jnp.zeros_like(y_ref[b])
            out = dot(rows_and_lanes([[y_ref[b], none], [none, y_ref[b + 1]]]), w)
            t_ref[b] = halves(out[: 2 * nf], nf)
            t_ref[b + 1] = halves(out[2 * nf :], nf)
            out = dot_nt(jnp.concatenate(xs, axis=0), w)
            u_ref[b] = stacked(halves(out[: 2 * nf, :LANES], nf))
            u_ref[b + 1] = stacked(halves(out[2 * nf :, LANES:], nf))
        return carry

    lax.fori_loop(0, blocks // LOCAL_STEP, body, 0)
    matrix = out_of_rows()
    low = lane_of((nf, LANES)) < 64

    def finish(i, carry):
        out = dot(u_ref[pl.ds(i * 32, 32)].reshape(32 * 2 * nf, LANES), matrix)
        for j in range(32):
            b = i * 32 + j
            t = None
            for k in range(0, kt, 2):
                at = slice(k // 2 * LANES, (k // 2 + 1) * LANES)
                v = jnp.where(low, t_ref[lax.rem(b + blocks - cols_ref[k, 0], blocks), :, at],
                              t_ref[lax.rem(b + blocks - cols_ref[k + 1, 0], blocks), :, at])
                t = v if t is None else t + v
            acc_ref[b] = z_ref[b, 0:nf] + halves(out[j * 2 * nf : (j + 1) * 2 * nf], nf) + t + turn(t)
        return carry

    lax.fori_loop(0, blocks // 32, finish, 0)
    for vector, natural in zip(vectors, naturals):
        to_natural(vector, natural, blocks)


def odd_sector():
    return lax.rem(lax.axis_index("sector"), 2)


def sends(way):
    return 1 - odd_sector() if way == 0 else odd_sector() if way == 1 else 5 - way


def receives(way):
    return odd_sector() if way == 0 else 1 - odd_sector() if way == 1 else way


def present(way, d):
    if way > 1:
        return None
    end = d * (lax.axis_size("slab") - 1)
    return jnp.where(lax.axis_index("slab") == end, 0.0, 1.0)


def absorb(acc_ref, incs, tile, send_ref, recv_ref, counts_ref, nf, cap):
    matrix = out_of_rows()
    low = lane_of((nf, LANES)) < 64
    for way in range(4):
        d = receives(way)
        there = present(way, d)

        def body(g, carry, d=d, way=way, there=there):
            rows = []
            back = []
            for j in range(0, ABSORB_STEP, 4):
                xs = []
                for i in range(4):
                    c = g * ABSORB_STEP + j + i
                    arr = jnp.concatenate([inc[c, at : at + nf // len(incs[way])] for inc, at in incs[way]], axis=0)
                    if there is not None:
                        arr = arr * there
                    hi, lo = split(arr)
                    xs.append(jnp.where(low, hi, turn(lo)))
                    weight = jnp.where(c < counts_ref[0, 0, d], 1.0, 0.0)
                    back.append(jnp.where(low, turn(arr), arr) * weight)
                ws = [tile(d * cap + g * ABSORB_STEP, j + i) for i in range(4)]
                rows += [stacked(u) for u in straight_products(xs, ws, nf)]
            out = dot(jnp.concatenate(rows, axis=0), matrix)
            spots = [recv_ref[d, g * ABSORB_STEP + j] for j in range(ABSORB_STEP)]
            old = [acc_ref[s] for s in spots]
            for j in range(ABSORB_STEP):
                acc_ref[spots[j]] = old[j] + halves(out[j * 2 * nf : (j + 1) * 2 * nf], nf)
            spots = [send_ref[d, g * ABSORB_STEP + j] for j in range(ABSORB_STEP)]
            old = [acc_ref[s] for s in spots]
            for j in range(ABSORB_STEP):
                acc_ref[spots[j]] = old[j] + back[j]
            return carry

        lax.fori_loop(0, cap // ABSORB_STEP, body, 0)


def second_kernel(nf, blocks, cap, acc_in, i0, i1, i2, i3, z_ref, winv_ref, wcoup_ref, send_hbm, recv_hbm, counts_hbm,
                  m0, m1, m2, m3, acc_ref, wd_ref, y0_ref, y_ref, send_ref, recv_ref, counts_ref, sems):
    listed = lists([send_hbm, recv_hbm, counts_hbm], [send_ref, recv_ref, counts_ref], sems)
    acc_ref[...] = acc_in[...]
    wd_ref[:, nf:] = z_ref[:, nf:]
    for i in range(3):
        listed.wait(i)
    coup = kept(wcoup_ref)
    absorb(acc_ref, [[(inc, 0)] for inc in (i0, i1, i2, i3)], coup, send_ref, recv_ref, counts_ref, nf, cap)
    matrix = into_rows()
    write_row_form(lambda b: acc_ref[b], y0_ref, nf, blocks, matrix)
    smooth_into(kept(winv_ref), y0_ref, wd_ref, nf, blocks)
    write_row_form(lambda b: wd_ref[b, 0:nf], y_ref, nf, blocks, matrix)
    write_messages(lambda b: wd_ref[b, 0:nf], y_ref, lambda way: None, coup, send_ref, recv_ref, counts_ref,
                   ((m0,), (m1,), (m2,), (m3,)), nf, cap)


def column_of(values, lane, at):
    return jnp.sum(jnp.where(lane == at, values, 0.0), axis=1, keepdims=True)


def packed(x):
    return jnp.where(lane_of((4, LANES)) < 64, x[0:4], turn(x[4:8]))


def third_kernel(nf, blocks, cap, acc_in, i0, i1, i2, i3, d0, d1, e2, e3, wcoup_ref, send_ref, recv_ref, counts_ref,
                 zn_ref, qn_ref, wn_ref, r0_ref, cd_ref, sn_ref, pay_ref, acc_ref, g_ref):
    acc_ref[...] = acc_in[...]
    incs = [[(i0, 0), (d0, 0)], [(i1, 0), (d1, 0)], [(i2, 0), (e2, nf)], [(i3, 0), (e3, nf)]]
    absorb(acc_ref, incs, kept(wcoup_ref), send_ref, recv_ref, counts_ref,
           acc_ref.shape[1], cap)
    to_natural(acc_ref, sn_ref, blocks)
    z = zn_ref[0:nf, :]
    q = qn_ref[...]
    w = wn_ref[...]
    r = r0_ref[...]
    s = sn_ref[0:nf, :]

    def inner(a, b):
        return jnp.sum(a * b, axis=1, keepdims=True)

    gamma = inner(r, z)
    base = inner(z, q)
    safe = jnp.where(base > 0.0, base, 1.0)
    centre = jnp.where(base > 0.0, jnp.clip(gamma / safe, 0.0, 4.0), 0.0)
    zc = z - centre * w
    kz = q - centre * s
    values = {
        16: gamma,
        17: base,
        18: inner(r - centre * q, zc),
        19: inner(q, zc),
        20: inner(q, w),
        21: inner(zc, kz),
        22: inner(zc, s),
        23: inner(w, s),
    }
    left_hi, left_lo = split(jnp.concatenate([z, w, zn_ref[nf:, :]], axis=0))
    right_hi, right_lo = split(jnp.concatenate([cd_ref[...], sn_ref[nf:, :]], axis=0))
    left = jnp.concatenate([left_hi, left_lo], axis=0).astype(BF16)
    products = dot_nt(left, right_hi.astype(BF16)) + dot_nt(left, right_lo.astype(BF16))
    g_ref[...] = jnp.zeros_like(g_ref)
    g_ref[:, 0:16] = products[:24] + products[24:]
    lane = lane_of((nf, LANES))
    pay = g_ref[0:8, :] + pltpu.roll(g_ref[8:16, :], 32, 1) + pltpu.roll(g_ref[16:24, :], 48, 1)
    for at, value in values.items():
        pay = jnp.where(lane == at, value, pay)
    pay = jnp.where((lane >= 24) & (lane < 30), centre, pay)
    pay_ref[...] = jnp.broadcast_to(packed(pay)[None], pay_ref.shape)


def last_kernel(nf, rho, all_ref, zn_ref, wn_ref, qn_ref, r0_ref, cd_ref, sn_ref, x_ref, res_ref):
    lane = lane_of((nf, LANES))
    total = lax.fori_loop(0, all_ref.shape[0], lambda d, t: t + all_ref[d], jnp.zeros((nf // 2, LANES), F32), unroll=16)
    total = jnp.concatenate([total, turn(total)], axis=0)

    def mat(a, b):
        out = None
        for g in range(a.shape[1]):
            term = a[:, g : g + 1] * b[g : g + 1, :]
            out = term if out is None else out + term
        return out

    t0 = total[:, 0:8]
    z_h = total[:, 8:16]
    cw = total[:, 32:40]
    w_h = total[:, 40:48]
    b = total[:, 48:56]
    d_h = total[:, 56:64]
    gamma0 = column_of(total, lane, 16)
    base = column_of(total, lane, 17) + rho * jnp.sum(t0 * t0, axis=1, keepdims=True)
    alpha0 = gamma0 / base
    wide = packed(jnp.broadcast_to(alpha0, (nf, LANES)))
    spot = lane_of((nf // 2, LANES)) % 64
    constant = (spot == 18) | (spot == 21)
    linear = (spot == 19) | (spot == 22)

    def about(d, carry):
        part = all_ref[d]
        off = wide - pltpu.roll(part, LANES - 6, 1)
        return carry + part * jnp.where(constant, 1.0, jnp.where(linear, -2.0 * off, off * off))

    sums = lax.fori_loop(0, all_ref.shape[0], about, jnp.zeros((nf // 2, LANES), F32), unroll=16)
    sums = jnp.concatenate([sums, turn(sums)], axis=0)
    gamma1 = jnp.sum(jnp.where((lane >= 18) & (lane < 21), sums, 0.0), axis=1, keepdims=True)
    delta = jnp.sum(jnp.where((lane >= 21) & (lane < 24), sums, 0.0), axis=1, keepdims=True)
    t0b = mat(t0, b)
    t0d = mat(t0, d_h)
    tw = cw + rho * t0b
    cz = t0 - alpha0 * tw
    step = alpha0 * rho
    gamma1 = gamma1 + step * jnp.sum(t0 * (step * t0b - 2.0 * (t0 - alpha0 * cw)), axis=1, keepdims=True)
    delta = delta + jnp.sum(step * t0 * (step * t0d - 2.0 * (z_h - alpha0 * w_h)) + rho * cz * cz, axis=1, keepdims=True)
    beta = gamma1 / gamma0
    alpha1 = gamma1 / (delta - beta * (gamma1 / alpha0))
    both = alpha0 * alpha1
    lead = alpha0 + alpha1 * (1.0 + beta)
    on_d = -(both * rho) * t0
    on_c = rho * (both * tw - lead * t0)
    chunk = 32 * LANES

    def body(i, carry):
        at = pl.ds(pl.multiple_of(i * chunk, chunk), chunk)
        x_ref[:, at] = lead * zn_ref[0:nf, at] - both * wn_ref[:, at] + weighted_rows(on_d, zn_ref.at[nf:], at)
        res_ref[:, at] = (
            r0_ref[:, at] - lead * qn_ref[:, at] + both * sn_ref[0:nf, at]
            + (weighted_rows(on_c, cd_ref, at) - weighted_rows(on_d, sn_ref.at[nf:], at))
        )
        return carry

    lax.fori_loop(0, x_ref.shape[1] // chunk, body, 0)


SMEM = pl.BlockSpec(memory_space=pltpu.SMEM)
VMEM = pl.BlockSpec(memory_space=pltpu.VMEM)
ANY = pl.BlockSpec(memory_space=pltpu.HBM)
PARAMS = pltpu.CompilerParams(vmem_limit_bytes=20 * 1024 * 1024)


def like(*shape, dtype=F32):
    return pltpu.VMEM(shape, dtype)


def in_hbm(x):
    return pltpu.with_memory_space_constraint(x, pltpu.HBM)


def call(kernel, ins, outs, scratch, name, flops=0):
    return pl.pallas_call(
        kernel, in_specs=ins, out_shape=outs, out_specs=jax.tree.map(lambda _: VMEM, outs), scratch_shapes=scratch,
        compiler_params=PARAMS, name=name,
        cost_estimate=pl.CostEstimate(flops=flops, transcendentals=0, bytes_accessed=8 << 20) if flops else None)


def along_slabs(one, two):
    slabs, sectors = lax.axis_size("slab"), lax.axis_size("sector")

    def steps(way):
        pairs = []
        for s in range(slabs):
            for e in range(sectors):
                to = s + 1 if (e + way) % 2 == 0 else s - 1
                target = (to, e) if 0 <= to < slabs else (s, e ^ 1)
                pairs.append((s * sectors + e, target[0] * sectors + target[1]))
        return pairs

    return lax.ppermute(one, AXES, steps(0)), lax.ppermute(two, AXES, steps(1))


def along_sectors(one, two):
    count = lax.axis_size("sector")
    up = [(i, (i + 1) % count) for i in range(count)]
    down = [((i + 1) % count, i) for i in range(count)]
    return lax.ppermute(one, "sector", up), lax.ppermute(two, "sector", down)


def exchange(msgs):
    return along_slabs(msgs[0], msgs[1]) + along_sectors(msgs[2], msgs[3])


def rows_of(x, group):
    n = x.shape[0]
    return x.reshape(n // group, group, 32, LANES).transpose(0, 2, 1, 3).reshape(n * 32, LANES)


def on_device(source, periods, tiles, columns, coupling, send_list, recv_rows, counts, cycle_edges, cycle_signs, inverse_blocks):
    src = source[0, 0]
    nf, width = src.shape
    blocks = width // TILE
    kt = tiles.shape[3]
    cap = coupling.shape[3]
    cycles = periods.shape[0]
    both = nf + cycles
    devices = lax.axis_size("slab") * lax.axis_size("sector")
    rho = 1.0 / (cycle_edges.shape[3] * devices)
    tiles2 = in_hbm(rows_of(tiles[0, 0].reshape(blocks * kt, TILE * TILE), kt))
    coup2 = in_hbm(rows_of(coupling[0, 0].reshape(4 * cap, TILE * TILE), 8))
    inv2 = in_hbm(rows_of(inverse_blocks[0, 0], 8))
    send, recv, cols = in_hbm(send_list[0, 0]), in_hbm(recv_rows[0, 0]), in_hbm(columns[0, 0].T)
    counts, periods, src = in_hbm(counts), in_hbm(periods), in_hbm(src)
    edges, signs = in_hbm(cycle_edges[0, 0]), in_hbm(cycle_signs[0, 0])
    msg = like(cap, nf, LANES)
    rows = pltpu.VMEM((blocks, 2 * nf, LANES), BF16)
    tables = [pltpu.SMEM(send.shape, jnp.int32), pltpu.SMEM(recv.shape, jnp.int32), pltpu.SMEM(counts.shape, jnp.int32),
              pltpu.SemaphoreType.DMA((3,))]
    rows_both = pltpu.VMEM((blocks, 2 * both, LANES), BF16)
    *msgs, z, r0, cd, winv, wcoup = call(
        functools.partial(first_kernel, both, blocks, cap),
        [ANY] * 9,
        [msg] * 2 + [like(cap, both, LANES)] * 2 + [msg] * 2 + [
            like(blocks, both, LANES), like(nf, width), like(cycles, width), like(blocks, LANES, LANES, dtype=BF16),
            like(4 * cap, LANES, LANES, dtype=BF16)],
        [pltpu.VMEM((blocks, both, LANES), F32), rows_both, rows_both, pltpu.VMEM(inv2.shape, F32),
         pltpu.VMEM(coup2.shape, F32), pltpu.VMEM(src.shape, F32), pltpu.VMEM(periods.shape, F32),
         pltpu.VMEM(edges.shape, jnp.int32), pltpu.VMEM(signs.shape, jnp.int32), pltpu.SMEM(send.shape, jnp.int32),
         pltpu.SMEM(recv.shape, jnp.int32), pltpu.SMEM(counts.shape, jnp.int32), pltpu.SemaphoreType.DMA((12,))],
        "first",
    )(src, periods, edges, signs, inv2, coup2, send, recv, counts)

    def local(n, fresh, tiles, *vectors):
        out = [like(blocks, n, LANES)]
        if fresh:
            out.append(like(blocks, LANES, kt // 2 * LANES, dtype=BF16))
        out += [like(both, width)] if fresh else [like(nf, width)] * 2
        form = pltpu.VMEM((blocks, 2 * n, LANES), BF16)
        scratch = [form, form, form, pltpu.VMEM((blocks, n, kt // 2 * LANES), F32), pltpu.SMEM(cols.shape, jnp.int32),
                   pltpu.SemaphoreType.DMA((1,))]
        if fresh:
            scratch += [pltpu.VMEM(tiles.shape, F32), pltpu.SemaphoreType.DMA((blocks // LOCAL_STEP,))]
        return call(
            functools.partial(local_kernel, n, blocks, kt, fresh, len(vectors)),
            [ANY, ANY if fresh else VMEM] + [VMEM] * len(vectors), out, scratch, "local", flops=2 * 10**9,
        )(cols, tiles, *vectors)

    incoming = exchange(msgs[:4])
    acc, forms, zn = local(nf, True, tiles2, z)
    acc, incoming, last = lax.optimization_barrier((acc, incoming, msgs[4:]))
    later = along_slabs(*last) + incoming[2:]
    *msgs, q, wd = call(
        functools.partial(second_kernel, nf, blocks, cap),
        [VMEM] * 8 + [ANY] * 3,
        [msg] * 4 + [like(blocks, nf, LANES), like(blocks, both, LANES)],
        [rows, rows] + tables,
        "second",
    )(acc, *incoming, z, winv, wcoup, send, recv, counts)
    msgs, later = lax.optimization_barrier((msgs, later))
    incoming = exchange(msgs)
    acc, wn, qn = local(both, False, forms, wd, q)
    sn, pay = call(
        functools.partial(third_kernel, nf, blocks, cap),
        [VMEM] * 10 + [SMEM] * 3 + [VMEM] * 5,
        [like(both, width), like(devices, nf // 2, LANES)],
        [pltpu.VMEM((blocks, both, LANES), F32), pltpu.VMEM((nf + both, LANES), F32)],
        "third",
    )(acc, *incoming, *later, wcoup, send, recv, counts, zn, qn, wn, r0, cd)
    everyone = lax.all_to_all(pay, AXES, 0, 0)
    out, res = call(
        functools.partial(last_kernel, nf, rho),
        [VMEM] * 7,
        [jax.ShapeDtypeStruct((nf, width), F32)] * 2,
        [],
        "last",
    )(everyone, zn, wn, qn, r0, cd, sn)
    return out[None, None], res[None, None]


def solution(mesh):
    two = P("slab", "sector")
    return jax.shard_map(
        on_device,
        mesh=mesh,
        in_specs=(two, P(), two, two, two, two, two, two, two, two, two),
        out_specs=(two, two),
        check_vma=False,
    )
```

```python
import functools

import jax
import jax.numpy as jnp
from jax import lax
from jax.experimental import pallas as pl
from jax.experimental.pallas import tpu as pltpu
from jax.sharding import PartitionSpec as P

TILE = 64
LANES = 128
F32 = jnp.float32
BF16 = jnp.bfloat16
AXES = ("slab", "sector")
ROWS_STEP = 64
SMOOTH_STEP = 64
SEND_STEP = 32
ABSORB_STEP = 32
LOCAL_STEP = 16


def lane_of(shape):
    return lax.broadcasted_iota(jnp.int32, shape, len(shape) - 1)


def split(x):
    hi = x.astype(BF16)
    lo = x - hi.astype(F32)
    return hi.astype(F32), lo


def turn(x):
    return pltpu.roll(x, 64, x.ndim - 1)


def into_rows():
    row = lax.broadcasted_iota(jnp.int32, (LANES, LANES), 0)
    col = lane_of((LANES, LANES))
    return jnp.where(row == 2 * (col % 32) + (col // 32) % 2, 1.0, 0.0).astype(BF16)


def out_of_rows():
    row = lax.broadcasted_iota(jnp.int32, (LANES, LANES), 0)
    col = lane_of((LANES, LANES))
    return jnp.where(col % 64 == 2 * (row % 32) + (row // 32) % 2, 1.0, 0.0).astype(BF16)


def stacked(x):
    hi, lo = split(x)
    return jnp.concatenate([hi, lo], axis=0).astype(BF16)


def single(ref, start, stride):
    v = ref[pl.ds(start, 32, stride=stride), :]
    t = turn(v)
    low = lane_of(v.shape) < 64
    return stacked(jnp.concatenate([jnp.where(low, v, t), jnp.where(low, t, v)], axis=0))


def pair(ref, start, stride):
    a = ref[pl.ds(start, 32, stride=stride), :]
    b = ref[pl.ds(start + 1, 32, stride=stride), :]
    low = lane_of(a.shape) < 64
    return stacked(jnp.concatenate([jnp.where(low, a, turn(b)), jnp.where(low, turn(a), b)], axis=0))


def dot(a, b):
    return lax.dot_general(a, b, (((1,), (0,)), ((), ())), preferred_element_type=F32)


def dot_nt(a, b):
    return lax.dot_general(a, b, (((1,), (1,)), ((), ())), preferred_element_type=F32)


def rows_and_lanes(parts):
    return jnp.concatenate([jnp.concatenate(row, axis=1) for row in parts], axis=0)


def turned_products(ys, ws, nf):
    none = jnp.zeros_like(ys[0])
    left = rows_and_lanes([[ys[0], none], [ys[1], none], [none, ys[2]], [none, ys[3]]])
    out = dot(left, rows_and_lanes([ws[:2], ws[2:]]))
    n = 2 * nf
    return [halves(out[i * n : (i + 1) * n, i % 2 * LANES : (i % 2 + 1) * LANES], nf) for i in range(4)]


def straight_products(xs, ws, nf):
    none = jnp.zeros_like(xs[0])
    left = rows_and_lanes([[xs[0], none], [none, xs[1]], [xs[2], none], [none, xs[3]]]).astype(BF16)
    out = dot_nt(left, rows_and_lanes([ws[:2], ws[2:]]))
    return [out[i * nf : (i + 1) * nf, i // 2 * LANES : (i // 2 + 1) * LANES] for i in range(4)]


def halves(out, nf):
    return out[:nf] + out[nf:]


def write_row_form(load, y_ref, nf, blocks, matrix):
    def body(i, carry):
        x = jnp.concatenate([stacked(load(i * ROWS_STEP + j)) for j in range(ROWS_STEP)], axis=0)
        out = dot(x, matrix).astype(BF16)
        for j in range(ROWS_STEP):
            y_ref[i * ROWS_STEP + j] = out[j * 2 * nf : (j + 1) * 2 * nf]
        return carry

    lax.fori_loop(0, blocks // ROWS_STEP, body, 0)


def to_natural(ref, nat_ref, blocks):
    rows = nat_ref.shape[0]
    low = lane_of((rows, LANES)) < 64
    for t in range(blocks // 2):
        a = ref[2 * t]
        b = ref[2 * t + 1]
        nat_ref[:, t * LANES : (t + 1) * LANES] = jnp.where(low, a[:rows], b[:rows])


def made(ref, keep_ref):
    def tile(first, j):
        w = single(ref, first * 32 + (j // 8) * 256 + j % 8, 8)
        keep_ref[first + j] = w
        return w

    return tile


def kept(keep_ref):
    return lambda first, j: keep_ref[first + j]


def smooth_into(tile, y_ref, out_ref, nf, blocks):
    def body(g, carry):
        for c in range(0, SMOOTH_STEP, 4):
            ws = [tile(g * SMOOTH_STEP, c + i) for i in range(4)]
            at = g * SMOOTH_STEP + c
            for i, value in enumerate(turned_products([y_ref[at + i] for i in range(4)], ws, nf)):
                out_ref[at + i, 0:nf] = value
        return carry

    lax.fori_loop(0, blocks // SMOOTH_STEP, body, 0)


def write_messages(load, y_ref, ready, tile, send_ref, recv_ref, counts_ref, msgs, nf, cap):
    low = lane_of((nf, LANES)) < 64
    for way in range(4):
        ready(way)
        d = sends(way)

        def body(g, carry, d=d, way=way):
            for j in range(0, SEND_STEP, 4):
                c = g * SEND_STEP + j
                ws = [tile(d * cap + g * SEND_STEP, j + i) for i in range(4)]
                ys = [y_ref[recv_ref[d, c + i]] for i in range(4)]
                for i, partner in enumerate(turned_products(ys, ws, nf)):
                    weight = jnp.where(c + i < counts_ref[0, 0, d], 1.0, 0.0)
                    value = jnp.where(low, load(send_ref[d, c + i]) * weight, partner)
                    at = 0
                    for msg in msgs[way]:
                        msg[c + i] = value[at : at + msg.shape[1]]
                        at += msg.shape[1]
            return carry

        lax.fori_loop(0, cap // SEND_STEP, body, 0)


class Copies:
    def __init__(self, sems, pairs):
        self.copies = [pltpu.make_async_copy(a, b, sems.at[i]) for i, (a, b) in enumerate(pairs)]
        for copy in self.copies:
            copy.start()

    def wait(self, i):
        self.copies[i].wait()


def lists(hbm, smem, sems):
    return Copies(sems, list(zip(hbm, smem)))


def quarters(hbm, vmem):
    rows = vmem.shape[0] // 4
    return [(hbm.at[pl.ds(d * rows, rows)], vmem.at[pl.ds(d * rows, rows)]) for d in range(4)]


def weighted_rows(coef, rows, at):
    out = None
    for g in range(coef.shape[1]):
        term = coef[:, g : g + 1] * rows[g : g + 1, at]
        out = term if out is None else out + term
    return out


def first_kernel(nf, blocks, cap, src_hbm, per_hbm, edges_hbm, signs_hbm, inv_hbm, coup_hbm, send_hbm, recv_hbm,
                 counts_hbm, m0, m1, m2, m3, d0, d1, z_ref, r0_ref, cd_ref, winv_ref, wcoup_ref,
                 x_ref, y0_ref, y_ref, inv_ref, coup_ref, src_ref, per_ref, edges_ref, signs_ref, send_ref, recv_ref,
                 counts_ref, sems):
    small = [(edges_hbm, edges_ref), (signs_hbm, signs_ref), (per_hbm, per_ref), (src_hbm, src_ref), (send_hbm, send_ref),
             (recv_hbm, recv_ref), (counts_hbm, counts_ref)]
    large = [(inv_hbm, inv_ref)] + quarters(coup_hbm, coup_ref)
    copies = Copies(sems, small + large)
    for i in range(len(small)):
        copies.wait(i)
    fields = src_ref.shape[0]
    width = src_ref.shape[1]
    count = edges_ref.shape[0]
    edges = edges_ref[...]
    orient = (2 * signs_ref[...] - 1).astype(F32)
    low = lane_of((fields, LANES)) < 64
    step = 32 * LANES
    place = lane_of((count, step))
    totals = per_ref[...].T

    def cycles(t, carry):
        at = pl.ds(pl.multiple_of(t * step, step), step)
        here = place + t * step
        total = jnp.zeros((count, step), F32)
        for l in range(edges.shape[1]):
            total = jnp.where(edges[:, l : l + 1] == here, orient[:, l : l + 1], total)
        cd_ref[:, at] = total
        r0_ref[:, at] = src_ref[:, at] + weighted_rows(totals, cd_ref, at)
        return carry

    lax.fori_loop(0, width // step, cycles, 0)
    for t in range(width // LANES):
        r = r0_ref[:, t * LANES : (t + 1) * LANES]
        c = cd_ref[:, t * LANES : (t + 1) * LANES]
        rt = turn(r)
        ct = turn(c)
        x_ref[2 * t] = jnp.concatenate([jnp.where(low, r, rt), jnp.where(low, c, ct)], axis=0)
        x_ref[2 * t + 1] = jnp.concatenate([jnp.where(low, rt, r), jnp.where(low, ct, c)], axis=0)
    matrix = into_rows()
    write_row_form(lambda b: x_ref[b], y0_ref, nf, blocks, matrix)
    copies.wait(len(small))
    smooth_into(made(inv_ref, winv_ref), y0_ref, z_ref, nf, blocks)
    write_row_form(lambda b: z_ref[b], y_ref, nf, blocks, matrix)


    def ready(way):
        for part in ((0, 1), (), (3,), (2,))[way]:
            copies.wait(len(small) + 1 + part)

    write_messages(lambda b: z_ref[b], y_ref, ready, made(coup_ref, wcoup_ref),
                   send_ref, recv_ref, counts_ref, ((m0, d0), (m1, d1), (m2,), (m3,)), nf, cap)


def local_kernel(nf, blocks, kt, fresh, plain, cols_hbm, tiles_in, *rest):
    vectors, rest = rest[:plain], rest[plain:]
    z_ref = vectors[0]
    acc_ref, rest = rest[0], rest[1:]
    w_ref, rest = (rest[0], rest[1:]) if fresh else (tiles_in, rest)
    naturals, (x_ref, y_ref, u_ref, t_ref, cols_ref, col_sem) = rest[:plain], rest[plain : plain + 6]
    listed = lists([cols_hbm], [cols_ref], col_sem)
    if fresh:
        tiles_ref, sems = rest[plain + 6 :]
        rows = LOCAL_STEP * kt * 32

        def copy(i):
            at = pl.ds(pl.multiple_of(i * rows, rows), rows)
            return pltpu.make_async_copy(tiles_in.at[at], tiles_ref.at[at], sems.at[i])

        for i in range(blocks // LOCAL_STEP):
            copy(i).start()
    write_row_form(lambda b: z_ref[b, 0:nf], y_ref, nf, blocks, into_rows())

    def left(b, carry):
        x_ref[b] = stacked(z_ref[b, 0:nf])
        return carry

    lax.fori_loop(0, blocks, left, 0, unroll=8)
    listed.wait(0)
    wide = lane_of((2 * nf, LANES)) < 64

    def body(i, carry):
        if fresh:
            copy(i).wait()
        for s in range(0, LOCAL_STEP, 2):
            xs, ws = [], []
            b = i * LOCAL_STEP + s
            for at in (b, b + 1):
                if fresh:
                    w = jnp.concatenate([pair(tiles_ref, at * (32 * kt) + k, kt) for k in range(0, kt, 2)], axis=1)
                    w_ref[at] = w
                    ws.append(w)
                else:
                    ws.append(w_ref[at])
                x = [x_ref[lax.rem(at + cols_ref[k, 0], blocks)] for k in range(kt)]
                xs.append(jnp.concatenate([jnp.where(wide, x[k], x[k + 1]) for k in range(0, kt, 2)], axis=1))
            w = jnp.concatenate(ws, axis=0)
            none = jnp.zeros_like(y_ref[b])
            out = dot(rows_and_lanes([[y_ref[b], none], [none, y_ref[b + 1]]]), w)
            t_ref[b] = halves(out[: 2 * nf], nf)
            t_ref[b + 1] = halves(out[2 * nf :], nf)
            out = dot_nt(jnp.concatenate(xs, axis=0), w)
            u_ref[b] = stacked(halves(out[: 2 * nf, :LANES], nf))
            u_ref[b + 1] = stacked(halves(out[2 * nf :, LANES:], nf))
        return carry

    lax.fori_loop(0, blocks // LOCAL_STEP, body, 0)
    matrix = out_of_rows()
    low = lane_of((nf, LANES)) < 64

    def finish(i, carry):
        out = dot(u_ref[pl.ds(i * 32, 32)].reshape(32 * 2 * nf, LANES), matrix)
        for j in range(32):
            b = i * 32 + j
            t = None
            for k in range(0, kt, 2):
                at = slice(k // 2 * LANES, (k // 2 + 1) * LANES)
                v = jnp.where(low, t_ref[lax.rem(b + blocks - cols_ref[k, 0], blocks), :, at],
                              t_ref[lax.rem(b + blocks - cols_ref[k + 1, 0], blocks), :, at])
                t = v if t is None else t + v
            acc_ref[b] = z_ref[b, 0:nf] + halves(out[j * 2 * nf : (j + 1) * 2 * nf], nf) + t + turn(t)
        return carry

    lax.fori_loop(0, blocks // 32, finish, 0)
    for vector, natural in zip(vectors, naturals):
        to_natural(vector, natural, blocks)


def odd_sector():
    return lax.rem(lax.axis_index("sector"), 2)


def sends(way):
    return 1 - odd_sector() if way == 0 else odd_sector() if way == 1 else 5 - way


def receives(way):
    return odd_sector() if way == 0 else 1 - odd_sector() if way == 1 else way


def present(way, d):
    if way > 1:
        return None
    end = d * (lax.axis_size("slab") - 1)
    return jnp.where(lax.axis_index("slab") == end, 0.0, 1.0)


def absorb(acc_ref, incs, tile, send_ref, recv_ref, counts_ref, nf, cap):
    matrix = out_of_rows()
    low = lane_of((nf, LANES)) < 64
    for way in range(4):
        d = receives(way)
        there = present(way, d)

        def body(g, carry, d=d, way=way, there=there):
            rows = []
            back = []
            for j in range(0, ABSORB_STEP, 4):
                xs = []
                for i in range(4):
                    c = g * ABSORB_STEP + j + i
                    arr = jnp.concatenate([inc[c, at : at + nf // len(incs[way])] for inc, at in incs[way]], axis=0)
                    if there is not None:
                        arr = arr * there
                    hi, lo = split(arr)
                    xs.append(jnp.where(low, hi, turn(lo)))
                    weight = jnp.where(c < counts_ref[0, 0, d], 1.0, 0.0)
                    back.append(jnp.where(low, turn(arr), arr) * weight)
                ws = [tile(d * cap + g * ABSORB_STEP, j + i) for i in range(4)]
                rows += [stacked(u) for u in straight_products(xs, ws, nf)]
            out = dot(jnp.concatenate(rows, axis=0), matrix)
            spots = [recv_ref[d, g * ABSORB_STEP + j] for j in range(ABSORB_STEP)]
            old = [acc_ref[s] for s in spots]
            for j in range(ABSORB_STEP):
                acc_ref[spots[j]] = old[j] + halves(out[j * 2 * nf : (j + 1) * 2 * nf], nf)
            spots = [send_ref[d, g * ABSORB_STEP + j] for j in range(ABSORB_STEP)]
            old = [acc_ref[s] for s in spots]
            for j in range(ABSORB_STEP):
                acc_ref[spots[j]] = old[j] + back[j]
            return carry

        lax.fori_loop(0, cap // ABSORB_STEP, body, 0)


def second_kernel(nf, blocks, cap, acc_in, i0, i1, i2, i3, z_ref, winv_ref, wcoup_ref, send_hbm, recv_hbm, counts_hbm,
                  m0, m1, m2, m3, acc_ref, wd_ref, y0_ref, y_ref, send_ref, recv_ref, counts_ref, sems):
    listed = lists([send_hbm, recv_hbm, counts_hbm], [send_ref, recv_ref, counts_ref], sems)
    acc_ref[...] = acc_in[...]
    wd_ref[:, nf:] = z_ref[:, nf:]
    for i in range(3):
        listed.wait(i)
    coup = kept(wcoup_ref)
    absorb(acc_ref, [[(inc, 0)] for inc in (i0, i1, i2, i3)], coup, send_ref, recv_ref, counts_ref, nf, cap)
    matrix = into_rows()
    write_row_form(lambda b: acc_ref[b], y0_ref, nf, blocks, matrix)
    smooth_into(kept(winv_ref), y0_ref, wd_ref, nf, blocks)
    write_row_form(lambda b: wd_ref[b, 0:nf], y_ref, nf, blocks, matrix)
    write_messages(lambda b: wd_ref[b, 0:nf], y_ref, lambda way: None, coup, send_ref, recv_ref, counts_ref,
                   ((m0,), (m1,), (m2,), (m3,)), nf, cap)


def column_of(values, lane, at):
    return jnp.sum(jnp.where(lane == at, values, 0.0), axis=1, keepdims=True)


def packed(x):
    return jnp.where(lane_of((4, LANES)) < 64, x[0:4], turn(x[4:8]))


def third_kernel(nf, blocks, cap, acc_in, i0, i1, i2, i3, d0, d1, e2, e3, wcoup_ref, send_ref, recv_ref, counts_ref,
                 zn_ref, qn_ref, wn_ref, r0_ref, cd_ref, sn_ref, pay_ref, acc_ref, g_ref):
    acc_ref[...] = acc_in[...]
    incs = [[(i0, 0), (d0, 0)], [(i1, 0), (d1, 0)], [(i2, 0), (e2, nf)], [(i3, 0), (e3, nf)]]
    absorb(acc_ref, incs, kept(wcoup_ref), send_ref, recv_ref, counts_ref,
           acc_ref.shape[1], cap)
    to_natural(acc_ref, sn_ref, blocks)
    z = zn_ref[0:nf, :]
    q = qn_ref[...]
    w = wn_ref[...]
    r = r0_ref[...]
    s = sn_ref[0:nf, :]

    def inner(a, b):
        return jnp.sum(a * b, axis=1, keepdims=True)

    gamma = inner(r, z)
    base = inner(z, q)
    safe = jnp.where(base > 0.0, base, 1.0)
    centre = jnp.where(base > 0.0, jnp.clip(gamma / safe, 0.0, 4.0), 0.0)
    zc = z - centre * w
    kz = q - centre * s
    values = {
        16: gamma,
        17: base,
        18: inner(r - centre * q, zc),
        19: inner(q, zc),
        20: inner(q, w),
        21: inner(zc, kz),
        22: inner(zc, s),
        23: inner(w, s),
    }
    left_hi, left_lo = split(jnp.concatenate([z, w, zn_ref[nf:, :]], axis=0))
    right_hi, right_lo = split(jnp.concatenate([cd_ref[...], sn_ref[nf:, :]], axis=0))
    left = jnp.concatenate([left_hi, left_lo], axis=0).astype(BF16)
    products = dot_nt(left, right_hi.astype(BF16)) + dot_nt(left, right_lo.astype(BF16))
    g_ref[...] = jnp.zeros_like(g_ref)
    g_ref[:, 0:16] = products[:24] + products[24:]
    lane = lane_of((nf, LANES))
    pay = g_ref[0:8, :] + pltpu.roll(g_ref[8:16, :], 32, 1) + pltpu.roll(g_ref[16:24, :], 48, 1)
    for at, value in values.items():
        pay = jnp.where(lane == at, value, pay)
    pay = jnp.where((lane >= 24) & (lane < 30), centre, pay)
    pay_ref[...] = jnp.broadcast_to(packed(pay)[None], pay_ref.shape)


def last_kernel(nf, rho, all_ref, zn_ref, wn_ref, qn_ref, r0_ref, cd_ref, sn_ref, x_ref, res_ref):
    lane = lane_of((nf, LANES))
    total = lax.fori_loop(0, all_ref.shape[0], lambda d, t: t + all_ref[d], jnp.zeros((nf // 2, LANES), F32), unroll=32)
    total = jnp.concatenate([total, turn(total)], axis=0)

    def mat(a, b):
        out = None
        for g in range(a.shape[1]):
            term = a[:, g : g + 1] * b[g : g + 1, :]
            out = term if out is None else out + term
        return out

    t0 = total[:, 0:8]
    z_h = total[:, 8:16]
    cw = total[:, 32:40]
    w_h = total[:, 40:48]
    b = total[:, 48:56]
    d_h = total[:, 56:64]
    gamma0 = column_of(total, lane, 16)
    base = column_of(total, lane, 17) + rho * jnp.sum(t0 * t0, axis=1, keepdims=True)
    alpha0 = gamma0 / base
    wide = packed(jnp.broadcast_to(alpha0, (nf, LANES)))
    spot = lane_of((nf // 2, LANES)) % 64
    constant = (spot == 18) | (spot == 21)
    linear = (spot == 19) | (spot == 22)

    def about(d, carry):
        part = all_ref[d]
        off = wide - pltpu.roll(part, LANES - 6, 1)
        return carry + part * jnp.where(constant, 1.0, jnp.where(linear, -2.0 * off, off * off))

    sums = lax.fori_loop(0, all_ref.shape[0], about, jnp.zeros((nf // 2, LANES), F32), unroll=32)
    sums = jnp.concatenate([sums, turn(sums)], axis=0)
    gamma1 = jnp.sum(jnp.where((lane >= 18) & (lane < 21), sums, 0.0), axis=1, keepdims=True)
    delta = jnp.sum(jnp.where((lane >= 21) & (lane < 24), sums, 0.0), axis=1, keepdims=True)
    t0b = mat(t0, b)
    t0d = mat(t0, d_h)
    tw = cw + rho * t0b
    cz = t0 - alpha0 * tw
    step = alpha0 * rho
    gamma1 = gamma1 + step * jnp.sum(t0 * (step * t0b - 2.0 * (t0 - alpha0 * cw)), axis=1, keepdims=True)
    delta = delta + jnp.sum(step * t0 * (step * t0d - 2.0 * (z_h - alpha0 * w_h)) + rho * cz * cz, axis=1, keepdims=True)
    beta = gamma1 / gamma0
    alpha1 = gamma1 / (delta - beta * (gamma1 / alpha0))
    both = alpha0 * alpha1
    lead = alpha0 + alpha1 * (1.0 + beta)
    on_d = -(both * rho) * t0
    on_c = rho * (both * tw - lead * t0)
    chunk = 32 * LANES

    def body(i, carry):
        at = pl.ds(pl.multiple_of(i * chunk, chunk), chunk)
        x_ref[:, at] = lead * zn_ref[0:nf, at] - both * wn_ref[:, at] + weighted_rows(on_d, zn_ref.at[nf:], at)
        res_ref[:, at] = (
            r0_ref[:, at] - lead * qn_ref[:, at] + both * sn_ref[0:nf, at]
            + (weighted_rows(on_c, cd_ref, at) - weighted_rows(on_d, sn_ref.at[nf:], at))
        )
        return carry

    lax.fori_loop(0, x_ref.shape[1] // chunk, body, 0)


SMEM = pl.BlockSpec(memory_space=pltpu.SMEM)
VMEM = pl.BlockSpec(memory_space=pltpu.VMEM)
ANY = pl.BlockSpec(memory_space=pltpu.HBM)
PARAMS = pltpu.CompilerParams(vmem_limit_bytes=20 * 1024 * 1024)


def like(*shape, dtype=F32):
    return pltpu.VMEM(shape, dtype)


def in_hbm(x):
    return pltpu.with_memory_space_constraint(x, pltpu.HBM)


def call(kernel, ins, outs, scratch, name, flops=0):
    return pl.pallas_call(
        kernel, in_specs=ins, out_shape=outs, out_specs=jax.tree.map(lambda _: VMEM, outs), scratch_shapes=scratch,
        compiler_params=PARAMS, name=name,
        cost_estimate=pl.CostEstimate(flops=flops, transcendentals=0, bytes_accessed=8 << 20) if flops else None)


def along_slabs(*blocks):
    slabs, sectors = lax.axis_size("slab"), lax.axis_size("sector")

    def steps(way):
        pairs = []
        for s in range(slabs):
            for e in range(sectors):
                to = s + 1 if (e + way) % 2 == 0 else s - 1
                target = (to, e) if 0 <= to < slabs else (s, e ^ 1)
                pairs.append((s * sectors + e, target[0] * sectors + target[1]))
        return pairs

    return tuple(lax.ppermute(block, AXES, steps(way)) for way, block in enumerate(blocks) if block is not None)


def along_sectors(one, two):
    count = lax.axis_size("sector")
    up = [(i, (i + 1) % count) for i in range(count)]
    down = [((i + 1) % count, i) for i in range(count)]
    return lax.ppermute(one, "sector", up), lax.ppermute(two, "sector", down)


def exchange(msgs):
    return along_slabs(msgs[0], msgs[1]) + along_sectors(msgs[2], msgs[3])


def rows_of(x, group):
    n = x.shape[0]
    return x.reshape(n // group, group, 32, LANES).transpose(0, 2, 1, 3).reshape(n * 32, LANES)


def on_device(source, periods, tiles, columns, coupling, send_list, recv_rows, counts, cycle_edges, cycle_signs, inverse_blocks):
    src = source[0, 0]
    nf, width = src.shape
    blocks = width // TILE
    kt = tiles.shape[3]
    cap = coupling.shape[3]
    cycles = periods.shape[0]
    both = nf + cycles
    devices = lax.axis_size("slab") * lax.axis_size("sector")
    rho = 1.0 / (cycle_edges.shape[3] * devices)
    tiles2 = in_hbm(rows_of(tiles[0, 0].reshape(blocks * kt, TILE * TILE), kt))
    coup2 = in_hbm(rows_of(coupling[0, 0].reshape(4 * cap, TILE * TILE), 8))
    inv2 = in_hbm(rows_of(inverse_blocks[0, 0], 8))
    send, recv, cols = in_hbm(send_list[0, 0]), in_hbm(recv_rows[0, 0]), in_hbm(columns[0, 0].T)
    counts, periods, src = in_hbm(counts), in_hbm(periods), in_hbm(src)
    edges, signs = in_hbm(cycle_edges[0, 0]), in_hbm(cycle_signs[0, 0])
    msg = like(cap, nf, LANES)
    rows = pltpu.VMEM((blocks, 2 * nf, LANES), BF16)
    tables = [pltpu.SMEM(send.shape, jnp.int32), pltpu.SMEM(recv.shape, jnp.int32), pltpu.SMEM(counts.shape, jnp.int32),
              pltpu.SemaphoreType.DMA((3,))]
    rows_both = pltpu.VMEM((blocks, 2 * both, LANES), BF16)
    *msgs, z, r0, cd, winv, wcoup = call(
        functools.partial(first_kernel, both, blocks, cap),
        [ANY] * 9,
        [msg] * 2 + [like(cap, both, LANES)] * 2 + [msg] * 2 + [
            like(blocks, both, LANES), like(nf, width), like(cycles, width), like(blocks, LANES, LANES, dtype=BF16),
            like(4 * cap, LANES, LANES, dtype=BF16)],
        [pltpu.VMEM((blocks, both, LANES), F32), rows_both, rows_both, pltpu.VMEM(inv2.shape, F32),
         pltpu.VMEM(coup2.shape, F32), pltpu.VMEM(src.shape, F32), pltpu.VMEM(periods.shape, F32),
         pltpu.VMEM(edges.shape, jnp.int32), pltpu.VMEM(signs.shape, jnp.int32), pltpu.SMEM(send.shape, jnp.int32),
         pltpu.SMEM(recv.shape, jnp.int32), pltpu.SMEM(counts.shape, jnp.int32), pltpu.SemaphoreType.DMA((12,))],
        "first",
    )(src, periods, edges, signs, inv2, coup2, send, recv, counts)

    def local(n, fresh, tiles, *vectors):
        out = [like(blocks, n, LANES)]
        if fresh:
            out.append(like(blocks, LANES, kt // 2 * LANES, dtype=BF16))
        out += [like(both, width)] if fresh else [like(nf, width)] * 2
        form = pltpu.VMEM((blocks, 2 * n, LANES), BF16)
        scratch = [form, form, form, pltpu.VMEM((blocks, n, kt // 2 * LANES), F32), pltpu.SMEM(cols.shape, jnp.int32),
                   pltpu.SemaphoreType.DMA((1,))]
        if fresh:
            scratch += [pltpu.VMEM(tiles.shape, F32), pltpu.SemaphoreType.DMA((blocks // LOCAL_STEP,))]
        return call(
            functools.partial(local_kernel, n, blocks, kt, fresh, len(vectors)),
            [ANY, ANY if fresh else VMEM] + [VMEM] * len(vectors), out, scratch, "local", flops=2 * 10**9,
        )(cols, tiles, *vectors)

    incoming = exchange(msgs[:4])
    early = along_slabs(None, msgs[5])
    acc, forms, zn = local(nf, True, tiles2, z)
    acc, incoming, last = lax.optimization_barrier((acc, incoming, msgs[4]))
    later = along_slabs(last, None) + early + incoming[2:]
    *msgs, q, wd = call(
        functools.partial(second_kernel, nf, blocks, cap),
        [VMEM] * 8 + [ANY] * 3,
        [msg] * 4 + [like(blocks, nf, LANES), like(blocks, both, LANES)],
        [rows, rows] + tables,
        "second",
    )(acc, *incoming, z, winv, wcoup, send, recv, counts)
    msgs, later = lax.optimization_barrier((msgs, later))
    incoming = exchange(msgs)
    acc, wn, qn = local(both, False, forms, wd, q)
    sn, pay = call(
        functools.partial(third_kernel, nf, blocks, cap),
        [VMEM] * 10 + [SMEM] * 3 + [VMEM] * 5,
        [like(both, width), like(devices, nf // 2, LANES)],
        [pltpu.VMEM((blocks, both, LANES), F32), pltpu.VMEM((nf + both, LANES), F32)],
        "third",
    )(acc, *incoming, *later, wcoup, send, recv, counts, zn, qn, wn, r0, cd)
    everyone = lax.all_to_all(pay, AXES, 0, 0)
    out, res = call(
        functools.partial(last_kernel, nf, rho),
        [VMEM] * 7,
        [jax.ShapeDtypeStruct((nf, width), F32)] * 2,
        [],
        "last",
    )(everyone, zn, wn, qn, r0, cd, sn)
    return out[None, None], res[None, None]


def solution(mesh):
    two = P("slab", "sector")
    return jax.shard_map(
        on_device,
        mesh=mesh,
        in_specs=(two, P(), two, two, two, two, two, two, two, two, two),
        out_specs=(two, two),
        check_vma=False,
    )
```

```python
import functools

import jax
import jax.numpy as jnp
from jax import lax
from jax.experimental import pallas as pl
from jax.experimental.pallas import tpu as pltpu
from jax.sharding import PartitionSpec as P

TILE = 64
LANES = 128
F32 = jnp.float32
BF16 = jnp.bfloat16
AXES = ("slab", "sector")
ROWS_STEP = 64
SMOOTH_STEP = 64
SEND_STEP = 32
ABSORB_STEP = 32
LOCAL_STEP = 16


def lane_of(shape):
    return lax.broadcasted_iota(jnp.int32, shape, len(shape) - 1)


def split(x):
    hi = x.astype(BF16)
    lo = x - hi.astype(F32)
    return hi.astype(F32), lo


def turn(x):
    return pltpu.roll(x, 64, x.ndim - 1)


def into_rows():
    row = lax.broadcasted_iota(jnp.int32, (LANES, LANES), 0)
    col = lane_of((LANES, LANES))
    return jnp.where(row == 2 * (col % 32) + (col // 32) % 2, 1.0, 0.0).astype(BF16)


def out_of_rows():
    row = lax.broadcasted_iota(jnp.int32, (LANES, LANES), 0)
    col = lane_of((LANES, LANES))
    return jnp.where(col % 64 == 2 * (row % 32) + (row // 32) % 2, 1.0, 0.0).astype(BF16)


def stacked(x):
    hi, lo = split(x)
    return jnp.concatenate([hi, lo], axis=0).astype(BF16)


def single(ref, start, stride):
    v = ref[pl.ds(start, 32, stride=stride), :]
    t = turn(v)
    low = lane_of(v.shape) < 64
    return stacked(jnp.concatenate([jnp.where(low, v, t), jnp.where(low, t, v)], axis=0))


def pair(ref, start, stride):
    a = ref[pl.ds(start, 32, stride=stride), :]
    b = ref[pl.ds(start + 1, 32, stride=stride), :]
    low = lane_of(a.shape) < 64
    return stacked(jnp.concatenate([jnp.where(low, a, turn(b)), jnp.where(low, turn(a), b)], axis=0))


def dot(a, b):
    return lax.dot_general(a, b, (((1,), (0,)), ((), ())), preferred_element_type=F32)


def dot_nt(a, b):
    return lax.dot_general(a, b, (((1,), (1,)), ((), ())), preferred_element_type=F32)


def rows_and_lanes(parts):
    return jnp.concatenate([jnp.concatenate(row, axis=1) for row in parts], axis=0)


def turned_products(ys, ws, nf):
    none = jnp.zeros_like(ys[0])
    left = rows_and_lanes([[ys[0], none], [ys[1], none], [none, ys[2]], [none, ys[3]]])
    out = dot(left, rows_and_lanes([ws[:2], ws[2:]]))
    n = 2 * nf
    return [halves(out[i * n : (i + 1) * n, i % 2 * LANES : (i % 2 + 1) * LANES], nf) for i in range(4)]


def straight_products(xs, ws, nf):
    none = jnp.zeros_like(xs[0])
    left = rows_and_lanes([[xs[0], none], [none, xs[1]], [xs[2], none], [none, xs[3]]]).astype(BF16)
    out = dot_nt(left, rows_and_lanes([ws[:2], ws[2:]]))
    return [out[i * nf : (i + 1) * nf, i // 2 * LANES : (i // 2 + 1) * LANES] for i in range(4)]


def halves(out, nf):
    return out[:nf] + out[nf:]


def write_row_form(load, y_ref, nf, blocks, matrix):
    def body(i, carry):
        x = jnp.concatenate([stacked(load(i * ROWS_STEP + j)) for j in range(ROWS_STEP)], axis=0)
        out = dot(x, matrix).astype(BF16)
        for j in range(ROWS_STEP):
            y_ref[i * ROWS_STEP + j] = out[j * 2 * nf : (j + 1) * 2 * nf]
        return carry

    lax.fori_loop(0, blocks // ROWS_STEP, body, 0)


def to_natural(ref, nat_ref, blocks):
    rows = nat_ref.shape[0]
    low = lane_of((rows, LANES)) < 64
    for t in range(blocks // 2):
        a = ref[2 * t]
        b = ref[2 * t + 1]
        nat_ref[:, t * LANES : (t + 1) * LANES] = jnp.where(low, a[:rows], b[:rows])


def made(ref, keep_ref):
    def tile(first, j):
        w = single(ref, first * 32 + (j // 8) * 256 + j % 8, 8)
        keep_ref[first + j] = w
        return w

    return tile


def kept(keep_ref):
    return lambda first, j: keep_ref[first + j]


def smooth_into(tile, y_ref, out_ref, nf, blocks):
    def body(g, carry):
        for c in range(0, SMOOTH_STEP, 4):
            ws = [tile(g * SMOOTH_STEP, c + i) for i in range(4)]
            at = g * SMOOTH_STEP + c
            for i, value in enumerate(turned_products([y_ref[at + i] for i in range(4)], ws, nf)):
                out_ref[at + i, 0:nf] = value
        return carry

    lax.fori_loop(0, blocks // SMOOTH_STEP, body, 0)


def write_messages(load, y_ref, ready, tile, send_ref, recv_ref, counts_ref, msgs, nf, cap):
    low = lane_of((nf, LANES)) < 64
    for way in range(4):
        ready(way)
        d = sends(way)

        def body(g, carry, d=d, way=way):
            for j in range(0, SEND_STEP, 4):
                c = g * SEND_STEP + j
                ws = [tile(d * cap + g * SEND_STEP, j + i) for i in range(4)]
                ys = [y_ref[recv_ref[d, c + i]] for i in range(4)]
                for i, partner in enumerate(turned_products(ys, ws, nf)):
                    weight = jnp.where(c + i < counts_ref[0, 0, d], 1.0, 0.0)
                    value = jnp.where(low, load(send_ref[d, c + i]) * weight, partner)
                    at = 0
                    for msg in msgs[way]:
                        msg[c + i] = value[at : at + msg.shape[1]]
                        at += msg.shape[1]
            return carry

        lax.fori_loop(0, cap // SEND_STEP, body, 0)


class Copies:
    def __init__(self, sems, pairs):
        self.copies = [pltpu.make_async_copy(a, b, sems.at[i]) for i, (a, b) in enumerate(pairs)]
        for copy in self.copies:
            copy.start()

    def wait(self, i):
        self.copies[i].wait()


def lists(hbm, smem, sems):
    return Copies(sems, list(zip(hbm, smem)))


def quarters(hbm, vmem):
    rows = vmem.shape[0] // 4
    return [(hbm.at[pl.ds(d * rows, rows)], vmem.at[pl.ds(d * rows, rows)]) for d in range(4)]


def weighted_rows(coef, rows, at):
    out = None
    for g in range(coef.shape[1]):
        term = coef[:, g : g + 1] * rows[g : g + 1, at]
        out = term if out is None else out + term
    return out


def first_kernel(nf, blocks, cap, src_hbm, per_hbm, edges_hbm, signs_hbm, inv_hbm, coup_hbm, send_hbm, recv_hbm,
                 counts_hbm, m0, m1, m2, m3, d0, d1, z_ref, r0_ref, cd_ref, winv_ref, wcoup_ref,
                 x_ref, y0_ref, y_ref, inv_ref, coup_ref, src_ref, per_ref, edges_ref, signs_ref, send_ref, recv_ref,
                 counts_ref, sems):
    small = [(edges_hbm, edges_ref), (signs_hbm, signs_ref), (per_hbm, per_ref), (src_hbm, src_ref), (send_hbm, send_ref),
             (recv_hbm, recv_ref), (counts_hbm, counts_ref)]
    large = [(inv_hbm, inv_ref)] + quarters(coup_hbm, coup_ref)
    copies = Copies(sems, small + large)
    for i in range(len(small)):
        copies.wait(i)
    fields = src_ref.shape[0]
    width = src_ref.shape[1]
    count = edges_ref.shape[0]
    edges = edges_ref[...]
    orient = (2 * signs_ref[...] - 1).astype(F32)
    low = lane_of((fields, LANES)) < 64
    step = 32 * LANES
    place = lane_of((count, step))
    totals = per_ref[...].T

    def cycles(t, carry):
        at = pl.ds(pl.multiple_of(t * step, step), step)
        here = place + t * step
        total = jnp.zeros((count, step), F32)
        for l in range(edges.shape[1]):
            total = jnp.where(edges[:, l : l + 1] == here, orient[:, l : l + 1], total)
        cd_ref[:, at] = total
        r0_ref[:, at] = src_ref[:, at] + weighted_rows(totals, cd_ref, at)
        return carry

    lax.fori_loop(0, width // step, cycles, 0)
    for t in range(width // LANES):
        r = r0_ref[:, t * LANES : (t + 1) * LANES]
        c = cd_ref[:, t * LANES : (t + 1) * LANES]
        rt = turn(r)
        ct = turn(c)
        x_ref[2 * t] = jnp.concatenate([jnp.where(low, r, rt), jnp.where(low, c, ct)], axis=0)
        x_ref[2 * t + 1] = jnp.concatenate([jnp.where(low, rt, r), jnp.where(low, ct, c)], axis=0)
    matrix = into_rows()
    write_row_form(lambda b: x_ref[b], y0_ref, nf, blocks, matrix)
    copies.wait(len(small))
    smooth_into(made(inv_ref, winv_ref), y0_ref, z_ref, nf, blocks)
    write_row_form(lambda b: z_ref[b], y_ref, nf, blocks, matrix)


    def ready(way):
        for part in ((0, 1), (), (2, 3), ())[way]:
            copies.wait(len(small) + 1 + part)

    write_messages(lambda b: z_ref[b], y_ref, ready, made(coup_ref, wcoup_ref),
                   send_ref, recv_ref, counts_ref, ((m0, d0), (m1, d1), (m2,), (m3,)), nf, cap)


def local_kernel(nf, blocks, kt, fresh, plain, cols_hbm, tiles_in, *rest):
    vectors, rest = rest[:plain], rest[plain:]
    z_ref = vectors[0]
    acc_ref, rest = rest[0], rest[1:]
    w_ref, rest = (rest[0], rest[1:]) if fresh else (tiles_in, rest)
    naturals, (x_ref, y_ref, u_ref, t_ref, cols_ref, col_sem) = rest[:plain], rest[plain : plain + 6]
    listed = lists([cols_hbm], [cols_ref], col_sem)
    if fresh:
        tiles_ref, sems = rest[plain + 6 :]
        rows = LOCAL_STEP * kt * 32

        def copy(i):
            at = pl.ds(pl.multiple_of(i * rows, rows), rows)
            return pltpu.make_async_copy(tiles_in.at[at], tiles_ref.at[at], sems.at[i])

        for i in range(blocks // LOCAL_STEP):
            copy(i).start()
    write_row_form(lambda b: z_ref[b, 0:nf], y_ref, nf, blocks, into_rows())

    def left(b, carry):
        x_ref[b] = stacked(z_ref[b, 0:nf])
        return carry

    lax.fori_loop(0, blocks, left, 0, unroll=8)
    listed.wait(0)
    wide = lane_of((2 * nf, LANES)) < 64

    def body(i, carry):
        if fresh:
            copy(i).wait()
        for s in range(0, LOCAL_STEP, 2):
            xs, ws = [], []
            b = i * LOCAL_STEP + s
            for at in (b, b + 1):
                if fresh:
                    w = jnp.concatenate([pair(tiles_ref, at * (32 * kt) + k, kt) for k in range(0, kt, 2)], axis=1)
                    w_ref[at] = w
                    ws.append(w)
                else:
                    ws.append(w_ref[at])
                x = [x_ref[lax.rem(at + cols_ref[k, 0], blocks)] for k in range(kt)]
                xs.append(jnp.concatenate([jnp.where(wide, x[k], x[k + 1]) for k in range(0, kt, 2)], axis=1))
            w = jnp.concatenate(ws, axis=0)
            none = jnp.zeros_like(y_ref[b])
            out = dot(rows_and_lanes([[y_ref[b], none], [none, y_ref[b + 1]]]), w)
            t_ref[b] = halves(out[: 2 * nf], nf)
            t_ref[b + 1] = halves(out[2 * nf :], nf)
            out = dot_nt(jnp.concatenate(xs, axis=0), w)
            u_ref[b] = stacked(halves(out[: 2 * nf, :LANES], nf))
            u_ref[b + 1] = stacked(halves(out[2 * nf :, LANES:], nf))
        return carry

    lax.fori_loop(0, blocks // LOCAL_STEP, body, 0)
    matrix = out_of_rows()
    low = lane_of((nf, LANES)) < 64

    def finish(i, carry):
        out = dot(u_ref[pl.ds(i * 64, 64)].reshape(64 * 2 * nf, LANES), matrix)
        for j in range(64):
            b = i * 64 + j
            t = None
            for k in range(0, kt, 2):
                at = slice(k // 2 * LANES, (k // 2 + 1) * LANES)
                v = jnp.where(low, t_ref[lax.rem(b + blocks - cols_ref[k, 0], blocks), :, at],
                              t_ref[lax.rem(b + blocks - cols_ref[k + 1, 0], blocks), :, at])
                t = v if t is None else t + v
            acc_ref[b] = z_ref[b, 0:nf] + halves(out[j * 2 * nf : (j + 1) * 2 * nf], nf) + t + turn(t)
        return carry

    lax.fori_loop(0, blocks // 64, finish, 0)
    for vector, natural in zip(vectors, naturals):
        to_natural(vector, natural, blocks)


def odd_sector():
    return lax.rem(lax.axis_index("sector"), 2)


def sends(way):
    odd = odd_sector()
    return (1 - odd, odd, 3 - odd, 2 + odd)[way]


def receives(way):
    odd = odd_sector()
    return (odd, 1 - odd, 3 - odd, 2 + odd)[way]


def present(way, d):
    if way > 1:
        return None
    end = d * (lax.axis_size("slab") - 1)
    return jnp.where(lax.axis_index("slab") == end, 0.0, 1.0)


def absorb(acc_ref, incs, tile, send_ref, recv_ref, counts_ref, nf, cap):
    matrix = out_of_rows()
    low = lane_of((nf, LANES)) < 64
    for way in range(4):
        d = receives(way)
        there = present(way, d)

        def body(g, carry, d=d, way=way, there=there):
            rows = []
            back = []
            for j in range(0, ABSORB_STEP, 4):
                xs = []
                for i in range(4):
                    c = g * ABSORB_STEP + j + i
                    arr = jnp.concatenate([inc[c, at : at + nf // len(incs[way])] for inc, at in incs[way]], axis=0)
                    if there is not None:
                        arr = arr * there
                    hi, lo = split(arr)
                    xs.append(jnp.where(low, hi, turn(lo)))
                    weight = jnp.where(c < counts_ref[0, 0, d], 1.0, 0.0)
                    back.append(jnp.where(low, turn(arr), arr) * weight)
                ws = [tile(d * cap + g * ABSORB_STEP, j + i) for i in range(4)]
                rows += [stacked(u) for u in straight_products(xs, ws, nf)]
            out = dot(jnp.concatenate(rows, axis=0), matrix)
            spots = [recv_ref[d, g * ABSORB_STEP + j] for j in range(ABSORB_STEP)]
            old = [acc_ref[s] for s in spots]
            for j in range(ABSORB_STEP):
                acc_ref[spots[j]] = old[j] + halves(out[j * 2 * nf : (j + 1) * 2 * nf], nf)
            spots = [send_ref[d, g * ABSORB_STEP + j] for j in range(ABSORB_STEP)]
            old = [acc_ref[s] for s in spots]
            for j in range(ABSORB_STEP):
                acc_ref[spots[j]] = old[j] + back[j]
            return carry

        lax.fori_loop(0, cap // ABSORB_STEP, body, 0)


def second_kernel(nf, blocks, cap, acc_in, i0, i1, i2, i3, z_ref, winv_ref, wcoup_ref, send_hbm, recv_hbm, counts_hbm,
                  m0, m1, m2, m3, acc_ref, wd_ref, y0_ref, y_ref, send_ref, recv_ref, counts_ref, sems):
    listed = lists([send_hbm, recv_hbm, counts_hbm], [send_ref, recv_ref, counts_ref], sems)
    acc_ref[...] = acc_in[...]
    wd_ref[:, nf:] = z_ref[:, nf:]
    for i in range(3):
        listed.wait(i)
    coup = kept(wcoup_ref)
    absorb(acc_ref, [[(inc, 0)] for inc in (i0, i1, i2, i3)], coup, send_ref, recv_ref, counts_ref, nf, cap)
    matrix = into_rows()
    write_row_form(lambda b: acc_ref[b], y0_ref, nf, blocks, matrix)
    smooth_into(kept(winv_ref), y0_ref, wd_ref, nf, blocks)
    write_row_form(lambda b: wd_ref[b, 0:nf], y_ref, nf, blocks, matrix)
    write_messages(lambda b: wd_ref[b, 0:nf], y_ref, lambda way: None, coup, send_ref, recv_ref, counts_ref,
                   ((m0,), (m1,), (m2,), (m3,)), nf, cap)


def column_of(values, lane, at):
    return jnp.sum(jnp.where(lane == at, values, 0.0), axis=1, keepdims=True)


def packed(x):
    return jnp.where(lane_of((4, LANES)) < 64, x[0:4], turn(x[4:8]))


def third_kernel(nf, blocks, cap, acc_in, i0, i1, i2, i3, d0, d1, e2, e3, wcoup_ref, send_ref, recv_ref, counts_ref,
                 zn_ref, qn_ref, wn_ref, r0_ref, cd_ref, sn_ref, pay_ref, acc_ref, g_ref):
    acc_ref[...] = acc_in[...]
    incs = [[(i0, 0), (d0, 0)], [(i1, 0), (d1, 0)], [(i2, 0), (e2, nf)], [(i3, 0), (e3, nf)]]
    absorb(acc_ref, incs, kept(wcoup_ref), send_ref, recv_ref, counts_ref,
           acc_ref.shape[1], cap)
    to_natural(acc_ref, sn_ref, blocks)
    z = zn_ref[0:nf, :]
    q = qn_ref[...]
    w = wn_ref[...]
    r = r0_ref[...]
    s = sn_ref[0:nf, :]

    def inner(a, b):
        return jnp.sum(a * b, axis=1, keepdims=True)

    gamma = inner(r, z)
    base = inner(z, q)
    safe = jnp.where(base > 0.0, base, 1.0)
    centre = jnp.where(base > 0.0, jnp.clip(gamma / safe, 0.0, 4.0), 0.0)
    zc = z - centre * w
    kz = q - centre * s
    values = {
        16: gamma,
        17: base,
        18: inner(r - centre * q, zc),
        19: inner(q, zc),
        20: inner(q, w),
        21: inner(zc, kz),
        22: inner(zc, s),
        23: inner(w, s),
    }
    left_hi, left_lo = split(jnp.concatenate([z, w, zn_ref[nf:, :]], axis=0))
    right_hi, right_lo = split(jnp.concatenate([cd_ref[...], sn_ref[nf:, :]], axis=0))
    left = jnp.concatenate([left_hi, left_lo], axis=0).astype(BF16)
    products = dot_nt(left, right_hi.astype(BF16)) + dot_nt(left, right_lo.astype(BF16))
    g_ref[...] = jnp.zeros_like(g_ref)
    g_ref[:, 0:16] = products[:24] + products[24:]
    lane = lane_of((nf, LANES))
    pay = g_ref[0:8, :] + pltpu.roll(g_ref[8:16, :], 32, 1) + pltpu.roll(g_ref[16:24, :], 48, 1)
    for at, value in values.items():
        pay = jnp.where(lane == at, value, pay)
    pay = jnp.where((lane >= 24) & (lane < 30), centre, pay)
    pay_ref[...] = jnp.broadcast_to(packed(pay)[None], pay_ref.shape)


def last_kernel(nf, rho, all_ref, zn_ref, wn_ref, qn_ref, r0_ref, cd_ref, sn_ref, x_ref, res_ref):
    lane = lane_of((nf, LANES))
    total = lax.fori_loop(0, all_ref.shape[0], lambda d, t: t + all_ref[d], jnp.zeros((nf // 2, LANES), F32), unroll=32)
    total = jnp.concatenate([total, turn(total)], axis=0)

    def mat(a, b):
        out = None
        for g in range(a.shape[1]):
            term = a[:, g : g + 1] * b[g : g + 1, :]
            out = term if out is None else out + term
        return out

    t0 = total[:, 0:8]
    z_h = total[:, 8:16]
    cw = total[:, 32:40]
    w_h = total[:, 40:48]
    b = total[:, 48:56]
    d_h = total[:, 56:64]
    gamma0 = column_of(total, lane, 16)
    base = column_of(total, lane, 17) + rho * jnp.sum(t0 * t0, axis=1, keepdims=True)
    alpha0 = gamma0 / base
    wide = packed(jnp.broadcast_to(alpha0, (nf, LANES)))
    spot = lane_of((nf // 2, LANES)) % 64
    constant = (spot == 18) | (spot == 21)
    linear = (spot == 19) | (spot == 22)

    def about(d, carry):
        part = all_ref[d]
        off = wide - pltpu.roll(part, LANES - 6, 1)
        return carry + part * jnp.where(constant, 1.0, jnp.where(linear, -2.0 * off, off * off))

    sums = lax.fori_loop(0, all_ref.shape[0], about, jnp.zeros((nf // 2, LANES), F32), unroll=32)
    sums = jnp.concatenate([sums, turn(sums)], axis=0)
    gamma1 = jnp.sum(jnp.where((lane >= 18) & (lane < 21), sums, 0.0), axis=1, keepdims=True)
    delta = jnp.sum(jnp.where((lane >= 21) & (lane < 24), sums, 0.0), axis=1, keepdims=True)
    t0b = mat(t0, b)
    t0d = mat(t0, d_h)
    tw = cw + rho * t0b
    cz = t0 - alpha0 * tw
    step = alpha0 * rho
    gamma1 = gamma1 + step * jnp.sum(t0 * (step * t0b - 2.0 * (t0 - alpha0 * cw)), axis=1, keepdims=True)
    delta = delta + jnp.sum(step * t0 * (step * t0d - 2.0 * (z_h - alpha0 * w_h)) + rho * cz * cz, axis=1, keepdims=True)
    beta = gamma1 / gamma0
    alpha1 = gamma1 / (delta - beta * (gamma1 / alpha0))
    both = alpha0 * alpha1
    lead = alpha0 + alpha1 * (1.0 + beta)
    on_d = -(both * rho) * t0
    on_c = rho * (both * tw - lead * t0)
    chunk = 32 * LANES

    def body(i, carry):
        at = pl.ds(pl.multiple_of(i * chunk, chunk), chunk)
        x_ref[:, at] = lead * zn_ref[0:nf, at] - both * wn_ref[:, at] + weighted_rows(on_d, zn_ref.at[nf:], at)
        res_ref[:, at] = (
            r0_ref[:, at] - lead * qn_ref[:, at] + both * sn_ref[0:nf, at]
            + (weighted_rows(on_c, cd_ref, at) - weighted_rows(on_d, sn_ref.at[nf:], at))
        )
        return carry

    lax.fori_loop(0, x_ref.shape[1] // chunk, body, 0)


SMEM = pl.BlockSpec(memory_space=pltpu.SMEM)
VMEM = pl.BlockSpec(memory_space=pltpu.VMEM)
ANY = pl.BlockSpec(memory_space=pltpu.HBM)
PARAMS = pltpu.CompilerParams(vmem_limit_bytes=20 * 1024 * 1024)


def like(*shape, dtype=F32):
    return pltpu.VMEM(shape, dtype)


def in_hbm(x):
    return pltpu.with_memory_space_constraint(x, pltpu.HBM)


def call(kernel, ins, outs, scratch, name, flops=0):
    return pl.pallas_call(
        kernel, in_specs=ins, out_shape=outs, out_specs=jax.tree.map(lambda _: VMEM, outs), scratch_shapes=scratch,
        compiler_params=PARAMS, name=name,
        cost_estimate=pl.CostEstimate(flops=flops, transcendentals=0, bytes_accessed=8 << 20) if flops else None)


def along_slabs(*blocks):
    slabs, sectors = lax.axis_size("slab"), lax.axis_size("sector")

    def steps(way):
        pairs = []
        for s in range(slabs):
            for e in range(sectors):
                to = s + 1 if (e + way) % 2 == 0 else s - 1
                target = (to, e) if 0 <= to < slabs else (s, e ^ 1)
                pairs.append((s * sectors + e, target[0] * sectors + target[1]))
        return pairs

    return tuple(lax.ppermute(block, AXES, steps(way)) for way, block in enumerate(blocks) if block is not None)


def along_sectors(one, two):
    count = lax.axis_size("sector")
    swaps = [[(e, (e + 1 if (e + way) % 2 == 0 else e - 1) % count) for e in range(count)] for way in range(2)]
    return lax.ppermute(one, "sector", swaps[0]), lax.ppermute(two, "sector", swaps[1])


def exchange(msgs):
    return along_slabs(msgs[0], msgs[1]) + along_sectors(msgs[2], msgs[3])


def rows_of(x, group):
    n = x.shape[0]
    return x.reshape(n // group, group, 32, LANES).transpose(0, 2, 1, 3).reshape(n * 32, LANES)


def on_device(source, periods, tiles, columns, coupling, send_list, recv_rows, counts, cycle_edges, cycle_signs, inverse_blocks):
    src = source[0, 0]
    nf, width = src.shape
    blocks = width // TILE
    kt = tiles.shape[3]
    cap = coupling.shape[3]
    cycles = periods.shape[0]
    both = nf + cycles
    devices = lax.axis_size("slab") * lax.axis_size("sector")
    rho = 1.0 / (cycle_edges.shape[3] * devices)
    tiles2 = in_hbm(rows_of(tiles[0, 0].reshape(blocks * kt, TILE * TILE), kt))
    coup2 = in_hbm(rows_of(coupling[0, 0].reshape(4 * cap, TILE * TILE), 8))
    inv2 = in_hbm(rows_of(inverse_blocks[0, 0], 8))
    send, recv, cols = in_hbm(send_list[0, 0]), in_hbm(recv_rows[0, 0]), in_hbm(columns[0, 0].T)
    counts, periods, src = in_hbm(counts), in_hbm(periods), in_hbm(src)
    edges, signs = in_hbm(cycle_edges[0, 0]), in_hbm(cycle_signs[0, 0])
    msg = like(cap, nf, LANES)
    rows = pltpu.VMEM((blocks, 2 * nf, LANES), BF16)
    tables = [pltpu.SMEM(send.shape, jnp.int32), pltpu.SMEM(recv.shape, jnp.int32), pltpu.SMEM(counts.shape, jnp.int32),
              pltpu.SemaphoreType.DMA((3,))]
    rows_both = pltpu.VMEM((blocks, 2 * both, LANES), BF16)
    *msgs, z, r0, cd, winv, wcoup = call(
        functools.partial(first_kernel, both, blocks, cap),
        [ANY] * 9,
        [msg] * 2 + [like(cap, both, LANES)] * 2 + [msg] * 2 + [
            like(blocks, both, LANES), like(nf, width), like(cycles, width), like(blocks, LANES, LANES, dtype=BF16),
            like(4 * cap, LANES, LANES, dtype=BF16)],
        [pltpu.VMEM((blocks, both, LANES), F32), rows_both, rows_both, pltpu.VMEM(inv2.shape, F32),
         pltpu.VMEM(coup2.shape, F32), pltpu.VMEM(src.shape, F32), pltpu.VMEM(periods.shape, F32),
         pltpu.VMEM(edges.shape, jnp.int32), pltpu.VMEM(signs.shape, jnp.int32), pltpu.SMEM(send.shape, jnp.int32),
         pltpu.SMEM(recv.shape, jnp.int32), pltpu.SMEM(counts.shape, jnp.int32), pltpu.SemaphoreType.DMA((12,))],
        "first",
    )(src, periods, edges, signs, inv2, coup2, send, recv, counts)

    def local(n, fresh, tiles, *vectors):
        out = [like(blocks, n, LANES)]
        if fresh:
            out.append(like(blocks, LANES, kt // 2 * LANES, dtype=BF16))
        out += [like(both, width)] if fresh else [like(nf, width)] * 2
        form = pltpu.VMEM((blocks, 2 * n, LANES), BF16)
        scratch = [form, form, form, pltpu.VMEM((blocks, n, kt // 2 * LANES), F32), pltpu.SMEM(cols.shape, jnp.int32),
                   pltpu.SemaphoreType.DMA((1,))]
        if fresh:
            scratch += [pltpu.VMEM(tiles.shape, F32), pltpu.SemaphoreType.DMA((blocks // LOCAL_STEP,))]
        return call(
            functools.partial(local_kernel, n, blocks, kt, fresh, len(vectors)),
            [ANY, ANY if fresh else VMEM] + [VMEM] * len(vectors), out, scratch, "local", flops=2 * 10**9,
        )(cols, tiles, *vectors)

    incoming = exchange(msgs[:4])
    early = along_slabs(None, msgs[5])
    acc, forms, zn = local(nf, True, tiles2, z)
    acc, incoming, last = lax.optimization_barrier((acc, incoming, msgs[4]))
    later = along_slabs(last, None) + early + incoming[2:]
    *msgs, q, wd = call(
        functools.partial(second_kernel, nf, blocks, cap),
        [VMEM] * 8 + [ANY] * 3,
        [msg] * 4 + [like(blocks, nf, LANES), like(blocks, both, LANES)],
        [rows, rows] + tables,
        "second",
    )(acc, *incoming, z, winv, wcoup, send, recv, counts)
    msgs, later = lax.optimization_barrier((msgs, later))
    incoming = exchange(msgs)
    acc, wn, qn = local(both, False, forms, wd, q)
    sn, pay = call(
        functools.partial(third_kernel, nf, blocks, cap),
        [VMEM] * 10 + [SMEM] * 3 + [VMEM] * 5,
        [like(both, width), like(devices, nf // 2, LANES)],
        [pltpu.VMEM((blocks, both, LANES), F32), pltpu.VMEM((nf + both, LANES), F32)],
        "third",
    )(acc, *incoming, *later, wcoup, send, recv, counts, zn, qn, wn, r0, cd)
    everyone = lax.all_to_all(pay, AXES, 0, 0)
    out, res = call(
        functools.partial(last_kernel, nf, rho),
        [VMEM] * 7,
        [jax.ShapeDtypeStruct((nf, width), F32)] * 2,
        [],
        "last",
    )(everyone, zn, wn, qn, r0, cd, sn)
    return out[None, None], res[None, None]


def solution(mesh):
    two = P("slab", "sector")
    return jax.shard_map(
        on_device,
        mesh=mesh,
        in_specs=(two, P(), two, two, two, two, two, two, two, two, two),
        out_specs=(two, two),
        check_vma=False,
    )
```
